32 devices in a mesh: role: 2 (over y), tile: 16 (over z, x, core).
Axes of the slice: x: 2, y: 2, z: 4, core: 2. Of those that a mesh axis runs over, the one named last changes fastest.
Arguments:
- fields_pair: float32 [2, 512, 16384], P('role', None, 'tile'), may hold values from 0 to 1
- velocity: float32 [16384], P('tile'), may hold values from -0.5 to 0.5
- growth: float32 [16384], P('tile'), may hold values from 0.05 to 0.5
- features: bfloat16 [512, 1024], replicated, may hold values from -6 to 6
- assignment: int32 [512], replicated, may hold values from 0 to 511, each once
- out_pair: float32 [2, 1024, 16384], P('role', None, 'tile'), may hold values from -0.1875 to 0.1875
- hidden_pair: float32 [2, 5, 1024, 1024], P('role', None, 'tile'), may hold values from -0.1875 to 0.1875
Outputs:
- fields_next: float32 [2, 512, 16384], P('role', None, 'tile')
- out_next: float32 [2, 1024, 16384], P('role', None, 'tile')
- hidden_next: float32 [2, 5, 1024, 1024], P('role', None, 'tile')
The draws below stay inside these ranges and needn't reach their ends.
Inputs may be any that keep to these rules, and one draw needn't show every extreme that they name: `assignment`: a permutation of the 512 members.
All inputs are finite; a program needn't handle non-finite values.
Results may differ from the reference program's by a relative error of at most 0.0022.
The reference program's roundings to bfloat16 on the way (of `residual`) count: a program that leaves them out, or rounds other values in their place, can miss the bound.
Values may be sent and summed in bfloat16 or wider, within the bound.
A program may use at most 192 MiB of HBM per device.

```python
import math
import jax
import jax.numpy as jnp

BATCH = 512
HID = 1024
LAYERS = 5
SLAB = 16384


def block_levels(stream_key, shape, split, low, high):
    def one(dim, parts):
        steps = jax.random.uniform(jax.random.fold_in(jax.random.fold_in(stream_key, 6), dim), (parts,), jnp.float32, low / len(split), high / len(split))
        return jnp.repeat(jnp.exp(steps), shape[dim] // parts).reshape((-1,) + (1,) * (len(shape) - dim - 1))

    loudness = one(*split[0])
    for cut in split[1:]:
        loudness = loudness * one(*cut)
    return loudness


def bell_draw(own_key, dims, width, bound, split=(), kind=jnp.bfloat16):
    drawn = width * jax.random.normal(own_key, dims, jnp.float32)
    if split:
        drawn = drawn * block_levels(own_key, dims, split, -0.22, 0.18)
    return jnp.clip(drawn, -bound, bound).astype(kind)


def setup_inputs(seed: int = 0) -> dict:
    streams_of = jax.random.split(jax.random.key(seed), 8)
    return {
        "fields_pair": jnp.clip(1.0 * jax.random.uniform(streams_of[0], (2, BATCH, SLAB), jnp.float32) ** block_levels(streams_of[0], (2, BATCH, SLAB), ((0, 2), (2, 16)), -0.2, 0.2), 0.0, 1.0),
        "velocity": jnp.clip(jax.random.uniform(streams_of[1], (SLAB,), jnp.float32, -0.5, 0.5) * block_levels(streams_of[1], (SLAB,), ((0, 16),), -0.4, 0.0), -0.5, 0.5),
        "growth": jnp.clip(jnp.exp(math.log(0.5) - 2.3025851 * jax.random.uniform(streams_of[2], (SLAB,), jnp.float32) ** block_levels(streams_of[2], (SLAB,), ((0, 16),), -0.2, 0.2)), 0.05, 0.5),
        "features": bell_draw(streams_of[3], (BATCH, HID), 1.0, 6.0),
        "assignment": jax.random.permutation(streams_of[4], BATCH).astype(jnp.int32),
        "out_pair": bell_draw(streams_of[5], (2, HID, SLAB), HID ** -0.5, 0.1875, ((0, 2), (2, 16)), jnp.float32),
        "hidden_pair": bell_draw(streams_of[6], (2, LAYERS, HID, HID), HID ** -0.5, 0.1875, ((0, 2), (2, 16)), jnp.float32),
    }


def silu_slope(values):
    logistic = jax.nn.sigmoid(values)
    return logistic * (1.0 + values * (1.0 - logistic))


def reference(fields_pair, velocity, growth, features, assignment, out_pair, hidden_pair):
    current = fields_pair[0]
    target = fields_pair[1]
    forward_cell = jnp.roll(current, -1, axis=1)
    outflow = jnp.maximum(velocity, 0.0) * current + jnp.minimum(velocity, 0.0) * forward_cell
    carried = current - outflow + jnp.roll(outflow, 1, axis=1)
    advanced = carried + growth * carried * (1.0 - carried)
    next_batch = jnp.take(advanced, assignment, axis=0)
    weights = hidden_pair[1]
    momenta = hidden_pair[0]
    inputs = []
    summed_list = []
    activation = features
    for layer_index in range(LAYERS):
        inputs.append(activation)
        summed = jnp.dot(activation, weights[layer_index].astype(jnp.bfloat16), preferred_element_type=jnp.float32)
        summed_list.append(summed)
        activation = jax.nn.silu(summed).astype(jnp.bfloat16)
    out_narrow = out_pair[1].astype(jnp.bfloat16)
    predicted = jnp.dot(activation, out_narrow, preferred_element_type=jnp.float32)
    residual = ((predicted - target) / BATCH).astype(jnp.bfloat16)
    grad_out = jnp.dot(activation.T, residual, preferred_element_type=jnp.float32)
    upstream = jnp.dot(residual, out_narrow.T, preferred_element_type=jnp.float32)
    gradients = []
    for layer_index in reversed(range(LAYERS)):
        slope = (upstream * silu_slope(summed_list[layer_index])).astype(jnp.bfloat16)
        gradients.append(jnp.dot(inputs[layer_index].T, slope, preferred_element_type=jnp.float32))
        if layer_index > 0:
            upstream = jnp.dot(slope, weights[layer_index].astype(jnp.bfloat16).T, preferred_element_type=jnp.float32)
    grad_hidden = jnp.stack(gradients[::-1])
    momentum_out = 0.9 * out_pair[0] + grad_out
    weight_out = out_pair[1] - 0.1 * momentum_out
    momentum_hidden = 0.9 * momenta + grad_hidden
    weight_hidden = weights - 0.1 * momentum_hidden
    return (jnp.stack([advanced, next_batch]), jnp.stack([momentum_out, weight_out]), jnp.stack([momentum_hidden, weight_hidden]))
```

```python
import functools

import jax
import jax.numpy as jnp
from jax import lax
from jax.experimental import pallas as pl
from jax.experimental.pallas import tpu as pltpu
from jax.sharding import PartitionSpec as P

momentum_decay = 0.9
step_size = 0.1


def extended(value, axis, dim, width):
    count, length = (lax.axis_size(axis), value.shape[dim])
    up = [(i, (i + 1) % count) for i in range(count)]
    down = [(j, i) for i, j in up]
    last = lax.slice_in_dim(value, length - width, length, axis=dim)
    leading = lax.slice_in_dim(value, 0, width, axis=dim)
    before = lax.ppermute(last, axis, up)
    after = lax.ppermute(leading, axis, down)
    return jnp.concatenate([before, value, after], axis=dim)


def silu_slope(values):
    logistic = jax.nn.sigmoid(values)
    return logistic * (1.0 + values * (1.0 - logistic))


def advance(padded, growth):
    states = padded[:-1]
    velocity_row = padded[-1]
    outflow = (
        jnp.maximum(velocity_row[:-1], 0.0) * states[:, :-1]
        + jnp.minimum(velocity_row[:-1], 0.0) * states[:, 1:]
    )
    carried = states[:, 1:-1] - outflow[:, 1:] + outflow[:, :-1]
    return carried + growth * carried * (1.0 - carried)


def to_trainer(value):
    return lax.ppermute(value.astype(jnp.bfloat16), "role", [(0, 1)])


def to_solver(value):
    return lax.ppermute(value.astype(jnp.bfloat16), "role", [(1, 0)])


def plain_training(features, hidden_narrow, out_narrow, own_fields, own_out, own_hidden, fields):
    layer_count, unit_rows = own_hidden.shape[:2]
    batch = own_fields.shape[0]
    first_unit = lax.axis_index("tile") * unit_rows
    momentum_out = to_trainer(own_out)
    momentum_hidden = to_trainer(own_hidden)
    full_hidden = [
        lax.all_gather(hidden_narrow[i], "tile", axis=0, tiled=True) for i in range(layer_count)
    ]
    inputs, summed_list = [], []
    activation = features
    for i in range(layer_count):
        inputs.append(activation)
        summed = jnp.dot(activation, full_hidden[i], preferred_element_type=jnp.float32)
        summed_list.append(summed)
        activation = jax.nn.silu(summed).astype(jnp.bfloat16)
    predicted = jnp.dot(activation, out_narrow, preferred_element_type=jnp.float32)
    residual = ((predicted - own_fields) / batch).astype(jnp.bfloat16)
    partial_grad = lax.dot_general(
        residual, out_narrow, (((1,), (1,)), ((), ())), preferred_element_type=jnp.float32
    )
    upstream = lax.psum(partial_grad, "tile")
    grad_out = jnp.dot(activation.T, residual, preferred_element_type=jnp.float32)
    sent_out = to_solver(grad_out)
    gradients, sent = [], []
    for i in reversed(range(layer_count)):
        slope = (upstream * silu_slope(summed_list[i])).astype(jnp.bfloat16)
        own_inputs = lax.dynamic_slice_in_dim(inputs[i], first_unit, unit_rows, 1)
        gradient = jnp.dot(own_inputs.T, slope, preferred_element_type=jnp.float32)
        gradients.append(gradient)
        sent.append(to_solver(gradient))
        if i > 0:
            upstream = lax.dot_general(
                slope, full_hidden[i], (((1,), (1,)), ((), ())), preferred_element_type=jnp.float32
            )
    solver_side = lax.axis_index("role") == 0
    grad_out = jnp.where(solver_side, sent_out.astype(jnp.float32), grad_out)
    other_hidden = jnp.where(solver_side, jnp.stack(sent[::-1]), momentum_hidden)
    return grad_out, jnp.stack(gradients[::-1]), momentum_out, other_hidden, to_trainer(fields)


LANES = 128
COLUMNS = 256


class Later:
    def __init__(self, build):
        self.build = build

    def start(self):
        self.build().start()

    def wait(self):
        self.build().wait()

    def wait_recv(self):
        self.build().wait_recv()

    def wait_send(self):
        self.build().wait_send()


def train_kernel(
    groups,
    features_hbm,
    fields_hbm,
    velocity_hbm,
    growth_hbm,
    assignment_hbm,
    out_hbm,
    hidden_hbm,
    fields_next,
    out_next,
    hidden_next,
    features_ref,
    own_fields,
    own_out,
    own_hidden,
    velocity_ref,
    growth_ref,
    assignment_ref,
    left_velocity,
    left_edge,
    right_edge,
    out_ref,
    got_out,
    got_hidden,
    got_fields,
    weights,
    inputs,
    factors,
    residual,
    slope_even,
    slope_odd,
    partial,
    slope,
    gradient,
    core_sum,
    x_away,
    x_sum,
    z_away,
    z_sum,
    z_send,
    z_recv,
    x_send,
    x_recv,
    core_send,
    core_recv,
    sum_send,
    sum_recv,
    slope_send,
    slope_recv,
    role_send,
    role_recv,
    edge_send,
    edge_recv,
    local_sem,
    keep_sem,
):
    layer_count, unit_rows, width = hidden_hbm.shape
    batch, cells = fields_hbm.shape
    rows = partial.shape[3]
    narrow, wide = jnp.bfloat16, jnp.float32
    tiles = groups * 4
    last = layer_count - 1
    role = lax.axis_index("role")
    tile = lax.axis_index("tile")
    core = lax.rem(tile, 2)
    x = lax.rem(tile // 2, 2)
    z = tile // 4
    solver = role == 0
    trainer = role == 1

    def device(z_at, x_at, core_at):
        return (role, z_at * 4 + x_at * 2 + core_at)

    z_places = [lax.rem(z + k, groups) for k in range(1, groups)]
    z_origins = [lax.rem(z + groups - k, groups) for k in range(1, groups)]
    z_peers = [device(place, x, core) for place in z_places]
    x_peer = device(z, 1 - x, core)
    core_peer = device(z, x, 1 - core)
    role_peer = (1 - role, tile)
    right_peer = (role, lax.rem(tile + 1, tiles))
    left_peer = (role, lax.rem(tile + tiles - 1, tiles))
    far_peer = (role, lax.rem(tile + tiles - 1 + 2 * core, tiles))
    sends, solver_sends, trainer_sends = [], [], []

    def remote(views, semaphores, slot, peer):
        def build():
            source, target = views()
            return pltpu.make_async_remote_copy(
                src_ref=source,
                dst_ref=target,
                send_sem=semaphores[0].at[slot],
                recv_sem=semaphores[1].at[slot],
                device_id=peer,
                device_id_type=pl.DeviceIdType.MESH,
            )

        return Later(build)

    def local(views, semaphores, slot):
        def build():
            source, target = views()
            return pltpu.make_async_copy(source, target, semaphores.at[slot])

        return Later(build)

    def twice(view):
        return lambda: (view(),) * 2

    def start(copy, among):
        copy.start()
        among.append(copy)
        return copy

    role_slots = [0]

    def across(view):
        slot = role_slots[0]
        role_slots[0] += 1
        return remote(twice(view), (role_send, role_recv), slot, role_peer)

    chunks = [pl.ds(j * COLUMNS, COLUMNS) for j in range(cells // COLUMNS)]
    parts = [pl.ds(j * COLUMNS, COLUMNS) for j in range(width // COLUMNS)]
    shares = [across(lambda i=i: weights.at[i, z, x, core]) for i in range(layer_count)]
    momenta = [across(lambda c=c: got_out.at[:, c]) for c in chunks]
    hidden_momentum = across(lambda: got_hidden)
    fresh = [across(lambda c=c: got_fields.at[:, c]) for c in chunks]
    residuals = [across(lambda c=c: residual.at[:, c]) for c in chunks]
    slope_shares = [across(lambda c=c: slope.at[z, x, core, :, c]) for c in parts]

    kept = [lambda c=c: (own_fields.at[:, c], fields_next.at[:, c]) for c in chunks]
    kept += [lambda c=c: (own_out.at[:, c], out_next.at[:, c]) for c in chunks]
    kept += [lambda: (own_hidden, hidden_next)]
    keeps = [local(views, keep_sem, k) for k, views in enumerate(kept)]
    keep_fields, keep_out = keeps[: len(chunks)], keeps[len(chunks) : -1]
    keep_hidden = keeps[-1]

    pairs = [lambda: (hidden_hbm, own_hidden)]
    pairs += [lambda c=c: (out_hbm.at[:, c], own_out.at[:, c]) for c in chunks]
    pairs += [
        lambda: (fields_hbm, own_fields),
        lambda: (velocity_hbm, velocity_ref),
        lambda: (growth_hbm, growth_ref),
        lambda: (assignment_hbm, assignment_ref),
        lambda: (features_hbm, features_ref),
    ]
    loads = [local(views, local_sem, k) for k, views in enumerate(pairs)]
    for load in loads:
        load.start()
    hidden_load, out_loads, small_loads = loads[0], loads[1 : 1 + len(chunks)], loads[1 + len(chunks) :]
    barrier = pltpu.get_barrier_semaphore()
    peers = z_peers + [x_peer, core_peer, role_peer, far_peer]
    for peer in peers:
        pl.semaphore_signal(barrier, inc=1, device_id=peer, device_id_type=pl.DeviceIdType.MESH)
    pl.semaphore_wait(barrier, len(peers))

    last_lanes = pl.ds(cells - LANES, LANES)
    edge_list = [
        (lambda: (fields_hbm.at[:, last_lanes], left_edge), right_peer),
        (lambda: (velocity_hbm.at[:, last_lanes], left_velocity), right_peer),
        (lambda: (fields_hbm.at[:, pl.ds(0, LANES)], right_edge), left_peer),
    ]
    edges = [
        remote(views, (edge_send, edge_recv), k, peer) for k, (views, peer) in enumerate(edge_list)
    ]

    z_copies = []
    x_copies = [[] for _ in range(layer_count)]
    core_copies = [[] for _ in range(layer_count)]

    def send_x(i, slot, place):
        view = twice(lambda: weights.at[i, place, x, core])
        copy = remote(view, (x_send, x_recv), (i, slot), x_peer)
        x_copies[i].append(start(copy, sends))

    def send_core(i, place, x_at):
        slot = len(core_copies[i])
        view = twice(lambda: weights.at[i, place, x_at, core])
        copy = remote(view, (core_send, core_recv), (i, slot), core_peer)
        core_copies[i].append(start(copy, sends))

    def send_share(i):
        @pl.when(solver)
        def _():
            shares[i].wait_recv()

        view = twice(lambda: weights.at[i, z, x, core])
        z_copies.append(
            [
                start(remote(view, (z_send, z_recv), (i, k), z_peers[k]), sends)
                for k in range(groups - 1)
            ]
        )
        send_x(i, 0, z)
        send_core(i, z, x)

    def columns_of(j):
        return pl.ds(pl.multiple_of(j * COLUMNS, COLUMNS), COLUMNS)

    def advance():
        velocity = velocity_ref[...]
        forward_speed = jnp.maximum(velocity, 0.0)
        backward_speed = jnp.minimum(velocity, 0.0)
        growth = growth_ref[...]
        before = left_velocity[:, LANES - 1 :]
        step = LANES // 2

        @pl.loop(0, batch // step)
        def _(j):
            band = pl.ds(pl.multiple_of(j * step, step), step)
            current = own_fields[band, :]
            lane = lax.broadcasted_iota(jnp.int32, current.shape, 1)
            following = jnp.where(
                lane == cells - 1, right_edge[band, :1], pltpu.roll(current, cells - 1, 1)
            )
            outflow = forward_speed * current + backward_speed * following
            inflow_edge = (
                jnp.maximum(before, 0.0) * left_edge[band, :][:, LANES - 1 :]
                + jnp.minimum(before, 0.0) * current[:, :1]
            )
            inflow = jnp.where(lane == 0, inflow_edge, pltpu.roll(outflow, 1, 1))
            carried = current - outflow + inflow
            advanced = carried + growth * carried * (1.0 - carried)
            own_fields[band, :] = advanced
            got_fields[band, :] = advanced.astype(narrow)

    @pl.when(solver)
    def _():
        for copy in edges:
            start(copy, solver_sends)
        for load, c, copy in zip(out_loads, chunks, momenta):
            load.wait()
            got_out[:, c] = own_out[:, c].astype(narrow)
            start(copy, solver_sends)
        hidden_load.wait()
        got_hidden[...] = own_hidden[...].astype(narrow)
        start(hidden_momentum, solver_sends)

    @pl.when(trainer)
    def _():
        hidden_load.wait()
        for i in range(layer_count):
            weights[i, z, x, core] = own_hidden[i].astype(narrow)
            start(shares[i], trainer_sends)

    send_share(0)
    send_share(1)

    for load in small_loads:
        load.wait()

    @pl.when(solver)
    def _():
        for copy in edges:
            copy.wait_recv()
        advance()
        for copy, written in zip(fresh, keep_fields):
            start(copy, solver_sends)
            written.start()

    @pl.when(trainer)
    def _():
        for load, c in zip(out_loads, chunks):
            load.wait()
            out_ref[:, c] = own_out[:, c].astype(narrow)

    def forward(i):
        @pl.loop(0, width // COLUMNS)
        def _(j):
            columns = columns_of(j)
            block = weights[i, :, :, :, :, columns].reshape(width, COLUMNS)
            activation = features_ref[...] if i == 0 else inputs[i - 1]
            summed = jnp.dot(activation, block, preferred_element_type=wide)
            logistic = jax.nn.sigmoid(summed)
            inputs[i, :, columns] = (summed * logistic).astype(narrow)
            factors[i, :, columns] = logistic * (1.0 + summed * (1.0 - logistic))

    for i in range(layer_count + 2):
        if i + 2 < layer_count:
            send_share(i + 2)
        if i < layer_count:
            for k in range(groups - 1):
                z_copies[i][k].wait_recv()
                send_x(i, k + 1, z_origins[k])
                send_core(i, z_origins[k], x)
        if 1 <= i <= layer_count:
            for slot, place in enumerate([z] + z_origins):
                x_copies[i - 1][slot].wait_recv()
                send_core(i - 1, place, 1 - x)
        if i >= 2:
            for copy in core_copies[i - 2]:
                copy.wait_recv()
            forward(i - 2)

    def update_out(j, decay, rate, other):
        c = chunks[j]

        @pl.loop(0, width // COLUMNS)
        def _(k):
            units = columns_of(k)
            grad = lax.dot_general(
                inputs[last, :, units],
                residual[:, c],
                (((0,), (0,)), ((), ())),
                preferred_element_type=wide,
            )
            if other is None:
                own_out[units, c] = decay * own_out[units, c] + grad
            else:
                fresh_momentum = decay * other[units, c].astype(wide) + grad
                own_out[units, c] = own_out[units, c] - rate * fresh_momentum

        keep_out[j].start()

    def update_solver(j):
        residuals[j].wait_recv()
        update_out(j, momentum_decay, None, None)

    def update_trainer(j):
        momenta[j].wait_recv()
        update_out(j, momentum_decay, step_size, got_out)

    core_sums, x_sums, z_sums, z_slopes, x_slopes, core_slopes = [], [], [], [], [], []

    def send_sum(views, j, slot, peer):
        return start(remote(views, (sum_send, sum_recv), (j, slot), peer), trainer_sends)

    @pl.when(trainer)
    def _():
        for j, c in enumerate(chunks):
            predicted = jnp.dot(inputs[last], out_ref[:, c], preferred_element_type=wide)
            residual[:, c] = ((predicted - own_fields[:, c]) / batch).astype(narrow)
            if j + 1 < len(chunks):
                start(residuals[j], trainer_sends)
        for j, columns in enumerate(parts):
            part = lax.dot_general(
                residual[...],
                out_ref[columns, :],
                (((1,), (1,)), ((), ())),
                preferred_element_type=wide,
            )
            partial[:, :, :, :, columns] = part.reshape(groups, 2, 2, rows, COLUMNS)
            core_sums.append(
                send_sum(
                    lambda columns=columns: (
                        partial.at[:, :, 1 - core, :, columns],
                        core_sum.at[:, :, :, columns],
                    ),
                    j,
                    0,
                    core_peer,
                )
            )
        for j, columns in enumerate(parts):
            core_sums[j].wait_recv()
            away = partial[:, 1 - x, core, :, columns] + core_sum[:, 1 - x, :, columns]
            x_away[:, :, columns] = away.astype(narrow)
            x_sums.append(
                send_sum(
                    lambda columns=columns: (x_away.at[:, :, columns], x_sum.at[:, :, columns]),
                    j,
                    1,
                    x_peer,
                )
            )
        update_trainer(0)
        for j, columns in enumerate(parts):
            near = partial[:, x, core, :, columns] + core_sum[:, x, :, columns]
            x_sums[j].wait_recv()
            near = near + x_sum[:, :, columns].astype(wide)
            partial[:, x, core, :, columns] = near
            z_away[:, :, columns] = near.astype(narrow)
            z_sums.append(
                [
                    send_sum(
                        lambda columns=columns, k=k: (
                            z_away.at[z_places[k], :, columns],
                            z_sum.at[k, :, columns],
                        ),
                        j,
                        2 + k,
                        z_peers[k],
                    )
                    for k in range(groups - 1)
                ]
            )
        update_trainer(1)

    @pl.when(solver)
    def _():
        update_solver(0)
        update_solver(1)

    own_rows = pl.ds(pl.multiple_of(tile * rows, rows), rows)

    def send_slope(view, j, slot, peer):
        return start(remote(twice(view), (slope_send, slope_recv), (j, slot), peer), sends)

    for j, columns in enumerate(parts):

        @pl.when(trainer)
        def _():
            upstream = partial[z, x, core, :, columns]
            for k in range(groups - 1):
                z_sums[j][k].wait_recv()
                upstream = upstream + z_sum[k, :, columns].astype(wide)
            slope[z, x, core, :, columns] = (upstream * factors[last, own_rows, columns]).astype(
                narrow
            )
            start(slope_shares[j], trainer_sends)

        @pl.when(solver)
        def _():
            slope_shares[j].wait_recv()

        view = lambda columns=columns: slope.at[z, x, core, :, columns]
        z_slopes.append([send_slope(view, j, k, z_peers[k]) for k in range(groups - 1)])

    @pl.when(trainer)
    def _():
        start(residuals[-1], trainer_sends)
        update_trainer(2)

    for j, columns in enumerate(parts):
        for copy in z_slopes[j]:
            copy.wait_recv()
        x_slopes.append(send_slope(
            lambda columns=columns: slope.at[:, x, core, :, columns], j, groups - 1, x_peer
        ))
    for j, columns in enumerate(parts):
        x_slopes[j].wait_recv()
        core_slopes.append(send_slope(
            lambda columns=columns: slope.at[:, :, core, :, columns], j, groups, core_peer
        ))

    @pl.when(trainer)
    def _():
        update_trainer(3)
        hidden_momentum.wait_recv()

    for copy in core_slopes:
        copy.wait_recv()

    per_block = LANES // unit_rows
    first_lane = pl.multiple_of((tile // per_block) * LANES, LANES)
    unit_first = pl.multiple_of(lax.rem(tile, per_block) * unit_rows, unit_rows)
    slopes = [slope.reshape(batch, width), slope_even, slope_odd]
    for step, i in enumerate(reversed(range(layer_count))):
        source = features_ref if i == 0 else inputs.at[i - 1]
        this_slope = slopes[0] if step == 0 else slopes[1 + step % 2]
        next_slope = slopes[1 + (step + 1) % 2]
        if i > 0:

            @pl.loop(0, width // COLUMNS)
            def _(j):
                columns = columns_of(j)
                block = weights.at[i].reshape(width, width)[columns, :]
                back = lax.dot_general(
                    this_slope[...],
                    block,
                    (((1,), (1,)), ((), ())),
                    preferred_element_type=wide,
                )
                next_slope[:, columns] = (back * factors[i - 1, :, columns]).astype(narrow)

        @pl.loop(0, width // COLUMNS)
        def _(j):
            columns = columns_of(j)
            gradient[:, columns] = lax.dot_general(
                source[:, pl.ds(first_lane, LANES)],
                this_slope[:, columns],
                (((0,), (0,)), ((), ())),
                preferred_element_type=wide,
            )

        own_units = pl.ds(unit_first, unit_rows)

        @pl.when(solver)
        def _():
            own_hidden[i] = momentum_decay * own_hidden[i] + gradient[own_units, :]

        @pl.when(trainer)
        def _():
            fresh_momentum = momentum_decay * got_hidden[i].astype(wide) + gradient[own_units, :]
            own_hidden[i] = own_hidden[i] - step_size * fresh_momentum

    keep_hidden.start()

    @pl.when(solver)
    def _():
        for j in range(2, len(chunks)):
            update_solver(j)

    @pl.when(trainer)
    def _():
        member = lax.broadcasted_iota(jnp.int32, (batch, batch), 0)
        chosen = jnp.where(member == assignment_ref[...], 1.0, 0.0).astype(narrow)
        for j, c in enumerate(chunks):
            fresh[j].wait_recv()
            own_fields[:, c] = lax.dot_general(
                chosen, got_fields[:, c], (((0,), (0,)), ((), ())), preferred_element_type=wide
            )
            keep_fields[j].start()

    for copy in sends:
        copy.wait_send()

    @pl.when(solver)
    def _():
        for copy in solver_sends:
            copy.wait_send()

    @pl.when(trainer)
    def _():
        for copy in trainer_sends:
            copy.wait_send()

    for copy in keeps:
        copy.wait()


def fused_step(fields, velocity, growth, features, assignment, own_out, own_hidden):
    layer_count, unit_rows, width = own_hidden.shape
    batch, cells = fields.shape
    groups = lax.axis_size("tile") // 4
    rows = batch // lax.axis_size("tile")
    narrow, wide = jnp.bfloat16, jnp.float32
    dma = pltpu.SemaphoreType.DMA
    anywhere = pl.BlockSpec(memory_space=pl.ANY)
    parts, pieces = width // COLUMNS, cells // COLUMNS
    role_slots = layer_count + 3 * pieces + 1 + parts
    return pl.pallas_call(
        functools.partial(train_kernel, groups),
        out_shape=(
            jax.ShapeDtypeStruct(fields.shape, wide),
            jax.ShapeDtypeStruct(own_out.shape, wide),
            jax.ShapeDtypeStruct(own_hidden.shape, wide),
        ),
        in_specs=[anywhere] * 7,
        out_specs=[anywhere] * 3,
        scratch_shapes=[
            pltpu.VMEM((batch, width), narrow),
            pltpu.VMEM((batch, cells), wide),
            pltpu.VMEM((width, cells), wide),
            pltpu.VMEM(own_hidden.shape, wide),
            pltpu.VMEM((1, cells), wide),
            pltpu.VMEM((1, cells), wide),
            pltpu.VMEM((1, batch), jnp.int32),
            pltpu.VMEM((1, LANES), wide),
            pltpu.VMEM((batch, LANES), wide),
            pltpu.VMEM((batch, LANES), wide),
            pltpu.VMEM((width, cells), narrow),
            pltpu.VMEM((width, cells), narrow),
            pltpu.VMEM(own_hidden.shape, narrow),
            pltpu.VMEM((batch, cells), narrow),
            pltpu.VMEM((layer_count, groups, 2, 2, unit_rows, width), narrow),
            pltpu.VMEM((layer_count, batch, width), narrow),
            pltpu.VMEM((layer_count, batch, width), wide),
            pltpu.VMEM((batch, cells), narrow),
            pltpu.VMEM((batch, width), narrow),
            pltpu.VMEM((batch, width), narrow),
            pltpu.VMEM((groups, 2, 2, rows, width), wide),
            pltpu.VMEM((groups, 2, 2, rows, width), narrow),
            pltpu.VMEM((LANES, width), wide),
            pltpu.VMEM((groups, 2, rows, width), wide),
            pltpu.VMEM((groups, rows, width), narrow),
            pltpu.VMEM((groups, rows, width), narrow),
            pltpu.VMEM((groups, rows, width), narrow),
            pltpu.VMEM((groups - 1, rows, width), narrow),
            dma((layer_count, groups - 1)),
            dma((layer_count, groups - 1)),
            dma((layer_count, groups)),
            dma((layer_count, groups)),
            dma((layer_count, 2 * groups)),
            dma((layer_count, 2 * groups)),
            dma((parts, groups + 1)),
            dma((parts, groups + 1)),
            dma((parts, groups + 1)),
            dma((parts, groups + 1)),
            dma((role_slots,)),
            dma((role_slots,)),
            dma((3,)),
            dma((3,)),
            dma((6 + pieces,)),
            dma((2 * pieces + 1,)),
        ],
        compiler_params=pltpu.CompilerParams(
            collective_id=0, has_side_effects=True, vmem_limit_bytes=64000000
        ),
        cost_estimate=pl.CostEstimate(
            flops=60 * batch * width * width, bytes_accessed=40 * batch * width, transcendentals=0
        ),
    )(
        features,
        fields,
        velocity[None, :],
        growth[None, :],
        assignment[None, :],
        own_out,
        own_hidden,
    )


def plain_body(fields_pair, velocity, growth, features, assignment, out_pair, hidden_pair):
    solver_side = lax.axis_index("role") == 0
    own_fields = fields_pair[0]
    own_out = out_pair[0]
    own_hidden = hidden_pair[0]
    stacked = jnp.concatenate([own_fields, velocity[None, :]], axis=0)
    advanced = advance(extended(stacked, "tile", 1, 1), growth)
    grad_out, grad_hidden, other_out, other_hidden, fresh_fields = plain_training(
        features,
        own_hidden.astype(jnp.bfloat16),
        own_out.astype(jnp.bfloat16),
        own_fields,
        own_out,
        own_hidden,
        advanced.astype(jnp.bfloat16),
    )
    grad_out, grad_hidden, other_out, other_hidden = (
        v.astype(jnp.float32) for v in (grad_out, grad_hidden, other_out, other_hidden)
    )
    out_next = jnp.where(
        solver_side,
        momentum_decay * own_out + grad_out,
        own_out - step_size * (momentum_decay * other_out + grad_out),
    )
    hidden_next = jnp.where(
        solver_side,
        momentum_decay * own_hidden + other_hidden,
        own_hidden - step_size * (momentum_decay * other_hidden + grad_hidden),
    )
    next_batch = jnp.take(fresh_fields, assignment, axis=0).astype(jnp.float32)
    fields_next = jnp.where(solver_side, advanced, next_batch)
    return (fields_next[None], out_next[None], hidden_next[None])


def body(fields_pair, velocity, growth, features, assignment, out_pair, hidden_pair):
    tiles = lax.axis_size("tile")
    batch, cells = fields_pair.shape[1:]
    layer_count, unit_rows, width = hidden_pair.shape[1:]
    fits = (
        lax.axis_size("role") == 2
        and tiles % 4 == 0
        and tiles > 4
        and batch % tiles == 0
        and (batch // tiles) % 16 == 0
        and LANES % unit_rows == 0
        and width % COLUMNS == 0
        and cells % COLUMNS == 0
        and cells // COLUMNS == 4
    )
    if not fits:
        return plain_body(
            fields_pair, velocity, growth, features, assignment, out_pair, hidden_pair
        )
    results = fused_step(
        fields_pair[0], velocity, growth, features, assignment, out_pair[0], hidden_pair[0]
    )
    return tuple(result[None] for result in results)


def solution(mesh):
    return jax.shard_map(
        body,
        mesh=mesh,
        in_specs=(
            P("role", None, "tile"),
            P("tile"),
            P("tile"),
            P(),
            P(),
            P("role", None, "tile"),
            P("role", None, "tile", None),
        ),
        out_specs=(P("role", None, "tile"), P("role", None, "tile"), P("role", None, "tile", None)),
        check_vma=False,
    )
```

```python
import functools

import jax
import jax.numpy as jnp
from jax import lax
from jax.experimental import pallas as pl
from jax.experimental.pallas import tpu as pltpu
from jax.sharding import PartitionSpec as P

momentum_decay = 0.9
step_size = 0.1


def extended(value, axis, dim, width):
    count, length = (lax.axis_size(axis), value.shape[dim])
    up = [(i, (i + 1) % count) for i in range(count)]
    down = [(j, i) for i, j in up]
    last = lax.slice_in_dim(value, length - width, length, axis=dim)
    leading = lax.slice_in_dim(value, 0, width, axis=dim)
    before = lax.ppermute(last, axis, up)
    after = lax.ppermute(leading, axis, down)
    return jnp.concatenate([before, value, after], axis=dim)


def silu_slope(values):
    logistic = jax.nn.sigmoid(values)
    return logistic * (1.0 + values * (1.0 - logistic))


def advance(padded, growth):
    states = padded[:-1]
    velocity_row = padded[-1]
    outflow = (
        jnp.maximum(velocity_row[:-1], 0.0) * states[:, :-1]
        + jnp.minimum(velocity_row[:-1], 0.0) * states[:, 1:]
    )
    carried = states[:, 1:-1] - outflow[:, 1:] + outflow[:, :-1]
    return carried + growth * carried * (1.0 - carried)


def to_trainer(value):
    return lax.ppermute(value.astype(jnp.bfloat16), "role", [(0, 1)])


def to_solver(value):
    return lax.ppermute(value.astype(jnp.bfloat16), "role", [(1, 0)])


def plain_training(features, hidden_narrow, out_narrow, own_fields, own_out, own_hidden, fields):
    layer_count, unit_rows = own_hidden.shape[:2]
    batch = own_fields.shape[0]
    first_unit = lax.axis_index("tile") * unit_rows
    momentum_out = to_trainer(own_out)
    momentum_hidden = to_trainer(own_hidden)
    full_hidden = [
        lax.all_gather(hidden_narrow[i], "tile", axis=0, tiled=True) for i in range(layer_count)
    ]
    inputs, summed_list = [], []
    activation = features
    for i in range(layer_count):
        inputs.append(activation)
        summed = jnp.dot(activation, full_hidden[i], preferred_element_type=jnp.float32)
        summed_list.append(summed)
        activation = jax.nn.silu(summed).astype(jnp.bfloat16)
    predicted = jnp.dot(activation, out_narrow, preferred_element_type=jnp.float32)
    residual = ((predicted - own_fields) / batch).astype(jnp.bfloat16)
    partial_grad = lax.dot_general(
        residual, out_narrow, (((1,), (1,)), ((), ())), preferred_element_type=jnp.float32
    )
    upstream = lax.psum(partial_grad, "tile")
    grad_out = jnp.dot(activation.T, residual, preferred_element_type=jnp.float32)
    sent_out = to_solver(grad_out)
    gradients, sent = [], []
    for i in reversed(range(layer_count)):
        slope = (upstream * silu_slope(summed_list[i])).astype(jnp.bfloat16)
        own_inputs = lax.dynamic_slice_in_dim(inputs[i], first_unit, unit_rows, 1)
        gradient = jnp.dot(own_inputs.T, slope, preferred_element_type=jnp.float32)
        gradients.append(gradient)
        sent.append(to_solver(gradient))
        if i > 0:
            upstream = lax.dot_general(
                slope, full_hidden[i], (((1,), (1,)), ((), ())), preferred_element_type=jnp.float32
            )
    solver_side = lax.axis_index("role") == 0
    grad_out = jnp.where(solver_side, sent_out.astype(jnp.float32), grad_out)
    other_hidden = jnp.where(solver_side, jnp.stack(sent[::-1]), momentum_hidden)
    return grad_out, jnp.stack(gradients[::-1]), momentum_out, other_hidden, to_trainer(fields)


LANES = 128
COLUMNS = 256


class Later:
    def __init__(self, build):
        self.build = build

    def start(self):
        self.build().start()

    def wait(self):
        self.build().wait()

    def wait_recv(self):
        self.build().wait_recv()

    def wait_send(self):
        self.build().wait_send()


def train_kernel(
    groups,
    features_hbm,
    fields_hbm,
    velocity_hbm,
    growth_hbm,
    assignment_hbm,
    out_hbm,
    hidden_hbm,
    fields_next,
    out_next,
    hidden_next,
    features_ref,
    own_fields,
    own_out,
    own_hidden,
    velocity_ref,
    growth_ref,
    assignment_ref,
    left_velocity,
    left_edge,
    right_edge,
    out_ref,
    got_out,
    got_hidden,
    got_fields,
    weights,
    inputs,
    factors,
    residual,
    slope_even,
    slope_odd,
    partial,
    slope,
    gradient,
    core_sum,
    x_away,
    x_sum,
    z_away,
    z_sum,
    z_send,
    z_recv,
    x_send,
    x_recv,
    core_send,
    core_recv,
    sum_send,
    sum_recv,
    slope_send,
    slope_recv,
    role_send,
    role_recv,
    edge_send,
    edge_recv,
    local_sem,
    keep_sem,
):
    layer_count, unit_rows, width = hidden_hbm.shape
    batch, cells = fields_hbm.shape
    rows = partial.shape[3]
    narrow, wide = jnp.bfloat16, jnp.float32
    tiles = groups * 4
    last = layer_count - 1
    role = lax.axis_index("role")
    tile = lax.axis_index("tile")
    core = lax.rem(tile, 2)
    x = lax.rem(tile // 2, 2)
    z = tile // 4
    solver = role == 0
    trainer = role == 1

    def device(z_at, x_at, core_at):
        return (role, z_at * 4 + x_at * 2 + core_at)

    z_places = [lax.rem(z + k, groups) for k in range(1, groups)]
    z_peers = [device(place, x, core) for place in z_places]
    x_peer = device(z, 1 - x, core)
    core_peer = device(z, x, 1 - core)
    role_peer = (1 - role, tile)
    right_peer = (role, lax.rem(tile + 1, tiles))
    left_peer = (role, lax.rem(tile + tiles - 1, tiles))
    far_peer = (role, lax.rem(tile + tiles - 1 + 2 * core, tiles))
    sends, solver_sends, trainer_sends = [], [], []

    def remote(views, semaphores, slot, peer, recv_slot=None):
        def build():
            source, target = views()
            return pltpu.make_async_remote_copy(
                src_ref=source,
                dst_ref=target,
                send_sem=semaphores[0].at[slot],
                recv_sem=semaphores[1].at[slot if recv_slot is None else recv_slot],
                device_id=peer,
                device_id_type=pl.DeviceIdType.MESH,
            )

        return Later(build)

    def local(views, semaphores, slot):
        def build():
            source, target = views()
            return pltpu.make_async_copy(source, target, semaphores.at[slot])

        return Later(build)

    def twice(view):
        return lambda: (view(),) * 2

    def start(copy, among):
        copy.start()
        among.append(copy)
        return copy

    role_slots = [0]

    def across(view):
        slot = role_slots[0]
        role_slots[0] += 1
        return remote(twice(view), (role_send, role_recv), slot, role_peer)

    chunks = [pl.ds(j * COLUMNS, COLUMNS) for j in range(cells // COLUMNS)]
    parts = [pl.ds(j * COLUMNS, COLUMNS) for j in range(width // COLUMNS)]
    shares = [across(lambda i=i: weights.at[i, z, x, core]) for i in range(layer_count)]
    momenta = [across(lambda c=c: got_out.at[:, c]) for c in chunks]
    hidden_momentum = across(lambda: got_hidden)
    fresh = [across(lambda c=c: got_fields.at[:, c]) for c in chunks]
    residuals = [across(lambda c=c: residual.at[:, c]) for c in chunks]
    slope_shares = [across(lambda c=c: slope.at[z, x, core, :, c]) for c in parts]

    kept = [lambda c=c: (own_fields.at[:, c], fields_next.at[:, c]) for c in chunks]
    kept += [lambda c=c: (own_out.at[:, c], out_next.at[:, c]) for c in chunks]
    kept += [lambda: (own_hidden, hidden_next)]
    keeps = [local(views, keep_sem, k) for k, views in enumerate(kept)]
    keep_fields, keep_out = keeps[: len(chunks)], keeps[len(chunks) : -1]
    keep_hidden = keeps[-1]

    pairs = [lambda: (hidden_hbm, own_hidden)]
    pairs += [lambda c=c: (out_hbm.at[:, c], own_out.at[:, c]) for c in chunks]
    pairs += [
        lambda: (fields_hbm, own_fields),
        lambda: (velocity_hbm, velocity_ref),
        lambda: (growth_hbm, growth_ref),
        lambda: (assignment_hbm, assignment_ref),
        lambda: (features_hbm, features_ref),
    ]
    loads = [local(views, local_sem, k) for k, views in enumerate(pairs)]
    for load in loads:
        load.start()
    hidden_load, out_loads, small_loads = loads[0], loads[1 : 1 + len(chunks)], loads[1 + len(chunks) :]
    barrier = pltpu.get_barrier_semaphore()
    peers = z_peers + [x_peer, core_peer, role_peer, far_peer]
    for peer in peers:
        pl.semaphore_signal(barrier, inc=1, device_id=peer, device_id_type=pl.DeviceIdType.MESH)
    pl.semaphore_wait(barrier, len(peers))

    last_lanes = pl.ds(cells - LANES, LANES)
    edge_list = [
        (lambda: (fields_hbm.at[:, last_lanes], left_edge), right_peer),
        (lambda: (velocity_hbm.at[:, last_lanes], left_velocity), right_peer),
        (lambda: (fields_hbm.at[:, pl.ds(0, LANES)], right_edge), left_peer),
    ]
    edges = [
        remote(views, (edge_send, edge_recv), k, peer) for k, (views, peer) in enumerate(edge_list)
    ]

    nearest = [
        sorted((p for p in range(groups) if p != q), key=lambda p: (abs(p - q), p))
        for q in range(groups)
    ]

    def pick(k):
        place = jnp.int32(nearest[0][k])
        for q in range(1, groups):
            place = jnp.where(z == q, nearest[q][k], place)
        return place

    z_origins = [pick(k) for k in range(groups - 1)]
    above = device(lax.rem(z + 1, groups), x, core)
    below = device(lax.rem(z + groups - 1, groups), x, core)
    spreads, relays = [], []

    def share_of(i, place, x_at):
        return twice(lambda: weights.at[i, place, x_at, core])

    def hop(i, place, x_at, slot, peer):
        return remote(
            share_of(i, place, x_at), (z_send, z_recv), (i, place, x_at, slot), peer, (i, place, x_at)
        )

    def spread(i, x_at):
        @pl.when(z < groups - 1)
        def _():
            hop(i, z, x_at, 0, above).start()

        @pl.when(z > 0)
        def _():
            hop(i, z, x_at, 1, below).start()

        spreads.append((i, x_at))

    def onward(k):
        rising = z_origins[k] < z
        return jnp.logical_or(
            jnp.logical_and(rising, z < groups - 1),
            jnp.logical_and(jnp.logical_not(rising), z > 0),
        )

    def relay(i, k, x_at, noted=True):
        place = z_origins[k]
        target = jnp.where(place < z, lax.rem(z + 1, groups), lax.rem(z + groups - 1, groups))
        hop(i, place, x_at, 0, above).wait_recv()

        @pl.when(onward(k))
        def _():
            hop(i, place, x_at, 0, device(target, x, core)).start()

        if noted:
            relays.append((i, k, x_at))
        if i < last:
            send_x(i, place)
        send_core(i, place, x_at)

    def x_copy(i, place):
        return remote(share_of(i, place, x), (x_send, x_recv), (i, place), x_peer)

    def x_arrival(i, place):
        return remote(share_of(i, place, 1 - x), (x_send, x_recv), (i, place), x_peer)

    def core_copy(i, place, x_at):
        return remote(share_of(i, place, x_at), (core_send, core_recv), (i, place, x_at), core_peer)

    def send_x(i, place):
        x_copy(i, place).start()

    def send_core(i, place, x_at):
        core_copy(i, place, x_at).start()

    def cross(i, place):
        x_arrival(i, place).wait_recv()
        send_core(i, place, 1 - x)

    def send_share(i):
        @pl.when(solver)
        def _():
            shares[i].wait_recv()

        spread(i, x)
        send_x(i, z)
        send_core(i, z, x)

    share_order = [last] + list(range(last))

    def columns_of(j):
        return pl.ds(pl.multiple_of(j * COLUMNS, COLUMNS), COLUMNS)

    def advance():
        velocity = velocity_ref[...]
        forward_speed = jnp.maximum(velocity, 0.0)
        backward_speed = jnp.minimum(velocity, 0.0)
        growth = growth_ref[...]
        before = left_velocity[:, LANES - 1 :]
        step = LANES // 2

        @pl.loop(0, batch // step)
        def _(j):
            band = pl.ds(pl.multiple_of(j * step, step), step)
            current = own_fields[band, :]
            lane = lax.broadcasted_iota(jnp.int32, current.shape, 1)
            following = jnp.where(
                lane == cells - 1, right_edge[band, :1], pltpu.roll(current, cells - 1, 1)
            )
            outflow = forward_speed * current + backward_speed * following
            inflow_edge = (
                jnp.maximum(before, 0.0) * left_edge[band, :][:, LANES - 1 :]
                + jnp.minimum(before, 0.0) * current[:, :1]
            )
            inflow = jnp.where(lane == 0, inflow_edge, pltpu.roll(outflow, 1, 1))
            carried = current - outflow + inflow
            advanced = carried + growth * carried * (1.0 - carried)
            own_fields[band, :] = advanced
            got_fields[band, :] = advanced.astype(narrow)

    @pl.when(solver)
    def _():
        for copy in edges:
            start(copy, solver_sends)
        for load, c, copy in zip(out_loads, chunks, momenta):
            load.wait()
            got_out[:, c] = own_out[:, c].astype(narrow)
            start(copy, solver_sends)
        hidden_load.wait()
        got_hidden[...] = own_hidden[...].astype(narrow)
        start(hidden_momentum, solver_sends)

    @pl.when(trainer)
    def _():
        hidden_load.wait()
        for i in range(layer_count):
            weights[i, z, x, core] = own_hidden[i].astype(narrow)
        for i in share_order:
            start(shares[i], trainer_sends)

    for i in share_order:
        send_share(i)

    for load in small_loads:
        load.wait()

    @pl.when(solver)
    def _():
        for copy in edges:
            copy.wait_recv()
        advance()
        for copy, written in zip(fresh, keep_fields):
            start(copy, solver_sends)
            written.start()

    @pl.when(trainer)
    def _():
        for load, c in zip(out_loads, chunks):
            load.wait()
            out_ref[:, c] = own_out[:, c].astype(narrow)

    def forward(i):
        @pl.loop(0, width // COLUMNS)
        def _(j):
            columns = columns_of(j)
            block = weights[i, :, :, :, :, columns].reshape(width, COLUMNS)
            activation = features_ref[...] if i == 0 else inputs[i - 1]
            summed = jnp.dot(activation, block, preferred_element_type=wide)
            logistic = jax.nn.sigmoid(summed)
            inputs[i, :, columns] = (summed * logistic).astype(narrow)
            factors[i, :, columns] = logistic * (1.0 + summed * (1.0 - logistic))

    def finish(i):
        for place in range(groups):
            for x_at in range(2):
                arrival = remote(
                    lambda place=place, x_at=x_at: (weights.at[i, place, x_at, 1 - core],) * 2,
                    (core_send, core_recv),
                    (i, place, x_at),
                    core_peer,
                )
                arrival.wait_recv()
        forward(i)

    relay(last, 0, x)
    cross(last, z)
    spread(last, 1 - x)
    for i in range(last):
        relay(i, 0, x)
    relay(last, 0, 1 - x)
    for i in range(last):
        cross(i, z)
    items = [(i, x) for i in range(last)] + [(last, x), (last, 1 - x)]
    for i, x_at in items:
        relay(i, 1, x_at)
    for i in range(last):
        cross(i, z_origins[0])
    inner = jnp.logical_and(z > 0, z < groups - 1)

    @pl.when(inner)
    def _():
        for i, x_at in items:
            relay(i, 2, x_at)

    for step, (i, x_at) in enumerate(items):

        @pl.when(jnp.logical_not(inner))
        def _():
            relay(i, 2, x_at, False)

        if step < last:
            cross(i, z_origins[1])
        if step >= 2:
            cross(step - 2, z_origins[2])
            finish(step - 2)
    finish(last)

    def update_out(j, decay, rate, other):
        c = chunks[j]

        @pl.loop(0, width // COLUMNS)
        def _(k):
            units = columns_of(k)
            grad = lax.dot_general(
                inputs[last, :, units],
                residual[:, c],
                (((0,), (0,)), ((), ())),
                preferred_element_type=wide,
            )
            if other is None:
                own_out[units, c] = decay * own_out[units, c] + grad
            else:
                fresh_momentum = decay * other[units, c].astype(wide) + grad
                own_out[units, c] = own_out[units, c] - rate * fresh_momentum

        keep_out[j].start()

    def update_solver(j):
        residuals[j].wait_recv()
        update_out(j, momentum_decay, None, None)

    def update_trainer(j):
        momenta[j].wait_recv()
        update_out(j, momentum_decay, step_size, got_out)

    core_sums, x_sums, z_sums, z_slopes, x_slopes, core_slopes = [], [], [], [], [], []

    def send_sum(views, j, slot, peer):
        return start(remote(views, (sum_send, sum_recv), (j, slot), peer), trainer_sends)

    @pl.when(trainer)
    def _():
        for j, c in enumerate(chunks):
            predicted = jnp.dot(inputs[last], out_ref[:, c], preferred_element_type=wide)
            residual[:, c] = ((predicted - own_fields[:, c]) / batch).astype(narrow)
            if j + 1 < len(chunks):
                start(residuals[j], trainer_sends)
        for j, columns in enumerate(parts):
            part = lax.dot_general(
                residual[...],
                out_ref[columns, :],
                (((1,), (1,)), ((), ())),
                preferred_element_type=wide,
            )
            partial[:, :, :, :, columns] = part.reshape(groups, 2, 2, rows, COLUMNS)
            core_sums.append(
                send_sum(
                    lambda columns=columns: (
                        partial.at[:, :, 1 - core, :, columns],
                        core_sum.at[:, :, :, columns],
                    ),
                    j,
                    0,
                    core_peer,
                )
            )
        for j, columns in enumerate(parts):
            core_sums[j].wait_recv()
            away = partial[:, 1 - x, core, :, columns] + core_sum[:, 1 - x, :, columns]
            x_away[:, :, columns] = away.astype(narrow)
            x_sums.append(
                send_sum(
                    lambda columns=columns: (x_away.at[:, :, columns], x_sum.at[:, :, columns]),
                    j,
                    1,
                    x_peer,
                )
            )
        update_trainer(0)
        for j, columns in enumerate(parts):
            near = partial[:, x, core, :, columns] + core_sum[:, x, :, columns]
            x_sums[j].wait_recv()
            near = near + x_sum[:, :, columns].astype(wide)
            partial[:, x, core, :, columns] = near
            z_away[:, :, columns] = near.astype(narrow)
            z_sums.append(
                [
                    send_sum(
                        lambda columns=columns, k=k: (
                            z_away.at[z_places[k], :, columns],
                            z_sum.at[k, :, columns],
                        ),
                        j,
                        2 + k,
                        z_peers[k],
                    )
                    for k in range(groups - 1)
                ]
            )
        update_trainer(1)

    @pl.when(solver)
    def _():
        update_solver(0)
        update_solver(1)

    own_rows = pl.ds(pl.multiple_of(tile * rows, rows), rows)

    def send_slope(view, j, slot, peer):
        return start(remote(twice(view), (slope_send, slope_recv), (j, slot), peer), sends)

    for j, columns in enumerate(parts):

        @pl.when(trainer)
        def _():
            upstream = partial[z, x, core, :, columns]
            for k in range(groups - 1):
                z_sums[j][k].wait_recv()
                upstream = upstream + z_sum[k, :, columns].astype(wide)
            slope[z, x, core, :, columns] = (upstream * factors[last, own_rows, columns]).astype(
                narrow
            )
            start(slope_shares[j], trainer_sends)

        @pl.when(solver)
        def _():
            slope_shares[j].wait_recv()

        view = lambda columns=columns: slope.at[z, x, core, :, columns]
        z_slopes.append([send_slope(view, j, k, z_peers[k]) for k in range(groups - 1)])

    @pl.when(trainer)
    def _():
        start(residuals[-1], trainer_sends)
        update_trainer(2)

    for j, columns in enumerate(parts):
        for copy in z_slopes[j]:
            copy.wait_recv()
        x_slopes.append(send_slope(
            lambda columns=columns: slope.at[:, x, core, :, columns], j, groups - 1, x_peer
        ))
    for j, columns in enumerate(parts):
        x_slopes[j].wait_recv()
        core_slopes.append(send_slope(
            lambda columns=columns: slope.at[:, :, core, :, columns], j, groups, core_peer
        ))

    @pl.when(trainer)
    def _():
        update_trainer(3)
        hidden_momentum.wait_recv()

    for copy in core_slopes:
        copy.wait_recv()

    per_block = LANES // unit_rows
    first_lane = pl.multiple_of((tile // per_block) * LANES, LANES)
    unit_first = pl.multiple_of(lax.rem(tile, per_block) * unit_rows, unit_rows)
    slopes = [slope.reshape(batch, width), slope_even, slope_odd]
    for step, i in enumerate(reversed(range(layer_count))):
        source = features_ref if i == 0 else inputs.at[i - 1]
        this_slope = slopes[0] if step == 0 else slopes[1 + step % 2]
        next_slope = slopes[1 + (step + 1) % 2]
        if i > 0:

            @pl.loop(0, width // COLUMNS)
            def _(j):
                columns = columns_of(j)
                block = weights.at[i].reshape(width, width)[columns, :]
                back = lax.dot_general(
                    this_slope[...],
                    block,
                    (((1,), (1,)), ((), ())),
                    preferred_element_type=wide,
                )
                next_slope[:, columns] = (back * factors[i - 1, :, columns]).astype(narrow)

        @pl.loop(0, width // COLUMNS)
        def _(j):
            columns = columns_of(j)
            gradient[:, columns] = lax.dot_general(
                source[:, pl.ds(first_lane, LANES)],
                this_slope[:, columns],
                (((0,), (0,)), ((), ())),
                preferred_element_type=wide,
            )

        own_units = pl.ds(unit_first, unit_rows)

        @pl.when(solver)
        def _():
            own_hidden[i] = momentum_decay * own_hidden[i] + gradient[own_units, :]

        @pl.when(trainer)
        def _():
            fresh_momentum = momentum_decay * got_hidden[i].astype(wide) + gradient[own_units, :]
            own_hidden[i] = own_hidden[i] - step_size * fresh_momentum

    keep_hidden.start()

    @pl.when(solver)
    def _():
        for j in range(2, len(chunks)):
            update_solver(j)

    @pl.when(trainer)
    def _():
        member = lax.broadcasted_iota(jnp.int32, (batch, batch), 0)
        chosen = jnp.where(member == assignment_ref[...], 1.0, 0.0).astype(narrow)
        for j, c in enumerate(chunks):
            fresh[j].wait_recv()
            own_fields[:, c] = lax.dot_general(
                chosen, got_fields[:, c], (((0,), (0,)), ((), ())), preferred_element_type=wide
            )
            keep_fields[j].start()

    for copy in sends:
        copy.wait_send()
    for i in range(layer_count):
        for place in range(groups):
            if i < last:
                x_copy(i, place).wait_send()
            for x_at in range(2):
                core_copy(i, place, x_at).wait_send()
    x_copy(last, z).wait_send()
    for i, x_at in spreads:

        @pl.when(z < groups - 1)
        def _():
            hop(i, z, x_at, 0, above).wait_send()

        @pl.when(z > 0)
        def _():
            hop(i, z, x_at, 1, below).wait_send()

    for i, k, x_at in relays:

        @pl.when(onward(k))
        def _():
            hop(i, z_origins[k], x_at, 0, above).wait_send()

    @pl.when(solver)
    def _():
        for copy in solver_sends:
            copy.wait_send()

    @pl.when(trainer)
    def _():
        for copy in trainer_sends:
            copy.wait_send()

    for copy in keeps:
        copy.wait()


def fused_step(fields, velocity, growth, features, assignment, own_out, own_hidden):
    layer_count, unit_rows, width = own_hidden.shape
    batch, cells = fields.shape
    groups = lax.axis_size("tile") // 4
    rows = batch // lax.axis_size("tile")
    narrow, wide = jnp.bfloat16, jnp.float32
    dma = pltpu.SemaphoreType.DMA
    anywhere = pl.BlockSpec(memory_space=pl.ANY)
    parts, pieces = width // COLUMNS, cells // COLUMNS
    role_slots = layer_count + 3 * pieces + 1 + parts
    return pl.pallas_call(
        functools.partial(train_kernel, groups),
        out_shape=(
            jax.ShapeDtypeStruct(fields.shape, wide),
            jax.ShapeDtypeStruct(own_out.shape, wide),
            jax.ShapeDtypeStruct(own_hidden.shape, wide),
        ),
        in_specs=[anywhere] * 7,
        out_specs=[anywhere] * 3,
        scratch_shapes=[
            pltpu.VMEM((batch, width), narrow),
            pltpu.VMEM((batch, cells), wide),
            pltpu.VMEM((width, cells), wide),
            pltpu.VMEM(own_hidden.shape, wide),
            pltpu.VMEM((1, cells), wide),
            pltpu.VMEM((1, cells), wide),
            pltpu.VMEM((1, batch), jnp.int32),
            pltpu.VMEM((1, LANES), wide),
            pltpu.VMEM((batch, LANES), wide),
            pltpu.VMEM((batch, LANES), wide),
            pltpu.VMEM((width, cells), narrow),
            pltpu.VMEM((width, cells), narrow),
            pltpu.VMEM(own_hidden.shape, narrow),
            pltpu.VMEM((batch, cells), narrow),
            pltpu.VMEM((layer_count, groups, 2, 2, unit_rows, width), narrow),
            pltpu.VMEM((layer_count, batch, width), narrow),
            pltpu.VMEM((layer_count, batch, width), wide),
            pltpu.VMEM((batch, cells), narrow),
            pltpu.VMEM((batch, width), narrow),
            pltpu.VMEM((batch, width), narrow),
            pltpu.VMEM((groups, 2, 2, rows, width), wide),
            pltpu.VMEM((groups, 2, 2, rows, width), narrow),
            pltpu.VMEM((LANES, width), wide),
            pltpu.VMEM((groups, 2, rows, width), wide),
            pltpu.VMEM((groups, rows, width), narrow),
            pltpu.VMEM((groups, rows, width), narrow),
            pltpu.VMEM((groups, rows, width), narrow),
            pltpu.VMEM((groups - 1, rows, width), narrow),
            dma((layer_count, groups, 2, 2)),
            dma((layer_count, groups, 2)),
            dma((layer_count, groups)),
            dma((layer_count, groups)),
            dma((layer_count, groups, 2)),
            dma((layer_count, groups, 2)),
            dma((parts, groups + 1)),
            dma((parts, groups + 1)),
            dma((parts, groups + 1)),
            dma((parts, groups + 1)),
            dma((role_slots,)),
            dma((role_slots,)),
            dma((3,)),
            dma((3,)),
            dma((6 + pieces,)),
            dma((2 * pieces + 1,)),
        ],
        compiler_params=pltpu.CompilerParams(
            collective_id=0, has_side_effects=True, vmem_limit_bytes=64000000
        ),
        cost_estimate=pl.CostEstimate(
            flops=60 * batch * width * width, bytes_accessed=40 * batch * width, transcendentals=0
        ),
    )(
        features,
        fields,
        velocity[None, :],
        growth[None, :],
        assignment[None, :],
        own_out,
        own_hidden,
    )


def plain_body(fields_pair, velocity, growth, features, assignment, out_pair, hidden_pair):
    solver_side = lax.axis_index("role") == 0
    own_fields = fields_pair[0]
    own_out = out_pair[0]
    own_hidden = hidden_pair[0]
    stacked = jnp.concatenate([own_fields, velocity[None, :]], axis=0)
    advanced = advance(extended(stacked, "tile", 1, 1), growth)
    grad_out, grad_hidden, other_out, other_hidden, fresh_fields = plain_training(
        features,
        own_hidden.astype(jnp.bfloat16),
        own_out.astype(jnp.bfloat16),
        own_fields,
        own_out,
        own_hidden,
        advanced.astype(jnp.bfloat16),
    )
    grad_out, grad_hidden, other_out, other_hidden = (
        v.astype(jnp.float32) for v in (grad_out, grad_hidden, other_out, other_hidden)
    )
    out_next = jnp.where(
        solver_side,
        momentum_decay * own_out + grad_out,
        own_out - step_size * (momentum_decay * other_out + grad_out),
    )
    hidden_next = jnp.where(
        solver_side,
        momentum_decay * own_hidden + other_hidden,
        own_hidden - step_size * (momentum_decay * other_hidden + grad_hidden),
    )
    next_batch = jnp.take(fresh_fields, assignment, axis=0).astype(jnp.float32)
    fields_next = jnp.where(solver_side, advanced, next_batch)
    return (fields_next[None], out_next[None], hidden_next[None])


def body(fields_pair, velocity, growth, features, assignment, out_pair, hidden_pair):
    tiles = lax.axis_size("tile")
    batch, cells = fields_pair.shape[1:]
    layer_count, unit_rows, width = hidden_pair.shape[1:]
    fits = (
        lax.axis_size("role") == 2
        and tiles == 16
        and layer_count > 2
        and batch % tiles == 0
        and (batch // tiles) % 16 == 0
        and LANES % unit_rows == 0
        and width % COLUMNS == 0
        and cells % COLUMNS == 0
        and cells // COLUMNS == 4
    )
    if not fits:
        return plain_body(
            fields_pair, velocity, growth, features, assignment, out_pair, hidden_pair
        )
    results = fused_step(
        fields_pair[0], velocity, growth, features, assignment, out_pair[0], hidden_pair[0]
    )
    return tuple(result[None] for result in results)


def solution(mesh):
    return jax.shard_map(
        body,
        mesh=mesh,
        in_specs=(
            P("role", None, "tile"),
            P("tile"),
            P("tile"),
            P(),
            P(),
            P("role", None, "tile"),
            P("role", None, "tile", None),
        ),
        out_specs=(P("role", None, "tile"), P("role", None, "tile"), P("role", None, "tile", None)),
        check_vma=False,
    )
```

```python
import functools

import jax
import jax.numpy as jnp
from jax import lax
from jax.experimental import pallas as pl
from jax.experimental.pallas import tpu as pltpu
from jax.sharding import PartitionSpec as P

momentum_decay = 0.9
step_size = 0.1


def extended(value, axis, dim, width):
    count, length = (lax.axis_size(axis), value.shape[dim])
    up = [(i, (i + 1) % count) for i in range(count)]
    down = [(j, i) for i, j in up]
    last = lax.slice_in_dim(value, length - width, length, axis=dim)
    leading = lax.slice_in_dim(value, 0, width, axis=dim)
    before = lax.ppermute(last, axis, up)
    after = lax.ppermute(leading, axis, down)
    return jnp.concatenate([before, value, after], axis=dim)


def silu_slope(values):
    logistic = jax.nn.sigmoid(values)
    return logistic * (1.0 + values * (1.0 - logistic))


def advance(padded, growth):
    states = padded[:-1]
    velocity_row = padded[-1]
    outflow = (
        jnp.maximum(velocity_row[:-1], 0.0) * states[:, :-1]
        + jnp.minimum(velocity_row[:-1], 0.0) * states[:, 1:]
    )
    carried = states[:, 1:-1] - outflow[:, 1:] + outflow[:, :-1]
    return carried + growth * carried * (1.0 - carried)


def to_trainer(value):
    return lax.ppermute(value.astype(jnp.bfloat16), "role", [(0, 1)])


def to_solver(value):
    return lax.ppermute(value.astype(jnp.bfloat16), "role", [(1, 0)])


def plain_training(features, hidden_narrow, out_narrow, own_fields, own_out, own_hidden, fields):
    layer_count, unit_rows = own_hidden.shape[:2]
    batch = own_fields.shape[0]
    first_unit = lax.axis_index("tile") * unit_rows
    momentum_out = to_trainer(own_out)
    momentum_hidden = to_trainer(own_hidden)
    full_hidden = [
        lax.all_gather(hidden_narrow[i], "tile", axis=0, tiled=True) for i in range(layer_count)
    ]
    inputs, summed_list = [], []
    activation = features
    for i in range(layer_count):
        inputs.append(activation)
        summed = jnp.dot(activation, full_hidden[i], preferred_element_type=jnp.float32)
        summed_list.append(summed)
        activation = jax.nn.silu(summed).astype(jnp.bfloat16)
    predicted = jnp.dot(activation, out_narrow, preferred_element_type=jnp.float32)
    residual = ((predicted - own_fields) / batch).astype(jnp.bfloat16)
    partial_grad = lax.dot_general(
        residual, out_narrow, (((1,), (1,)), ((), ())), preferred_element_type=jnp.float32
    )
    upstream = lax.psum(partial_grad, "tile")
    grad_out = jnp.dot(activation.T, residual, preferred_element_type=jnp.float32)
    sent_out = to_solver(grad_out)
    gradients, sent = [], []
    for i in reversed(range(layer_count)):
        slope = (upstream * silu_slope(summed_list[i])).astype(jnp.bfloat16)
        own_inputs = lax.dynamic_slice_in_dim(inputs[i], first_unit, unit_rows, 1)
        gradient = jnp.dot(own_inputs.T, slope, preferred_element_type=jnp.float32)
        gradients.append(gradient)
        sent.append(to_solver(gradient))
        if i > 0:
            upstream = lax.dot_general(
                slope, full_hidden[i], (((1,), (1,)), ((), ())), preferred_element_type=jnp.float32
            )
    solver_side = lax.axis_index("role") == 0
    grad_out = jnp.where(solver_side, sent_out.astype(jnp.float32), grad_out)
    other_hidden = jnp.where(solver_side, jnp.stack(sent[::-1]), momentum_hidden)
    return grad_out, jnp.stack(gradients[::-1]), momentum_out, other_hidden, to_trainer(fields)


LANES = 128
COLUMNS = 256


class Later:
    def __init__(self, build):
        self.build = build

    def start(self):
        self.build().start()

    def wait(self):
        self.build().wait()

    def wait_recv(self):
        self.build().wait_recv()

    def wait_send(self):
        self.build().wait_send()


def train_kernel(
    groups,
    features_hbm,
    fields_hbm,
    velocity_hbm,
    growth_hbm,
    assignment_hbm,
    out_hbm,
    hidden_hbm,
    own_fields,
    own_out,
    own_hidden,
    features_ref,
    velocity_ref,
    growth_ref,
    assignment_ref,
    left_velocity,
    left_edge,
    right_edge,
    out_ref,
    got_out,
    got_hidden,
    got_fields,
    weights,
    inputs,
    top,
    factors,
    residual,
    slope_even,
    slope_odd,
    partial,
    core_away,
    slope,
    gradient,
    got_gradient,
    core_sum,
    x_away,
    x_sum,
    z_away,
    z_sum,
    z_send,
    z_recv,
    x_send,
    x_recv,
    core_send,
    core_recv,
    sum_send,
    sum_recv,
    slope_send,
    slope_recv,
    role_send,
    role_recv,
    pair_send,
    pair_recv,
    edge_send,
    edge_recv,
    local_sem,
):
    layer_count, unit_rows, width = hidden_hbm.shape
    batch, cells = fields_hbm.shape
    rows = partial.shape[2]
    half = batch // 2
    narrow, wide = jnp.bfloat16, jnp.float32
    tiles = groups * 4
    last = layer_count - 1
    role = lax.axis_index("role")
    tile = lax.axis_index("tile")
    core = lax.rem(tile, 2)
    x = lax.rem(tile // 2, 2)
    z = tile // 4
    solver = role == 0
    trainer = role == 1

    def device(z_at, x_at, core_at):
        return (role, z_at * 4 + x_at * 2 + core_at)

    z_places = [lax.rem(z + k, groups) for k in range(1, groups)]
    z_peers = [device(place, x, core) for place in z_places]
    x_peer = device(z, 1 - x, core)
    core_peer = device(z, x, 1 - core)
    role_peer = (1 - role, tile)
    right_peer = (role, lax.rem(tile + 1, tiles))
    left_peer = (role, lax.rem(tile + tiles - 1, tiles))
    far_peer = (role, lax.rem(tile + tiles - 1 + 2 * core, tiles))
    sends, solver_sends, trainer_sends = [], [], []

    def remote(views, semaphores, slot, peer, recv_slot=None):
        def build():
            source, target = views()
            return pltpu.make_async_remote_copy(
                src_ref=source,
                dst_ref=target,
                send_sem=semaphores[0].at[slot],
                recv_sem=semaphores[1].at[slot if recv_slot is None else recv_slot],
                device_id=peer,
                device_id_type=pl.DeviceIdType.MESH,
            )

        return Later(build)

    def local(views, semaphores, slot):
        def build():
            source, target = views()
            return pltpu.make_async_copy(source, target, semaphores.at[slot])

        return Later(build)

    def twice(view):
        return lambda: (view(),) * 2

    def start(copy, among):
        copy.start()
        among.append(copy)
        return copy

    role_slots = [0]

    def across(view):
        slot = role_slots[0]
        role_slots[0] += 1
        return remote(twice(view), (role_send, role_recv), slot, role_peer)

    chunks = [pl.ds(j * COLUMNS, COLUMNS) for j in range(cells // COLUMNS)]
    parts = [pl.ds(j * COLUMNS, COLUMNS) for j in range(width // COLUMNS)]
    pieces = [pl.ds(j * LANES, LANES) for j in range(width // LANES)]
    per_part = COLUMNS // LANES
    shares = [across(lambda i=i: weights.at[i, z, x, core]) for i in range(layer_count)]
    momenta = [across(lambda c=c: got_out.at[:, c]) for c in chunks]
    hidden_momentum = across(lambda: got_hidden)
    fresh = [across(lambda c=c: got_fields.at[:, c]) for c in chunks]
    residuals = [across(lambda c=c: residual.at[:, :, :, :, c]) for c in chunks]
    slope_shares = [across(lambda c=c: slope.at[z, x, :, c]) for c in pieces]

    pairs = [lambda: (hidden_hbm, own_hidden)]
    pairs += [lambda c=c: (out_hbm.at[:, c], own_out.at[:, c]) for c in chunks]
    pairs += [
        lambda: (fields_hbm, own_fields),
        lambda: (velocity_hbm, velocity_ref),
        lambda: (growth_hbm, growth_ref),
        lambda: (assignment_hbm, assignment_ref),
        lambda: (features_hbm, features_ref),
    ]
    loads = [local(views, local_sem, k) for k, views in enumerate(pairs)]
    for load in loads:
        load.start()
    hidden_load, out_loads, small_loads = loads[0], loads[1 : 1 + len(chunks)], loads[1 + len(chunks) :]
    barrier = pltpu.get_barrier_semaphore()
    peers = z_peers + [x_peer, core_peer, role_peer, far_peer]
    for peer in peers:
        pl.semaphore_signal(barrier, inc=1, device_id=peer, device_id_type=pl.DeviceIdType.MESH)
    pl.semaphore_wait(barrier, len(peers))

    last_lanes = pl.ds(cells - LANES, LANES)
    edge_list = [
        (lambda: (fields_hbm.at[:, last_lanes], left_edge), right_peer),
        (lambda: (velocity_hbm.at[:, last_lanes], left_velocity), right_peer),
        (lambda: (fields_hbm.at[:, pl.ds(0, LANES)], right_edge), left_peer),
    ]
    edges = [
        remote(views, (edge_send, edge_recv), k, peer) for k, (views, peer) in enumerate(edge_list)
    ]

    nearest = [
        sorted((p for p in range(groups) if p != q), key=lambda p: (abs(p - q), p))
        for q in range(groups)
    ]

    def pick(k):
        place = jnp.int32(nearest[0][k])
        for q in range(1, groups):
            place = jnp.where(z == q, nearest[q][k], place)
        return place

    z_origins = [pick(k) for k in range(groups - 1)]
    above = device(lax.rem(z + 1, groups), x, core)
    below = device(lax.rem(z + groups - 1, groups), x, core)
    spreads, relays = [], []

    def share_of(i, place, x_at):
        return twice(lambda: weights.at[i, place, x_at, core])

    def hop(i, place, x_at, slot, peer):
        return remote(
            share_of(i, place, x_at), (z_send, z_recv), (i, place, x_at, slot), peer, (i, place, x_at)
        )

    def spread(i, x_at):
        @pl.when(z < groups - 1)
        def _():
            hop(i, z, x_at, 0, above).start()

        @pl.when(z > 0)
        def _():
            hop(i, z, x_at, 1, below).start()

        spreads.append((i, x_at))

    def onward(k):
        rising = z_origins[k] < z
        return jnp.logical_or(
            jnp.logical_and(rising, z < groups - 1),
            jnp.logical_and(jnp.logical_not(rising), z > 0),
        )

    def relay(i, k, x_at, noted=True):
        place = z_origins[k]
        target = jnp.where(place < z, lax.rem(z + 1, groups), lax.rem(z + groups - 1, groups))
        hop(i, place, x_at, 0, above).wait_recv()

        @pl.when(onward(k))
        def _():
            hop(i, place, x_at, 0, device(target, x, core)).start()

        if noted:
            relays.append((i, k, x_at))
        if i < last:
            send_x(i, place)
        send_core(i, place, x_at)

    def x_copy(i, place):
        return remote(share_of(i, place, x), (x_send, x_recv), (i, place), x_peer)

    def x_arrival(i, place):
        return remote(share_of(i, place, 1 - x), (x_send, x_recv), (i, place), x_peer)

    def core_copy(i, place, x_at):
        return remote(share_of(i, place, x_at), (core_send, core_recv), (i, place, x_at), core_peer)

    def send_x(i, place):
        x_copy(i, place).start()

    def send_core(i, place, x_at):
        core_copy(i, place, x_at).start()

    def cross(i, place):
        x_arrival(i, place).wait_recv()
        send_core(i, place, 1 - x)

    def send_share(i):
        @pl.when(solver)
        def _():
            shares[i].wait_recv()

        spread(i, x)
        send_x(i, z)
        send_core(i, z, x)

    share_order = [last] + list(range(last))

    def columns_of(j):
        return pl.ds(pl.multiple_of(j * COLUMNS, COLUMNS), COLUMNS)

    def advance():
        velocity = velocity_ref[...]
        forward_speed = jnp.maximum(velocity, 0.0)
        backward_speed = jnp.minimum(velocity, 0.0)
        growth = growth_ref[...]
        before = left_velocity[:, LANES - 1 :]
        step = LANES // 2

        @pl.loop(0, batch // step)
        def _(j):
            band = pl.ds(pl.multiple_of(j * step, step), step)
            current = own_fields[band, :]
            lane = lax.broadcasted_iota(jnp.int32, current.shape, 1)
            following = jnp.where(
                lane == cells - 1, right_edge[band, :1], pltpu.roll(current, cells - 1, 1)
            )
            outflow = forward_speed * current + backward_speed * following
            inflow_edge = (
                jnp.maximum(before, 0.0) * left_edge[band, :][:, LANES - 1 :]
                + jnp.minimum(before, 0.0) * current[:, :1]
            )
            inflow = jnp.where(lane == 0, inflow_edge, pltpu.roll(outflow, 1, 1))
            carried = current - outflow + inflow
            advanced = carried + growth * carried * (1.0 - carried)
            own_fields[band, :] = advanced
            got_fields[band, :] = advanced.astype(narrow)

    @pl.when(solver)
    def _():
        for copy in edges:
            start(copy, solver_sends)
        for load, c, copy in zip(out_loads, chunks, momenta):
            load.wait()
            got_out[:, c] = own_out[:, c].astype(narrow)
            start(copy, solver_sends)
        hidden_load.wait()
        got_hidden[...] = own_hidden[...].astype(narrow)
        start(hidden_momentum, solver_sends)

    @pl.when(trainer)
    def _():
        hidden_load.wait()
        for i in range(layer_count):
            weights[i, z, x, core] = own_hidden[i].astype(narrow)
        for i in share_order:
            start(shares[i], trainer_sends)

    for i in share_order:
        send_share(i)

    for load in small_loads:
        load.wait()

    @pl.when(solver)
    def _():
        for copy in edges:
            copy.wait_recv()
        advance()
        for copy in fresh:
            start(copy, solver_sends)

    @pl.when(trainer)
    def _():
        for load, c in zip(out_loads, chunks):
            load.wait()
            out_ref[:, c] = own_out[:, c].astype(narrow)

    pair_slots = [0]

    def beside(views):
        slot = pair_slots[0]
        pair_slots[0] += 1
        return remote(views, (pair_send, pair_recv), slot, core_peer)

    tops = [beside(twice(lambda c=c: top.at[:, :, core, :, c])) for c in parts]
    own_units = pl.ds(pl.multiple_of(core * unit_rows, unit_rows), unit_rows)
    other_units = pl.ds(pl.multiple_of((1 - core) * unit_rows, unit_rows), unit_rows)
    halves = [
        beside(lambda i=i: (gradient.at[i, other_units, :], got_gradient.at[i]))
        for i in range(layer_count)
    ]

    def forward_columns(i, columns):
        block = weights[i, :, :, :, :, columns].reshape(width, COLUMNS)
        activation = features_ref[:, :, core] if i == 0 else inputs[i - 1]
        summed = jnp.dot(activation.reshape(half, width), block, preferred_element_type=wide)
        logistic = jax.nn.sigmoid(summed)
        result = (summed * logistic).astype(narrow).reshape(groups, 2, rows, COLUMNS)
        factor = logistic * (1.0 + summed * (1.0 - logistic))
        factors[i, :, :, :, columns] = factor.reshape(groups, 2, rows, COLUMNS)
        return result

    def forward(i):
        if i == last:
            for c, copy in zip(parts, tops):
                top[:, :, core, :, c] = forward_columns(i, c)
                start(copy, sends)
        else:

            @pl.loop(0, width // COLUMNS)
            def _(j):
                columns = columns_of(j)
                inputs[i, :, :, :, columns] = forward_columns(i, columns)

    def finish(i):
        for place in range(groups):
            for x_at in range(2):
                arrival = remote(
                    lambda place=place, x_at=x_at: (weights.at[i, place, x_at, 1 - core],) * 2,
                    (core_send, core_recv),
                    (i, place, x_at),
                    core_peer,
                )
                arrival.wait_recv()
        forward(i)

    relay(last, 0, x)
    cross(last, z)
    spread(last, 1 - x)
    for i in range(last):
        relay(i, 0, x)
    relay(last, 0, 1 - x)
    for i in range(last):
        cross(i, z)
    items = [(i, x) for i in range(last)] + [(last, x), (last, 1 - x)]
    for i, x_at in items:
        relay(i, 1, x_at)
    for i in range(last):
        cross(i, z_origins[0])
    inner = jnp.logical_and(z > 0, z < groups - 1)

    @pl.when(inner)
    def _():
        for i, x_at in items:
            relay(i, 2, x_at)

    for step, (i, x_at) in enumerate(items):

        @pl.when(jnp.logical_not(inner))
        def _():
            relay(i, 2, x_at, False)

        if step < last:
            cross(i, z_origins[1])
        if step >= 2:
            cross(step - 2, z_origins[2])
            finish(step - 2)
    finish(last)

    def update_out(j, decay, rate, other):
        c = chunks[j]

        @pl.loop(0, width // COLUMNS)
        def _(k):
            units = columns_of(k)
            grad = lax.dot_general(
                top[:, :, :, :, units].reshape(batch, COLUMNS),
                residual[:, :, :, :, c].reshape(batch, COLUMNS),
                (((0,), (0,)), ((), ())),
                preferred_element_type=wide,
            )
            if other is None:
                own_out[units, c] = decay * own_out[units, c] + grad
            else:
                fresh_momentum = decay * other[units, c].astype(wide) + grad
                own_out[units, c] = own_out[units, c] - rate * fresh_momentum

    def update_solver(j):
        residuals[j].wait_recv()
        update_out(j, momentum_decay, None, None)

    def update_trainer(j):
        momenta[j].wait_recv()
        update_out(j, momentum_decay, step_size, got_out)

    x_sums, z_sums = [], []

    def send_sum(views, j, slot, peer):
        return start(remote(views, (sum_send, sum_recv), (j, slot), peer), trainer_sends)

    core_sums = [
        remote(
            lambda c=c: (core_away.at[:, :, :, c], core_sum.at[:, :, :, c]),
            (sum_send, sum_recv),
            (j, 0),
            core_peer,
        )
        for j, c in enumerate(parts)
    ]
    targets = own_fields.reshape(groups, 2, 2, rows, cells)

    def residual_columns(side, c):
        rows_of = top[:, :, side].reshape(half, width)
        predicted = jnp.dot(rows_of, out_ref[:, c], preferred_element_type=wide)
        wanted = targets[:, :, side, :, c].reshape(half, COLUMNS)
        kept = ((predicted - wanted) / batch).astype(narrow)
        residual[:, :, side, :, c] = kept.reshape(groups, 2, rows, COLUMNS)

    def upstream_columns(side, c):
        return lax.dot_general(
            residual[:, :, side].reshape(half, cells),
            out_ref[c, :],
            (((1,), (1,)), ((), ())),
            preferred_element_type=wide,
        ).reshape(groups, 2, rows, COLUMNS)

    @pl.when(trainer)
    def _():
        for c in chunks:
            residual_columns(core, c)
        for copy in tops:
            copy.wait_recv()
        for j, c in enumerate(chunks):
            residual_columns(1 - core, c)
            if j < 2:
                start(residuals[j], trainer_sends)
        for c, copy in zip(parts, core_sums):
            core_away[:, :, :, c] = upstream_columns(1 - core, c)
            start(copy, trainer_sends)
        for j, c in enumerate(parts):
            partial[:, :, :, c] = upstream_columns(core, c)
            core_sums[j].wait_recv()
            x_away[:, :, c] = (partial[:, 1 - x, :, c] + core_sum[:, 1 - x, :, c]).astype(narrow)
            for q in range(j * per_part, (j + 1) * per_part):
                x_sums.append(
                    send_sum(
                        lambda c=pieces[q]: (x_away.at[:, :, c], x_sum.at[:, :, c]), q, 1, x_peer
                    )
                )
        update_trainer(0)
        for j, c in enumerate(pieces):
            near = partial[:, x, :, c] + core_sum[:, x, :, c]
            x_sums[j].wait_recv()
            near = near + x_sum[:, :, c].astype(wide)
            partial[:, x, :, c] = near
            z_away[:, :, c] = near.astype(narrow)
            z_sums.append(
                [
                    send_sum(
                        lambda c=c, k=k: (z_away.at[z_places[k], :, c], z_sum.at[k, :, c]),
                        j,
                        2 + k,
                        z_peers[k],
                    )
                    for k in range(groups - 1)
                ]
            )
        update_trainer(1)

    @pl.when(solver)
    def _():
        for copy in tops:
            copy.wait_recv()
        update_solver(0)
        update_solver(1)

    def send_slope(view, j, slot, peer):
        return start(remote(twice(view), (slope_send, slope_recv), (j, slot), peer), sends)

    z_slopes, x_slopes = [], []
    for j, c in enumerate(pieces):

        @pl.when(trainer)
        def _():
            upstream = partial[z, x, :, c]
            for k in range(groups - 1):
                z_sums[j][k].wait_recv()
                upstream = upstream + z_sum[k, :, c].astype(wide)
            slope[z, x, :, c] = (upstream * factors[last, z, x, :, c]).astype(narrow)
            start(slope_shares[j], trainer_sends)

        @pl.when(solver)
        def _():
            slope_shares[j].wait_recv()

        view = lambda c=c: slope.at[z, x, :, c]
        z_slopes.append([send_slope(view, j, k, z_peers[k]) for k in range(groups - 1)])

    @pl.when(trainer)
    def _():
        for copy in residuals[2:]:
            start(copy, trainer_sends)
        update_trainer(2)

    for j, c in enumerate(pieces):
        for copy in z_slopes[j]:
            copy.wait_recv()
        x_slopes.append(send_slope(lambda c=c: slope.at[:, x, :, c], j, groups - 1, x_peer))

    @pl.when(trainer)
    def _():
        update_trainer(3)
        hidden_momentum.wait_recv()

    for copy in x_slopes:
        copy.wait_recv()

    first_lane = pl.multiple_of((tile // 2) * LANES, LANES)

    def update_hidden(i):
        halves[i].wait_recv()
        total = gradient[i, own_units, :] + got_gradient[i]

        @pl.when(solver)
        def _():
            own_hidden[i] = momentum_decay * own_hidden[i] + total

        @pl.when(trainer)
        def _():
            fresh_momentum = momentum_decay * got_hidden[i].astype(wide) + total
            own_hidden[i] = own_hidden[i] - step_size * fresh_momentum

    slopes = [slope, slope_even, slope_odd]
    for step, i in enumerate(reversed(range(layer_count))):
        this_slope = slopes[0] if step == 0 else slopes[1 + step % 2]
        next_slope = slopes[1 + (step + 1) % 2]
        if i > 0:

            @pl.loop(0, width // COLUMNS)
            def _(j):
                columns = columns_of(j)
                block = weights.at[i].reshape(width, width)[columns, :]
                back = lax.dot_general(
                    this_slope[...].reshape(half, width),
                    block,
                    (((1,), (1,)), ((), ())),
                    preferred_element_type=wide,
                )
                factor = factors[i - 1, :, :, :, columns].reshape(half, COLUMNS)
                next_slope[:, :, :, columns] = (
                    (back * factor).astype(narrow).reshape(groups, 2, rows, COLUMNS)
                )

        lanes = pl.ds(first_lane, LANES)
        own_inputs = features_ref[:, :, core, :, lanes] if i == 0 else inputs[i - 1, :, :, :, lanes]

        @pl.loop(0, width // COLUMNS)
        def _(j):
            columns = columns_of(j)
            gradient[i, :, columns] = lax.dot_general(
                own_inputs.reshape(half, LANES),
                this_slope[:, :, :, columns].reshape(half, COLUMNS),
                (((0,), (0,)), ((), ())),
                preferred_element_type=wide,
            )

        start(halves[i], sends)
        if i < last:
            update_hidden(i + 1)

    @pl.when(solver)
    def _():
        for j in range(2, len(chunks)):
            update_solver(j)

    @pl.when(trainer)
    def _():
        member = lax.broadcasted_iota(jnp.int32, (batch, batch), 0)
        chosen = jnp.where(member == assignment_ref[...], 1.0, 0.0).astype(narrow)
        for j, c in enumerate(chunks):
            fresh[j].wait_recv()
            own_fields[:, c] = lax.dot_general(
                chosen, got_fields[:, c], (((0,), (0,)), ((), ())), preferred_element_type=wide
            )

    update_hidden(0)

    for copy in sends:
        copy.wait_send()
    for i in range(layer_count):
        for place in range(groups):
            if i < last:
                x_copy(i, place).wait_send()
            for x_at in range(2):
                core_copy(i, place, x_at).wait_send()
    x_copy(last, z).wait_send()
    for i, x_at in spreads:

        @pl.when(z < groups - 1)
        def _():
            hop(i, z, x_at, 0, above).wait_send()

        @pl.when(z > 0)
        def _():
            hop(i, z, x_at, 1, below).wait_send()

    for i, k, x_at in relays:

        @pl.when(onward(k))
        def _():
            hop(i, z_origins[k], x_at, 0, above).wait_send()

    @pl.when(solver)
    def _():
        for copy in solver_sends:
            copy.wait_send()

    @pl.when(trainer)
    def _():
        for copy in trainer_sends:
            copy.wait_send()


def fused_step(fields, velocity, growth, features, assignment, own_out, own_hidden):
    layer_count, unit_rows, width = own_hidden.shape
    batch, cells = fields.shape
    groups = lax.axis_size("tile") // 4
    rows = batch // lax.axis_size("tile")
    narrow, wide = jnp.bfloat16, jnp.float32
    dma = pltpu.SemaphoreType.DMA
    anywhere = pl.BlockSpec(memory_space=pltpu.HBM)
    parts, pieces = width // COLUMNS, cells // COLUMNS
    splits = width // LANES
    role_slots = layer_count + 3 * pieces + 1 + splits
    split = (groups, 2, 2, rows, width)
    return pl.pallas_call(
        functools.partial(train_kernel, groups),
        out_shape=(
            jax.ShapeDtypeStruct(fields.shape, wide),
            jax.ShapeDtypeStruct(own_out.shape, wide),
            jax.ShapeDtypeStruct(own_hidden.shape, wide),
        ),
        in_specs=[anywhere] * 7,
        out_specs=[pl.BlockSpec(memory_space=pltpu.VMEM)] * 3,
        scratch_shapes=[
            pltpu.VMEM(split, narrow),
            pltpu.VMEM((1, cells), wide),
            pltpu.VMEM((1, cells), wide),
            pltpu.VMEM((1, batch), jnp.int32),
            pltpu.VMEM((1, LANES), wide),
            pltpu.VMEM((batch, LANES), wide),
            pltpu.VMEM((batch, LANES), wide),
            pltpu.VMEM((width, cells), narrow),
            pltpu.VMEM((width, cells), narrow),
            pltpu.VMEM(own_hidden.shape, narrow),
            pltpu.VMEM((batch, cells), narrow),
            pltpu.VMEM((layer_count, groups, 2, 2, unit_rows, width), narrow),
            pltpu.VMEM((layer_count - 1, groups, 2, rows, width), narrow),
            pltpu.VMEM(split, narrow),
            pltpu.VMEM((layer_count, groups, 2, rows, width), wide),
            pltpu.VMEM((groups, 2, 2, rows, cells), narrow),
            pltpu.VMEM((groups, 2, rows, width), narrow),
            pltpu.VMEM((groups, 2, rows, width), narrow),
            pltpu.VMEM((groups, 2, rows, width), wide),
            pltpu.VMEM((groups, 2, rows, width), wide),
            pltpu.VMEM((groups, 2, rows, width), narrow),
            pltpu.VMEM((layer_count, LANES, width), wide),
            pltpu.VMEM(own_hidden.shape, wide),
            pltpu.VMEM((groups, 2, rows, width), wide),
            pltpu.VMEM((groups, rows, width), narrow),
            pltpu.VMEM((groups, rows, width), narrow),
            pltpu.VMEM((groups, rows, width), narrow),
            pltpu.VMEM((groups - 1, rows, width), narrow),
            dma((layer_count, groups, 2, 2)),
            dma((layer_count, groups, 2)),
            dma((layer_count, groups)),
            dma((layer_count, groups)),
            dma((layer_count, groups, 2)),
            dma((layer_count, groups, 2)),
            dma((splits, groups + 1)),
            dma((splits, groups + 1)),
            dma((splits, groups)),
            dma((splits, groups)),
            dma((role_slots,)),
            dma((role_slots,)),
            dma((parts + layer_count,)),
            dma((parts + layer_count,)),
            dma((3,)),
            dma((3,)),
            dma((6 + pieces,)),
        ],
        compiler_params=pltpu.CompilerParams(
            collective_id=0, has_side_effects=True, vmem_limit_bytes=46000000
        ),
        cost_estimate=pl.CostEstimate(
            flops=60 * batch * width * width, bytes_accessed=40 * batch * width, transcendentals=0
        ),
    )(
        *(
            pltpu.with_memory_space_constraint(value, pltpu.HBM)
            for value in (
                features.reshape(split),
                fields,
                velocity[None, :],
                growth[None, :],
                assignment[None, :],
                own_out,
                own_hidden,
            )
        )
    )


def plain_body(fields_pair, velocity, growth, features, assignment, out_pair, hidden_pair):
    solver_side = lax.axis_index("role") == 0
    own_fields = fields_pair[0]
    own_out = out_pair[0]
    own_hidden = hidden_pair[0]
    stacked = jnp.concatenate([own_fields, velocity[None, :]], axis=0)
    advanced = advance(extended(stacked, "tile", 1, 1), growth)
    grad_out, grad_hidden, other_out, other_hidden, fresh_fields = plain_training(
        features,
        own_hidden.astype(jnp.bfloat16),
        own_out.astype(jnp.bfloat16),
        own_fields,
        own_out,
        own_hidden,
        advanced.astype(jnp.bfloat16),
    )
    grad_out, grad_hidden, other_out, other_hidden = (
        v.astype(jnp.float32) for v in (grad_out, grad_hidden, other_out, other_hidden)
    )
    out_next = jnp.where(
        solver_side,
        momentum_decay * own_out + grad_out,
        own_out - step_size * (momentum_decay * other_out + grad_out),
    )
    hidden_next = jnp.where(
        solver_side,
        momentum_decay * own_hidden + other_hidden,
        own_hidden - step_size * (momentum_decay * other_hidden + grad_hidden),
    )
    next_batch = jnp.take(fresh_fields, assignment, axis=0).astype(jnp.float32)
    fields_next = jnp.where(solver_side, advanced, next_batch)
    return (fields_next[None], out_next[None], hidden_next[None])


def body(fields_pair, velocity, growth, features, assignment, out_pair, hidden_pair):
    tiles = lax.axis_size("tile")
    batch, cells = fields_pair.shape[1:]
    layer_count, unit_rows, width = hidden_pair.shape[1:]
    fits = (
        lax.axis_size("role") == 2
        and tiles == 16
        and layer_count > 2
        and batch % tiles == 0
        and (batch // tiles) % 16 == 0
        and LANES == 2 * unit_rows
        and width % COLUMNS == 0
        and cells % COLUMNS == 0
        and cells // COLUMNS == 4
    )
    if not fits:
        return plain_body(
            fields_pair, velocity, growth, features, assignment, out_pair, hidden_pair
        )
    results = fused_step(
        fields_pair[0], velocity, growth, features, assignment, out_pair[0], hidden_pair[0]
    )
    return tuple(result[None] for result in results)


def solution(mesh):
    return jax.shard_map(
        body,
        mesh=mesh,
        in_specs=(
            P("role", None, "tile"),
            P("tile"),
            P("tile"),
            P(),
            P(),
            P("role", None, "tile"),
            P("role", None, "tile", None),
        ),
        out_specs=(P("role", None, "tile"), P("role", None, "tile"), P("role", None, "tile", None)),
        check_vma=False,
    )
```

```python
import functools

import jax
import jax.numpy as jnp
from jax import lax
from jax.experimental import pallas as pl
from jax.experimental.pallas import tpu as pltpu
from jax.sharding import PartitionSpec as P

momentum_decay = 0.9
step_size = 0.1


def extended(value, axis, dim, width):
    count, length = (lax.axis_size(axis), value.shape[dim])
    up = [(i, (i + 1) % count) for i in range(count)]
    down = [(j, i) for i, j in up]
    last = lax.slice_in_dim(value, length - width, length, axis=dim)
    leading = lax.slice_in_dim(value, 0, width, axis=dim)
    before = lax.ppermute(last, axis, up)
    after = lax.ppermute(leading, axis, down)
    return jnp.concatenate([before, value, after], axis=dim)


def silu_slope(values):
    logistic = jax.nn.sigmoid(values)
    return logistic * (1.0 + values * (1.0 - logistic))


def advance(padded, growth):
    states = padded[:-1]
    velocity_row = padded[-1]
    outflow = (
        jnp.maximum(velocity_row[:-1], 0.0) * states[:, :-1]
        + jnp.minimum(velocity_row[:-1], 0.0) * states[:, 1:]
    )
    carried = states[:, 1:-1] - outflow[:, 1:] + outflow[:, :-1]
    return carried + growth * carried * (1.0 - carried)


def to_trainer(value):
    return lax.ppermute(value.astype(jnp.bfloat16), "role", [(0, 1)])


def to_solver(value):
    return lax.ppermute(value.astype(jnp.bfloat16), "role", [(1, 0)])


def plain_training(features, hidden_narrow, out_narrow, own_fields, own_out, own_hidden, fields):
    layer_count, unit_rows = own_hidden.shape[:2]
    batch = own_fields.shape[0]
    first_unit = lax.axis_index("tile") * unit_rows
    momentum_out = to_trainer(own_out)
    momentum_hidden = to_trainer(own_hidden)
    full_hidden = [
        lax.all_gather(hidden_narrow[i], "tile", axis=0, tiled=True) for i in range(layer_count)
    ]
    inputs, summed_list = [], []
    activation = features
    for i in range(layer_count):
        inputs.append(activation)
        summed = jnp.dot(activation, full_hidden[i], preferred_element_type=jnp.float32)
        summed_list.append(summed)
        activation = jax.nn.silu(summed).astype(jnp.bfloat16)
    predicted = jnp.dot(activation, out_narrow, preferred_element_type=jnp.float32)
    residual = ((predicted - own_fields) / batch).astype(jnp.bfloat16)
    partial_grad = lax.dot_general(
        residual, out_narrow, (((1,), (1,)), ((), ())), preferred_element_type=jnp.float32
    )
    upstream = lax.psum(partial_grad, "tile")
    grad_out = jnp.dot(activation.T, residual, preferred_element_type=jnp.float32)
    sent_out = to_solver(grad_out)
    gradients, sent = [], []
    for i in reversed(range(layer_count)):
        slope = (upstream * silu_slope(summed_list[i])).astype(jnp.bfloat16)
        own_inputs = lax.dynamic_slice_in_dim(inputs[i], first_unit, unit_rows, 1)
        gradient = jnp.dot(own_inputs.T, slope, preferred_element_type=jnp.float32)
        gradients.append(gradient)
        sent.append(to_solver(gradient))
        if i > 0:
            upstream = lax.dot_general(
                slope, full_hidden[i], (((1,), (1,)), ((), ())), preferred_element_type=jnp.float32
            )
    solver_side = lax.axis_index("role") == 0
    grad_out = jnp.where(solver_side, sent_out.astype(jnp.float32), grad_out)
    other_hidden = jnp.where(solver_side, jnp.stack(sent[::-1]), momentum_hidden)
    return grad_out, jnp.stack(gradients[::-1]), momentum_out, other_hidden, to_trainer(fields)


LANES = 128
COLUMNS = 256


class Later:
    def __init__(self, build):
        self.build = build

    def start(self):
        self.build().start()

    def wait(self):
        self.build().wait()

    def wait_recv(self):
        self.build().wait_recv()

    def wait_send(self):
        self.build().wait_send()


def train_kernel(
    groups,
    features_hbm,
    fields_hbm,
    velocity_hbm,
    growth_hbm,
    assignment_hbm,
    out_hbm,
    hidden_hbm,
    own_fields,
    own_out,
    own_hidden,
    features_ref,
    velocity_ref,
    growth_ref,
    assignment_ref,
    left_velocity,
    left_edge,
    right_edge,
    lent_fields,
    out_ref,
    got_out,
    got_hidden,
    got_fields,
    weights,
    inputs,
    top,
    factors,
    residual,
    slope_even,
    slope_odd,
    partial,
    core_away,
    slope,
    gradient,
    got_gradient,
    core_sum,
    x_away,
    x_sum,
    z_away,
    z_sum,
    z_send,
    z_recv,
    x_send,
    x_recv,
    core_send,
    core_recv,
    sum_send,
    sum_recv,
    slope_send,
    slope_recv,
    role_send,
    role_recv,
    pair_send,
    pair_recv,
    edge_send,
    edge_recv,
    local_sem,
):
    layer_count, unit_rows, width = hidden_hbm.shape
    batch, cells = fields_hbm.shape
    rows = partial.shape[2]
    half = batch // 2
    narrow, wide = jnp.bfloat16, jnp.float32
    tiles = groups * 4
    last = layer_count - 1
    role = lax.axis_index("role")
    tile = lax.axis_index("tile")
    core = lax.rem(tile, 2)
    x = lax.rem(tile // 2, 2)
    z = tile // 4
    solver = role == 0
    trainer = role == 1

    def device(z_at, x_at, core_at):
        return (role, z_at * 4 + x_at * 2 + core_at)

    z_places = [lax.rem(z + k, groups) for k in range(1, groups)]
    z_peers = [device(place, x, core) for place in z_places]
    x_peer = device(z, 1 - x, core)
    core_peer = device(z, x, 1 - core)
    role_peer = (1 - role, tile)
    right_peer = (role, lax.rem(tile + 1, tiles))
    left_peer = (role, lax.rem(tile + tiles - 1, tiles))
    far_peer = (role, lax.rem(tile + tiles - 1 + 2 * core, tiles))

    def remote(views, sent, arrived, peer):
        def build():
            source, target = views()
            return pltpu.make_async_remote_copy(
                src_ref=source,
                dst_ref=target,
                send_sem=sent[0].at[sent[1]],
                recv_sem=arrived[0].at[arrived[1]],
                device_id=peer,
                device_id_type=pl.DeviceIdType.MESH,
            )

        return Later(build)

    def local(views, semaphores, slot):
        def build():
            source, target = views()
            return pltpu.make_async_copy(source, target, semaphores.at[slot])

        return Later(build)

    def twice(view):
        return lambda: (view(),) * 2

    def across(view, kind, slot):
        return remote(twice(view), (role_send, kind), (role_recv, slot), role_peer)

    chunks = [pl.ds(j * COLUMNS, COLUMNS) for j in range(cells // COLUMNS)]
    parts = [pl.ds(j * COLUMNS, COLUMNS) for j in range(width // COLUMNS)]
    pieces = [pl.ds(j * LANES, LANES) for j in range(width // LANES)]
    per_part = COLUMNS // LANES
    count = len(chunks)
    lent = count // 2
    lent_cells = pl.ds(lent * COLUMNS, (count - lent) * COLUMNS)
    momenta = [across(lambda c=c: got_out.at[:, c], 0, j) for j, c in enumerate(chunks)]
    hidden_momentum = across(lambda: got_hidden, 1, count)
    fresh = [
        across(lambda c=c: got_fields.at[:, c], 2, count + 1 + j) for j, c in enumerate(chunks)
    ]
    shares = [across(lambda i=i: weights.at[i, z, x, core], 0, i) for i in range(layer_count)]
    lent_out = across(lambda: out_ref.at[:, lent_cells], 1, layer_count)
    lent_target = remote(
        lambda: (own_fields.at[:, lent_cells], lent_fields),
        (role_send, 2),
        (role_recv, layer_count + 1),
        role_peer,
    )
    residuals = [
        across(lambda c=c: residual.at[:, :, :, :, c], 3, layer_count + 2 + j)
        for j, c in enumerate(chunks[:lent])
    ]
    slope_shares = [
        across(lambda c=c: slope.at[z, x, :, c], 4, layer_count + 2 + lent + j)
        for j, c in enumerate(pieces)
    ]

    pairs = [lambda: (hidden_hbm, own_hidden)]
    pairs += [lambda c=c: (out_hbm.at[:, c], own_out.at[:, c]) for c in chunks]
    pairs += [
        lambda: (fields_hbm, own_fields),
        lambda: (velocity_hbm, velocity_ref),
        lambda: (growth_hbm, growth_ref),
        lambda: (assignment_hbm, assignment_ref),
        lambda: (features_hbm, features_ref),
    ]
    loads = [local(views, local_sem, k) for k, views in enumerate(pairs)]
    for load in loads:
        load.start()
    hidden_load, out_loads, small_loads = loads[0], loads[1 : 1 + len(chunks)], loads[1 + len(chunks) :]
    barrier = pltpu.get_barrier_semaphore()
    peers = z_peers + [x_peer, core_peer, role_peer, far_peer]
    for peer in peers:
        pl.semaphore_signal(barrier, inc=1, device_id=peer, device_id_type=pl.DeviceIdType.MESH)
    pl.semaphore_wait(barrier, len(peers))

    last_lanes = pl.ds(cells - LANES, LANES)
    edge_list = [
        (lambda: (fields_hbm.at[:, last_lanes], left_edge), right_peer),
        (lambda: (velocity_hbm.at[:, last_lanes], left_velocity), right_peer),
        (lambda: (fields_hbm.at[:, pl.ds(0, LANES)], right_edge), left_peer),
    ]
    edges = [
        remote(views, (edge_send, k), (edge_recv, k), peer)
        for k, (views, peer) in enumerate(edge_list)
    ]

    nearest = [
        sorted((p for p in range(groups) if p != q), key=lambda p: (abs(p - q), p))
        for q in range(groups)
    ]

    def pick(k):
        place = jnp.int32(nearest[0][k])
        for q in range(1, groups):
            place = jnp.where(z == q, nearest[q][k], place)
        return place

    z_origins = [pick(k) for k in range(groups - 1)]
    inner = jnp.logical_and(z > 0, z < groups - 1)

    def share_of(i, place, x_at):
        return twice(lambda: weights.at[i, place, x_at, core])

    def hop(i, place, item, kind, target):
        rank = jnp.where(place > target, place - 1, place)
        x_at = 1 - x if item == layer_count else x
        return remote(
            share_of(i, place, x_at),
            (z_send, kind + 2 * (item // layer_count)),
            (z_recv, (item, rank)),
            device(target, x, core),
        )

    def spread(item):
        i = min(item, last)

        @pl.when(z < groups - 1)
        def _():
            hop(i, z, item, 0, lax.rem(z + 1, groups)).start()

        @pl.when(z > 0)
        def _():
            hop(i, z, item, jnp.where(z == groups - 1, 0, 1), lax.rem(z + groups - 1, groups)).start()

    def onward(k):
        rising = z_origins[k] < z
        return jnp.logical_or(
            jnp.logical_and(rising, z < groups - 1),
            jnp.logical_and(jnp.logical_not(rising), z > 0),
        )

    def relay(item, k):
        i = min(item, last)
        place = z_origins[k]
        hop(i, place, item, 1, z).wait_recv()

        @pl.when(onward(k))
        def _():
            target = jnp.where(place < z, lax.rem(z + 1, groups), lax.rem(z + groups - 1, groups))
            hop(i, place, item, 1, target).start()

        if i < last:
            send_x(i, place, k)
        send_core(i, place, 1 - x if item == layer_count else x)

    def x_slot(i, k):
        return [0, 1, 2 + i, 2 + last + i][k + 1] if i < last else 2 + 2 * last

    def send_x(i, place, k):
        remote(share_of(i, place, x), (x_send, i // last), (x_recv, x_slot(i, k)), x_peer).start()

    def send_core(i, place, x_at):
        remote(share_of(i, place, x_at), (core_send, 0), (core_recv, i), core_peer).start()

    def arrived_x(views, slot):
        remote(twice(views), (x_send, 0), (x_recv, slot), x_peer).wait_recv()

    def cross(i, k):
        place = z if k < 0 else z_origins[k]
        arrived_x(lambda: weights.at[i, place, 1 - x, core], x_slot(i, k))
        send_core(i, place, 1 - x)

    def cross_wave(k):
        place = z if k < 0 else z_origins[k]
        arrived_x(lambda: weights.at[pl.ds(0, last), place, 1 - x, core], k + 1)
        for i in range(last):
            send_core(i, place, 1 - x)

    def send_share(i):
        @pl.when(solver)
        def _():
            shares[i].wait_recv()

        spread(i)
        send_x(i, z, -1)
        send_core(i, z, x)

    share_order = [last] + list(range(last))

    def columns_of(j):
        return pl.ds(pl.multiple_of(j * COLUMNS, COLUMNS), COLUMNS)

    def advance():
        velocity = velocity_ref[...]
        forward_speed = jnp.maximum(velocity, 0.0)
        backward_speed = jnp.minimum(velocity, 0.0)
        growth = growth_ref[...]
        before = left_velocity[:, LANES - 1 :]
        step = LANES // 2

        @pl.loop(0, batch // step)
        def _(j):
            band = pl.ds(pl.multiple_of(j * step, step), step)
            current = own_fields[band, :]
            lane = lax.broadcasted_iota(jnp.int32, current.shape, 1)
            following = jnp.where(
                lane == cells - 1, right_edge[band, :1], pltpu.roll(current, cells - 1, 1)
            )
            outflow = forward_speed * current + backward_speed * following
            inflow_edge = (
                jnp.maximum(before, 0.0) * left_edge[band, :][:, LANES - 1 :]
                + jnp.minimum(before, 0.0) * current[:, :1]
            )
            inflow = jnp.where(lane == 0, inflow_edge, pltpu.roll(outflow, 1, 1))
            carried = current - outflow + inflow
            advanced = carried + growth * carried * (1.0 - carried)
            own_fields[band, :] = advanced
            got_fields[band, :] = advanced.astype(narrow)

    @pl.when(solver)
    def _():
        for copy in edges:
            copy.start()
        for load, c, copy in zip(out_loads, chunks, momenta):
            load.wait()
            got_out[:, c] = own_out[:, c].astype(narrow)
            copy.start()
        hidden_load.wait()
        got_hidden[...] = own_hidden[...].astype(narrow)
        hidden_momentum.start()

    @pl.when(trainer)
    def _():
        hidden_load.wait()
        for i in range(layer_count):
            weights[i, z, x, core] = own_hidden[i].astype(narrow)
        for i in share_order:
            shares[i].start()

    for i in share_order:
        send_share(i)

    for load in small_loads:
        load.wait()

    @pl.when(solver)
    def _():
        for copy in edges:
            copy.wait_recv()
        advance()
        for copy in fresh:
            copy.start()

    @pl.when(trainer)
    def _():
        lent_target.start()
        for j in reversed(range(count)):
            out_loads[j].wait()
            out_ref[:, chunks[j]] = own_out[:, chunks[j]].astype(narrow)
            if j == lent:
                lent_out.start()

    def beside(views, kind, slot):
        return remote(views, (pair_send, kind), (pair_recv, slot), core_peer)

    tops = [beside(twice(lambda c=c: top.at[:, :, core, :, c]), 0, 0) for c in parts]
    all_tops = beside(twice(lambda: top.at[:, :, core]), 0, 0)
    own_units = pl.ds(pl.multiple_of(core * unit_rows, unit_rows), unit_rows)
    other_units = pl.ds(pl.multiple_of((1 - core) * unit_rows, unit_rows), unit_rows)
    halves = [
        beside(lambda i=i: (gradient.at[i, other_units, :], got_gradient.at[i]), 1, 1 + i)
        for i in range(layer_count)
    ]
    all_halves = beside(lambda: (gradient.at[:, other_units, :], got_gradient), 1, 1)

    def forward_columns(i, columns):
        block = weights[i, :, :, :, :, columns].reshape(width, COLUMNS)
        activation = features_ref[:, :, core] if i == 0 else inputs[i - 1]
        summed = jnp.dot(activation.reshape(half, width), block, preferred_element_type=wide)
        logistic = jax.nn.sigmoid(summed)
        result = (summed * logistic).astype(narrow).reshape(groups, 2, rows, COLUMNS)
        factor = logistic * (1.0 + summed * (1.0 - logistic))
        factors[i, :, :, :, columns] = factor.reshape(groups, 2, rows, COLUMNS)
        return result

    def forward(i):
        for c in parts:
            if i == last:
                top[:, :, core, :, c] = forward_columns(i, c)
            else:
                inputs[i, :, :, :, c] = forward_columns(i, c)
        if i == last:
            for copy in tops:
                copy.start()

    def finish(i):
        remote(
            twice(lambda: weights.at[i, :, :, 1 - core]), (core_send, 0), (core_recv, i), core_peer
        ).wait_recv()
        forward(i)

    relay(last, 0)
    cross(last, -1)
    spread(layer_count)
    for i in range(last):
        relay(i, 0)
    relay(layer_count, 0)
    cross_wave(-1)
    for item in range(layer_count + 1):
        relay(item, 1)
    cross_wave(0)

    @pl.when(inner)
    def _():
        for item in range(layer_count + 1):
            relay(item, 2)

    for item in range(layer_count + 1):

        @pl.when(jnp.logical_not(inner))
        def _():
            relay(item, 2)

        if item < last:
            cross(item, 1)
        if 1 <= item <= last:
            cross(item - 1, 2)
        if item >= 2:
            finish(item - 2)
    finish(last)

    def update_out(j, decay, rate, other):
        c = chunks[j]

        for units in parts:
            grad = lax.dot_general(
                top[:, :, :, :, units].reshape(batch, COLUMNS),
                residual[:, :, :, :, c].reshape(batch, COLUMNS),
                (((0,), (0,)), ((), ())),
                preferred_element_type=wide,
            )
            if other is None:
                own_out[units, c] = decay * own_out[units, c] + grad
            else:
                fresh_momentum = decay * other[units, c].astype(wide) + grad
                own_out[units, c] = own_out[units, c] - rate * fresh_momentum

    def update_solver(j):
        residuals[j].wait_recv()
        update_out(j, momentum_decay, None, None)

    def update_trainer(j):
        momenta[j].wait_recv()
        update_out(j, momentum_decay, step_size, got_out)

    def summed(views, kind, slot, peer):
        return remote(views, (sum_send, kind), (sum_recv, slot), peer)

    core_sums = [
        summed(lambda c=c: (core_away.at[:, :, :, c], core_sum.at[:, :, :, c]), 0, j, core_peer)
        for j, c in enumerate(parts)
    ]
    x_sums = [
        summed(lambda c=c: (x_away.at[:, :, c], x_sum.at[:, :, c]), 1, len(parts) + j, x_peer)
        for j, c in enumerate(pieces)
    ]
    z_base = len(parts) + len(pieces)
    z_sums = [
        [
            summed(
                lambda c=c, k=k: (z_away.at[z_places[k], :, c], z_sum.at[k, :, c]),
                2,
                z_base + j,
                z_peers[k],
            )
            for k in range(groups - 1)
        ]
        for j, c in enumerate(pieces)
    ]
    others = pl.ds(0, groups - 1)
    all_sums = [
        summed(lambda: (core_away, core_sum), 0, 0, core_peer),
        summed(lambda: (x_away, x_sum), 1, 0, x_peer),
        summed(lambda: (z_away.at[others], z_sum), 2, 0, x_peer),
    ]
    targets = own_fields.reshape(groups, 2, 2, rows, cells)

    def residual_columns(side, c, wanted):
        rows_of = top[:, :, side].reshape(half, width)
        predicted = jnp.dot(rows_of, out_ref[:, c], preferred_element_type=wide)
        kept = ((predicted - wanted.reshape(half, COLUMNS)) / batch).astype(narrow)
        residual[:, :, side, :, c] = kept.reshape(groups, 2, rows, COLUMNS)

    def upstream_columns(side, c):
        return lax.dot_general(
            residual[:, :, side].reshape(half, cells),
            out_ref[c, :],
            (((1,), (1,)), ((), ())),
            preferred_element_type=wide,
        ).reshape(groups, 2, rows, COLUMNS)

    @pl.when(trainer)
    def _():
        for c in chunks:
            residual_columns(core, c, targets[:, :, core, :, c])
        all_tops.wait_recv()
        for c in chunks:
            residual_columns(1 - core, c, targets[:, :, 1 - core, :, c])
        for copy in residuals:
            copy.start()
        for c in parts:
            core_away[:, :, :, c] = upstream_columns(1 - core, c)
        for copy in core_sums:
            copy.start()
        for j, c in enumerate(parts):
            partial[:, :, :, c] = upstream_columns(core, c)
            core_sums[j].wait_recv()
            x_away[:, :, c] = (partial[:, 1 - x, :, c] + core_sum[:, 1 - x, :, c]).astype(narrow)
            for copy in x_sums[j * per_part : (j + 1) * per_part]:
                copy.start()
        update_trainer(0)
        for j, c in enumerate(pieces):
            near = partial[:, x, :, c] + core_sum[:, x, :, c]
            x_sums[j].wait_recv()
            near = near + x_sum[:, :, c].astype(wide)
            partial[:, x, :, c] = near
            z_away[:, :, c] = near.astype(narrow)
            for copy in z_sums[j]:
                copy.start()
        update_trainer(1)

    @pl.when(solver)
    def _():
        all_tops.wait_recv()
        lent_out.wait_recv()
        lent_target.wait_recv()
        lent_wanted = lent_fields.reshape(groups, 2, 2, rows, cells - lent * COLUMNS)
        for j in range(lent, count):
            for side in range(2):
                residual_columns(side, chunks[j], lent_wanted[:, :, side, :, chunks[j - lent]])
        for j in range(lent, count):
            update_out(j, momentum_decay, None, None)
        for j in range(lent):
            update_solver(j)

    def z_slope(c, slot, peer):
        return remote(
            twice(lambda: slope.at[z, x, :, c]), (slope_send, 0), (slope_recv, slot), peer
        )

    for j, c in enumerate(pieces):

        @pl.when(trainer)
        def _():
            summed(
                lambda: (z_away.at[others, :, c], z_sum.at[:, :, c]), 2, z_base + j, x_peer
            ).wait_recv()
            upstream = partial[z, x, :, c]
            for k in range(groups - 1):
                upstream = upstream + z_sum[k, :, c].astype(wide)
            slope[z, x, :, c] = (upstream * factors[last, z, x, :, c]).astype(narrow)
            slope_shares[j].start()

        @pl.when(solver)
        def _():
            slope_shares[j].wait_recv()

        for peer in z_peers:
            z_slope(c, j, peer).start()

    @pl.when(trainer)
    def _():
        update_trainer(2)

    def x_slope(view):
        return remote(twice(view), (slope_send, 1), (slope_recv, len(pieces)), x_peer)

    for j, c in enumerate(pieces):
        remote(
            twice(lambda: slope.at[others, x, :, c]), (slope_send, 0), (slope_recv, j), x_peer
        ).wait_recv()
        x_slope(lambda: slope.at[:, x, :, c]).start()

    @pl.when(trainer)
    def _():
        update_trainer(3)
        hidden_momentum.wait_recv()

    all_x_slopes = x_slope(lambda: slope.at[:, 1 - x])
    all_x_slopes.wait_recv()

    first_lane = pl.multiple_of((tile // 2) * LANES, LANES)

    def update_hidden(i):
        halves[i].wait_recv()
        total = gradient[i, own_units, :] + got_gradient[i]

        @pl.when(solver)
        def _():
            own_hidden[i] = momentum_decay * own_hidden[i] + total

        @pl.when(trainer)
        def _():
            fresh_momentum = momentum_decay * got_hidden[i].astype(wide) + total
            own_hidden[i] = own_hidden[i] - step_size * fresh_momentum

    slopes = [slope, slope_even, slope_odd]
    for step, i in enumerate(reversed(range(layer_count))):
        this_slope = slopes[0] if step == 0 else slopes[1 + step % 2]
        next_slope = slopes[1 + (step + 1) % 2]
        lanes = pl.ds(first_lane, LANES)
        own_inputs = features_ref[:, :, core, :, lanes] if i == 0 else inputs[i - 1, :, :, :, lanes]
        for c in parts:
            if i > 0:
                back = lax.dot_general(
                    this_slope[...].reshape(half, width),
                    weights.at[i].reshape(width, width)[c, :],
                    (((1,), (1,)), ((), ())),
                    preferred_element_type=wide,
                )
                factor = factors[i - 1, :, :, :, c].reshape(half, COLUMNS)
                next_slope[:, :, :, c] = (
                    (back * factor).astype(narrow).reshape(groups, 2, rows, COLUMNS)
                )
            gradient[i, :, c] = lax.dot_general(
                own_inputs.reshape(half, LANES),
                this_slope[:, :, :, c].reshape(half, COLUMNS),
                (((0,), (0,)), ((), ())),
                preferred_element_type=wide,
            )
        halves[i].start()
        if i < last:
            update_hidden(i + 1)

    @pl.when(trainer)
    def _():
        lent_target.wait_send()
        member = lax.broadcasted_iota(jnp.int32, (batch, batch), 0)
        chosen = jnp.where(member == assignment_ref[...], 1.0, 0.0).astype(narrow)
        for j, c in enumerate(chunks):
            fresh[j].wait_recv()
            own_fields[:, c] = lax.dot_general(
                chosen, got_fields[:, c], (((0,), (0,)), ((), ())), preferred_element_type=wide
            )

    update_hidden(0)

    def gone(view, semaphore, slot):
        remote(twice(view), (semaphore, slot), (x_recv, 0), x_peer).wait_send()

    gone(lambda: weights.at[:, :, :, core], core_send, 0)
    gone(lambda: weights.at[pl.ds(0, last), :, x, core], x_send, 0)
    gone(lambda: weights.at[last, z, x, core], x_send, 1)
    gone(lambda: weights.at[:, z, x, core], z_send, 0)
    gone(lambda: weights.at[last, z, x, core], z_send, 2)

    @pl.when(inner)
    def _():
        gone(lambda: weights.at[:, :, x, core], z_send, 1)
        gone(lambda: weights.at[last, :, x, core], z_send, 3)

    all_tops.wait_send()
    all_halves.wait_send()
    gone(lambda: slope.at[others, x], slope_send, 0)
    gone(lambda: slope.at[:, x], slope_send, 1)

    @pl.when(solver)
    def _():
        for copy in edges:
            copy.wait_send()
        gone(lambda: got_out, role_send, 0)
        gone(lambda: got_hidden, role_send, 1)
        gone(lambda: got_fields, role_send, 2)

    @pl.when(trainer)
    def _():
        for copy in all_sums:
            copy.wait_send()
        gone(lambda: weights.at[:, z, x, core], role_send, 0)
        gone(lambda: out_ref.at[:, lent_cells], role_send, 1)
        gone(lambda: residual.at[:, :, :, :, pl.ds(0, lent * COLUMNS)], role_send, 3)
        gone(lambda: slope.at[z, x], role_send, 4)


def fused_step(fields, velocity, growth, features, assignment, own_out, own_hidden):
    layer_count, unit_rows, width = own_hidden.shape
    batch, cells = fields.shape
    groups = lax.axis_size("tile") // 4
    rows = batch // lax.axis_size("tile")
    narrow, wide = jnp.bfloat16, jnp.float32
    dma = pltpu.SemaphoreType.DMA
    anywhere = pl.BlockSpec(memory_space=pltpu.HBM)
    parts, pieces = width // COLUMNS, cells // COLUMNS
    splits = width // LANES
    splits = width // LANES
    role_slots = layer_count + 3 * pieces + 1 + splits
    split = (groups, 2, 2, rows, width)
    return pl.pallas_call(
        functools.partial(train_kernel, groups),
        out_shape=(
            jax.ShapeDtypeStruct(fields.shape, wide),
            jax.ShapeDtypeStruct(own_out.shape, wide),
            jax.ShapeDtypeStruct(own_hidden.shape, wide),
        ),
        in_specs=[anywhere] * 7,
        out_specs=[pl.BlockSpec(memory_space=pltpu.VMEM)] * 3,
        scratch_shapes=[
            pltpu.VMEM(split, narrow),
            pltpu.VMEM((1, cells), wide),
            pltpu.VMEM((1, cells), wide),
            pltpu.VMEM((1, batch), jnp.int32),
            pltpu.VMEM((1, LANES), wide),
            pltpu.VMEM((batch, LANES), wide),
            pltpu.VMEM((batch, LANES), wide),
            pltpu.VMEM((batch, cells // 2), wide),
            pltpu.VMEM((width, cells), narrow),
            pltpu.VMEM((width, cells), narrow),
            pltpu.VMEM(own_hidden.shape, narrow),
            pltpu.VMEM((batch, cells), narrow),
            pltpu.VMEM((layer_count, groups, 2, 2, unit_rows, width), narrow),
            pltpu.VMEM((layer_count - 1, groups, 2, rows, width), narrow),
            pltpu.VMEM(split, narrow),
            pltpu.VMEM((layer_count, groups, 2, rows, width), wide),
            pltpu.VMEM((groups, 2, 2, rows, cells), narrow),
            pltpu.VMEM((groups, 2, rows, width), narrow),
            pltpu.VMEM((groups, 2, rows, width), narrow),
            pltpu.VMEM((groups, 2, rows, width), wide),
            pltpu.VMEM((groups, 2, rows, width), wide),
            pltpu.VMEM((groups, 2, rows, width), narrow),
            pltpu.VMEM((layer_count, LANES, width), wide),
            pltpu.VMEM(own_hidden.shape, wide),
            pltpu.VMEM((groups, 2, rows, width), wide),
            pltpu.VMEM((groups, rows, width), narrow),
            pltpu.VMEM((groups, rows, width), narrow),
            pltpu.VMEM((groups, rows, width), narrow),
            pltpu.VMEM((groups - 1, rows, width), narrow),
            dma((4,)),
            dma((layer_count + 1, groups - 1)),
            dma((2,)),
            dma((2 * layer_count + 1,)),
            dma((1,)),
            dma((layer_count,)),
            dma((3,)),
            dma((parts + 2 * splits,)),
            dma((2,)),
            dma((splits + 1,)),
            dma((5,)),
            dma((layer_count + 2 + pieces // 2 + splits,)),
            dma((2,)),
            dma((1 + layer_count,)),
            dma((3,)),
            dma((3,)),
            dma((6 + pieces,)),
        ],
        compiler_params=pltpu.CompilerParams(
            collective_id=0, has_side_effects=True, vmem_limit_bytes=46000000
        ),
        cost_estimate=pl.CostEstimate(
            flops=60 * batch * width * width, bytes_accessed=40 * batch * width, transcendentals=0
        ),
    )(
        *(
            pltpu.with_memory_space_constraint(value, pltpu.HBM)
            for value in (
                features.reshape(split),
                fields,
                velocity[None, :],
                growth[None, :],
                assignment[None, :],
                own_out,
                own_hidden,
            )
        )
    )


def plain_body(fields_pair, velocity, growth, features, assignment, out_pair, hidden_pair):
    solver_side = lax.axis_index("role") == 0
    own_fields = fields_pair[0]
    own_out = out_pair[0]
    own_hidden = hidden_pair[0]
    stacked = jnp.concatenate([own_fields, velocity[None, :]], axis=0)
    advanced = advance(extended(stacked, "tile", 1, 1), growth)
    grad_out, grad_hidden, other_out, other_hidden, fresh_fields = plain_training(
        features,
        own_hidden.astype(jnp.bfloat16),
        own_out.astype(jnp.bfloat16),
        own_fields,
        own_out,
        own_hidden,
        advanced.astype(jnp.bfloat16),
    )
    grad_out, grad_hidden, other_out, other_hidden = (
        v.astype(jnp.float32) for v in (grad_out, grad_hidden, other_out, other_hidden)
    )
    out_next = jnp.where(
        solver_side,
        momentum_decay * own_out + grad_out,
        own_out - step_size * (momentum_decay * other_out + grad_out),
    )
    hidden_next = jnp.where(
        solver_side,
        momentum_decay * own_hidden + other_hidden,
        own_hidden - step_size * (momentum_decay * other_hidden + grad_hidden),
    )
    next_batch = jnp.take(fresh_fields, assignment, axis=0).astype(jnp.float32)
    fields_next = jnp.where(solver_side, advanced, next_batch)
    return (fields_next[None], out_next[None], hidden_next[None])


def body(fields_pair, velocity, growth, features, assignment, out_pair, hidden_pair):
    tiles = lax.axis_size("tile")
    batch, cells = fields_pair.shape[1:]
    layer_count, unit_rows, width = hidden_pair.shape[1:]
    fits = (
        lax.axis_size("role") == 2
        and tiles == 16
        and layer_count > 2
        and batch % tiles == 0
        and (batch // tiles) % 16 == 0
        and LANES == 2 * unit_rows
        and width % COLUMNS == 0
        and cells % COLUMNS == 0
        and cells // COLUMNS == 4
    )
    if not fits:
        return plain_body(
            fields_pair, velocity, growth, features, assignment, out_pair, hidden_pair
        )
    results = fused_step(
        fields_pair[0], velocity, growth, features, assignment, out_pair[0], hidden_pair[0]
    )
    return tuple(result[None] for result in results)


def solution(mesh):
    return jax.shard_map(
        body,
        mesh=mesh,
        in_specs=(
            P("role", None, "tile"),
            P("tile"),
            P("tile"),
            P(),
            P(),
            P("role", None, "tile"),
            P("role", None, "tile", None),
        ),
        out_specs=(P("role", None, "tile"), P("role", None, "tile"), P("role", None, "tile", None)),
        check_vma=False,
    )
```

```python
import functools

import jax
import jax.numpy as jnp
from jax import lax
from jax.experimental import pallas as pl
from jax.experimental.pallas import tpu as pltpu
from jax.sharding import PartitionSpec as P

momentum_decay = 0.9
step_size = 0.1


def extended(value, axis, dim, width):
    count, length = (lax.axis_size(axis), value.shape[dim])
    up = [(i, (i + 1) % count) for i in range(count)]
    down = [(j, i) for i, j in up]
    last = lax.slice_in_dim(value, length - width, length, axis=dim)
    leading = lax.slice_in_dim(value, 0, width, axis=dim)
    before = lax.ppermute(last, axis, up)
    after = lax.ppermute(leading, axis, down)
    return jnp.concatenate([before, value, after], axis=dim)


def silu_slope(values):
    logistic = jax.nn.sigmoid(values)
    return logistic * (1.0 + values * (1.0 - logistic))


def advance(padded, growth):
    states = padded[:-1]
    velocity_row = padded[-1]
    outflow = (
        jnp.maximum(velocity_row[:-1], 0.0) * states[:, :-1]
        + jnp.minimum(velocity_row[:-1], 0.0) * states[:, 1:]
    )
    carried = states[:, 1:-1] - outflow[:, 1:] + outflow[:, :-1]
    return carried + growth * carried * (1.0 - carried)


def to_trainer(value):
    return lax.ppermute(value.astype(jnp.bfloat16), "role", [(0, 1)])


def to_solver(value):
    return lax.ppermute(value.astype(jnp.bfloat16), "role", [(1, 0)])


def plain_training(features, hidden_narrow, out_narrow, own_fields, own_out, own_hidden, fields):
    layer_count, unit_rows = own_hidden.shape[:2]
    batch = own_fields.shape[0]
    first_unit = lax.axis_index("tile") * unit_rows
    momentum_out = to_trainer(own_out)
    momentum_hidden = to_trainer(own_hidden)
    full_hidden = [
        lax.all_gather(hidden_narrow[i], "tile", axis=0, tiled=True) for i in range(layer_count)
    ]
    inputs, summed_list = [], []
    activation = features
    for i in range(layer_count):
        inputs.append(activation)
        summed = jnp.dot(activation, full_hidden[i], preferred_element_type=jnp.float32)
        summed_list.append(summed)
        activation = jax.nn.silu(summed).astype(jnp.bfloat16)
    predicted = jnp.dot(activation, out_narrow, preferred_element_type=jnp.float32)
    residual = ((predicted - own_fields) / batch).astype(jnp.bfloat16)
    partial_grad = lax.dot_general(
        residual, out_narrow, (((1,), (1,)), ((), ())), preferred_element_type=jnp.float32
    )
    upstream = lax.psum(partial_grad, "tile")
    grad_out = jnp.dot(activation.T, residual, preferred_element_type=jnp.float32)
    sent_out = to_solver(grad_out)
    gradients, sent = [], []
    for i in reversed(range(layer_count)):
        slope = (upstream * silu_slope(summed_list[i])).astype(jnp.bfloat16)
        own_inputs = lax.dynamic_slice_in_dim(inputs[i], first_unit, unit_rows, 1)
        gradient = jnp.dot(own_inputs.T, slope, preferred_element_type=jnp.float32)
        gradients.append(gradient)
        sent.append(to_solver(gradient))
        if i > 0:
            upstream = lax.dot_general(
                slope, full_hidden[i], (((1,), (1,)), ((), ())), preferred_element_type=jnp.float32
            )
    solver_side = lax.axis_index("role") == 0
    grad_out = jnp.where(solver_side, sent_out.astype(jnp.float32), grad_out)
    other_hidden = jnp.where(solver_side, jnp.stack(sent[::-1]), momentum_hidden)
    return grad_out, jnp.stack(gradients[::-1]), momentum_out, other_hidden, to_trainer(fields)


LANES = 128
COLUMNS = 256


LAG = 3


class Later:
    def __init__(self, build):
        self.build = build

    def start(self):
        self.build().start()

    def wait(self):
        self.build().wait()

    def wait_recv(self):
        self.build().wait_recv()

    def wait_send(self):
        self.build().wait_send()


def train_kernel(
    groups,
    features_hbm,
    fields_hbm,
    velocity_hbm,
    growth_hbm,
    assignment_hbm,
    out_hbm,
    hidden_hbm,
    own_fields,
    own_out,
    own_hidden,
    features_ref,
    velocity_ref,
    growth_ref,
    assignment_ref,
    left_velocity,
    left_edge,
    right_edge,
    lent_fields,
    out_ref,
    got_out,
    got_hidden,
    got_fields,
    weights,
    inputs,
    top,
    factors,
    residual,
    slope_even,
    slope_odd,
    partial,
    core_away,
    slope,
    gradient,
    got_gradient,
    core_sum,
    x_away,
    x_sum,
    z_away,
    z_sum,
    z_send,
    z_recv,
    x_send,
    x_recv,
    core_send,
    core_recv,
    sum_send,
    sum_recv,
    slope_send,
    slope_recv,
    role_send,
    role_recv,
    pair_send,
    pair_recv,
    edge_send,
    edge_recv,
    local_sem,
):
    layer_count, unit_rows, width = hidden_hbm.shape
    batch, cells = fields_hbm.shape
    rows = partial.shape[2]
    half = batch // 2
    narrow, wide = jnp.bfloat16, jnp.float32
    tiles = groups * 4
    last = layer_count - 1
    role = lax.axis_index("role")
    tile = lax.axis_index("tile")
    core = lax.rem(tile, 2)
    x = lax.rem(tile // 2, 2)
    z = tile // 4
    solver = role == 0
    trainer = role == 1

    def device(z_at, x_at, core_at):
        return (role, z_at * 4 + x_at * 2 + core_at)

    z_places = [lax.rem(z + k, groups) for k in range(1, groups)]
    z_peers = [device(place, x, core) for place in z_places]
    x_peer = device(z, 1 - x, core)
    core_peer = device(z, x, 1 - core)
    role_peer = (1 - role, tile)
    right_peer = (role, lax.rem(tile + 1, tiles))
    left_peer = (role, lax.rem(tile + tiles - 1, tiles))
    far_peer = (role, lax.rem(tile + tiles - 1 + 2 * core, tiles))

    def remote(views, sent, arrived, peer):
        def build():
            source, target = views()
            return pltpu.make_async_remote_copy(
                src_ref=source,
                dst_ref=target,
                send_sem=sent[0].at[sent[1]],
                recv_sem=arrived[0].at[arrived[1]],
                device_id=peer,
                device_id_type=pl.DeviceIdType.MESH,
            )

        return Later(build)

    def local(views, semaphores, slot):
        def build():
            source, target = views()
            return pltpu.make_async_copy(source, target, semaphores.at[slot])

        return Later(build)

    def twice(view):
        return lambda: (view(),) * 2

    def across(view, kind, slot):
        return remote(twice(view), (role_send, kind), (role_recv, slot), role_peer)

    chunks = [pl.ds(j * COLUMNS, COLUMNS) for j in range(cells // COLUMNS)]
    parts = [pl.ds(j * COLUMNS, COLUMNS) for j in range(width // COLUMNS)]
    pieces = [pl.ds(j * LANES, LANES) for j in range(width // LANES)]
    per_part = COLUMNS // LANES
    count = len(chunks)
    lent = count // 2
    lent_cells = pl.ds(lent * COLUMNS, (count - lent) * COLUMNS)
    momenta = [across(lambda c=c: got_out.at[:, c], 0, j) for j, c in enumerate(chunks)]
    hidden_momentum = across(lambda: got_hidden, 1, count)
    fresh = [
        across(lambda c=c: got_fields.at[:, c], 2, count + 1 + j) for j, c in enumerate(chunks)
    ]
    shares = [across(lambda i=i: weights.at[i, z, x, core], 0, i) for i in range(layer_count)]
    lent_out = across(lambda: out_ref.at[:, lent_cells], 1, layer_count)
    lent_target = remote(
        lambda: (own_fields.at[:, lent_cells], lent_fields),
        (role_send, 2),
        (role_recv, layer_count + 1),
        role_peer,
    )
    residuals = [
        across(lambda c=c: residual.at[:, :, :, :, c], 3, layer_count + 2 + j)
        for j, c in enumerate(chunks[:lent])
    ]
    slope_shares = [
        across(lambda c=c: slope.at[z, x, :, c], 4, layer_count + 2 + lent + j)
        for j, c in enumerate(pieces)
    ]

    pairs = [lambda: (hidden_hbm, own_hidden)]
    pairs += [lambda c=c: (out_hbm.at[:, c], own_out.at[:, c]) for c in chunks]
    pairs += [
        lambda: (fields_hbm, own_fields),
        lambda: (velocity_hbm, velocity_ref),
        lambda: (growth_hbm, growth_ref),
        lambda: (assignment_hbm, assignment_ref),
        lambda: (features_hbm, features_ref),
    ]
    loads = [local(views, local_sem, k) for k, views in enumerate(pairs)]
    for load in loads:
        load.start()
    hidden_load, out_loads, small_loads = loads[0], loads[1 : 1 + len(chunks)], loads[1 + len(chunks) :]
    barrier = pltpu.get_barrier_semaphore()
    peers = z_peers + [x_peer, core_peer, role_peer, far_peer]
    for peer in peers:
        pl.semaphore_signal(barrier, inc=1, device_id=peer, device_id_type=pl.DeviceIdType.MESH)
    pl.semaphore_wait(barrier, len(peers))

    last_lanes = pl.ds(cells - LANES, LANES)
    edge_list = [
        (lambda: (fields_hbm.at[:, last_lanes], left_edge), right_peer),
        (lambda: (velocity_hbm.at[:, last_lanes], left_velocity), right_peer),
        (lambda: (fields_hbm.at[:, pl.ds(0, LANES)], right_edge), left_peer),
    ]
    edges = [
        remote(views, (edge_send, k), (edge_recv, k), peer)
        for k, (views, peer) in enumerate(edge_list)
    ]

    nearest = [
        sorted((p for p in range(groups) if p != q), key=lambda p: (abs(p - q), p))
        for q in range(groups)
    ]

    def pick(k):
        place = jnp.int32(nearest[0][k])
        for q in range(1, groups):
            place = jnp.where(z == q, nearest[q][k], place)
        return place

    z_origins = [pick(k) for k in range(groups - 1)]
    inner = jnp.logical_and(z > 0, z < groups - 1)

    def share_of(i, place, x_at):
        return twice(lambda: weights.at[i, place, x_at, core])

    def hop(i, place, item, kind, target):
        rank = jnp.where(place > target, place - 1, place)
        x_at = 1 - x if item == layer_count else x
        return remote(
            share_of(i, place, x_at),
            (z_send, kind + 2 * (item // layer_count)),
            (z_recv, (item, rank)),
            device(target, x, core),
        )

    def spread(item):
        i = min(item, last)

        @pl.when(z < groups - 1)
        def _():
            hop(i, z, item, 0, lax.rem(z + 1, groups)).start()

        @pl.when(z > 0)
        def _():
            hop(i, z, item, jnp.where(z == groups - 1, 0, 1), lax.rem(z + groups - 1, groups)).start()

    def onward(k):
        rising = z_origins[k] < z
        return jnp.logical_or(
            jnp.logical_and(rising, z < groups - 1),
            jnp.logical_and(jnp.logical_not(rising), z > 0),
        )

    def relay(item, k):
        i = min(item, last)
        place = z_origins[k]
        hop(i, place, item, 1, z).wait_recv()

        @pl.when(onward(k))
        def _():
            target = jnp.where(place < z, lax.rem(z + 1, groups), lax.rem(z + groups - 1, groups))
            hop(i, place, item, 1, target).start()

        if i < last:
            send_x(i, place, k)
        send_core(i, place, 1 - x if item == layer_count else x)

    def x_slot(i, k):
        return [0, 1, 2 + i, 2 + last + i][k + 1] if i < last else 2 + 2 * last

    def send_x(i, place, k):
        remote(share_of(i, place, x), (x_send, i // last), (x_recv, x_slot(i, k)), x_peer).start()

    def send_core(i, place, x_at):
        remote(share_of(i, place, x_at), (core_send, 0), (core_recv, i), core_peer).start()

    def arrived_x(views, slot):
        remote(twice(views), (x_send, 0), (x_recv, slot), x_peer).wait_recv()

    def cross(i, k):
        place = z if k < 0 else z_origins[k]
        arrived_x(lambda: weights.at[i, place, 1 - x, core], x_slot(i, k))
        send_core(i, place, 1 - x)

    def cross_wave(k):
        place = z if k < 0 else z_origins[k]
        arrived_x(lambda: weights.at[pl.ds(0, last), place, 1 - x, core], k + 1)
        for i in range(last):
            send_core(i, place, 1 - x)

    def send_share(i):
        @pl.when(solver)
        def _():
            shares[i].wait_recv()

        if i < last:
            spread(i)
        send_x(i, z, -1)
        send_core(i, z, x)

    share_order = [last] + list(range(last))

    def columns_of(j):
        return pl.ds(pl.multiple_of(j * COLUMNS, COLUMNS), COLUMNS)

    def advance():
        velocity = velocity_ref[...]
        forward_speed = jnp.maximum(velocity, 0.0)
        backward_speed = jnp.minimum(velocity, 0.0)
        growth = growth_ref[...]
        before = left_velocity[:, LANES - 1 :]
        step = LANES // 2

        @pl.loop(0, batch // step)
        def _(j):
            band = pl.ds(pl.multiple_of(j * step, step), step)
            current = own_fields[band, :]
            lane = lax.broadcasted_iota(jnp.int32, current.shape, 1)
            following = jnp.where(
                lane == cells - 1, right_edge[band, :1], pltpu.roll(current, cells - 1, 1)
            )
            outflow = forward_speed * current + backward_speed * following
            inflow_edge = (
                jnp.maximum(before, 0.0) * left_edge[band, :][:, LANES - 1 :]
                + jnp.minimum(before, 0.0) * current[:, :1]
            )
            inflow = jnp.where(lane == 0, inflow_edge, pltpu.roll(outflow, 1, 1))
            carried = current - outflow + inflow
            advanced = carried + growth * carried * (1.0 - carried)
            own_fields[band, :] = advanced
            got_fields[band, :] = advanced.astype(narrow)

    @pl.when(solver)
    def _():
        for copy in edges:
            copy.start()
        for load, c, copy in zip(out_loads, chunks, momenta):
            load.wait()
            got_out[:, c] = own_out[:, c].astype(narrow)
            copy.start()
        hidden_load.wait()
        got_hidden[...] = own_hidden[...].astype(narrow)
        hidden_momentum.start()

    @pl.when(trainer)
    def _():
        hidden_load.wait()
        for i in range(layer_count):
            weights[i, z, x, core] = own_hidden[i].astype(narrow)
        for i in share_order:
            shares[i].start()

    for i in share_order:
        send_share(i)

    for load in small_loads:
        load.wait()

    @pl.when(solver)
    def _():
        for copy in edges:
            copy.wait_recv()
        advance()
        for copy in fresh:
            copy.start()

    @pl.when(trainer)
    def _():
        lent_target.start()
        for j in reversed(range(count)):
            out_loads[j].wait()
            out_ref[:, chunks[j]] = own_out[:, chunks[j]].astype(narrow)
            if j == lent:
                lent_out.start()

    def beside(views, kind, slot):
        return remote(views, (pair_send, kind), (pair_recv, slot), core_peer)

    tops = [beside(twice(lambda c=c: top.at[:, :, core, :, c]), 0, 0) for c in parts]
    all_tops = beside(twice(lambda: top.at[:, :, core]), 0, 0)
    own_units = pl.ds(pl.multiple_of(core * unit_rows, unit_rows), unit_rows)
    other_units = pl.ds(pl.multiple_of((1 - core) * unit_rows, unit_rows), unit_rows)
    halves = [
        beside(lambda i=i: (gradient.at[i, other_units, :], got_gradient.at[i]), 1, 1 + i)
        for i in range(layer_count)
    ]
    all_halves = beside(lambda: (gradient.at[:, other_units, :], got_gradient), 1, 1)

    def forward_columns(i, columns):
        block = weights[i, :, :, :, :, columns].reshape(width, COLUMNS)
        activation = features_ref[:, :, core] if i == 0 else inputs[i - 1]
        summed = jnp.dot(activation.reshape(half, width), block, preferred_element_type=wide)
        logistic = jax.nn.sigmoid(summed)
        result = (summed * logistic).astype(narrow).reshape(groups, 2, rows, COLUMNS)
        factor = logistic * (1.0 + summed * (1.0 - logistic))
        factors[i, :, :, :, columns] = factor.reshape(groups, 2, rows, COLUMNS)
        return result

    def forward(i):
        for c in parts:
            if i == last:
                top[:, :, core, :, c] = forward_columns(i, c)
            else:
                inputs[i, :, :, :, c] = forward_columns(i, c)
        if i == last:
            for copy in tops:
                copy.start()

    def finish(i):
        remote(
            twice(lambda: weights.at[i, :, :, 1 - core]), (core_send, 0), (core_recv, i), core_peer
        ).wait_recv()
        forward(i)

    outer = jnp.logical_not(inner)
    lagging = [last, layer_count]

    @pl.when(inner)
    def _():
        for item in range(last):
            relay(item, 0)
            relay(item, 1)

    @pl.when(outer)
    def _():
        for item in range(last):
            relay(item, 0)

    spread(last)
    cross(last, -1)
    cross_wave(-1)

    @pl.when(inner)
    def _():
        for item in range(last):
            relay(item, 2)

    @pl.when(outer)
    def _():
        for item in range(last):
            relay(item, 1)

    spread(layer_count)
    cross_wave(0)

    @pl.when(inner)
    def _():
        for k in range(2):
            for item in lagging:
                relay(item, k)

    for item in range(last):

        @pl.when(outer)
        def _():
            relay(item, 2)

        cross(item, 1)

    @pl.when(inner)
    def _():
        for item in lagging:
            relay(item, 2)

    held = [(item, k) for k in range(groups - 1) for item in lagging]
    for i in range(last):

        @pl.when(outer)
        def _():
            for item, k in [held[:2], held[2:3], held[3:4], held[4:5]][i]:
                relay(item, k)

        cross(i, 2)
        if i > 0:
            finish(i - 1)
    finish(last - 1)

    @pl.when(outer)
    def _():
        for item, k in held[5:]:
            relay(item, k)

    finish(last)

    def update_out(j, decay, rate, other):
        c = chunks[j]

        for units in parts:
            grad = lax.dot_general(
                top[:, :, :, :, units].reshape(batch, COLUMNS),
                residual[:, :, :, :, c].reshape(batch, COLUMNS),
                (((0,), (0,)), ((), ())),
                preferred_element_type=wide,
            )
            if other is None:
                own_out[units, c] = decay * own_out[units, c] + grad
            else:
                fresh_momentum = decay * other[units, c].astype(wide) + grad
                own_out[units, c] = own_out[units, c] - rate * fresh_momentum

    def update_solver(j):
        residuals[j].wait_recv()
        update_out(j, momentum_decay, None, None)

    def update_trainer(j):
        momenta[j].wait_recv()
        update_out(j, momentum_decay, step_size, got_out)

    def summed(views, kind, slot, peer):
        return remote(views, (sum_send, kind), (sum_recv, slot), peer)

    core_sums = [
        summed(lambda c=c: (core_away.at[:, :, :, c], core_sum.at[:, :, :, c]), 0, j, core_peer)
        for j, c in enumerate(parts)
    ]
    x_sums = [
        summed(lambda c=c: (x_away.at[:, :, c], x_sum.at[:, :, c]), 1, len(parts) + j, x_peer)
        for j, c in enumerate(pieces)
    ]
    z_base = len(parts) + len(pieces)
    z_sums = [
        [
            summed(
                lambda c=c, k=k: (z_away.at[z_places[k], :, c], z_sum.at[k, :, c]),
                2,
                z_base + j,
                z_peers[k],
            )
            for k in range(groups - 1)
        ]
        for j, c in enumerate(pieces)
    ]
    others = pl.ds(0, groups - 1)
    all_sums = [
        summed(lambda: (core_away, core_sum), 0, 0, core_peer),
        summed(lambda: (x_away, x_sum), 1, 0, x_peer),
        summed(lambda: (z_away.at[others], z_sum), 2, 0, x_peer),
    ]
    targets = own_fields.reshape(groups, 2, 2, rows, cells)

    def residual_columns(side, c, wanted):
        rows_of = top[:, :, side].reshape(half, width)
        predicted = jnp.dot(rows_of, out_ref[:, c], preferred_element_type=wide)
        kept = ((predicted - wanted.reshape(half, COLUMNS)) / batch).astype(narrow)
        residual[:, :, side, :, c] = kept.reshape(groups, 2, rows, COLUMNS)

    def upstream_columns(side, c):
        return lax.dot_general(
            residual[:, :, side].reshape(half, cells),
            out_ref[c, :],
            (((1,), (1,)), ((), ())),
            preferred_element_type=wide,
        ).reshape(groups, 2, rows, COLUMNS)

    @pl.when(trainer)
    def _():
        for c in chunks:
            residual_columns(core, c, targets[:, :, core, :, c])
        early = len(parts) // 2
        for c in parts[:early]:
            partial[:, :, :, c] = upstream_columns(core, c)
        all_tops.wait_recv()
        for c in chunks:
            residual_columns(1 - core, c, targets[:, :, 1 - core, :, c])
        residuals[0].start()
        for c in parts:
            core_away[:, :, :, c] = upstream_columns(1 - core, c)
        for copy in core_sums:
            copy.start()
        for c in parts[early:]:
            partial[:, :, :, c] = upstream_columns(core, c)
        for j, c in enumerate(parts):
            core_sums[j].wait_recv()
            x_away[:, :, c] = (partial[:, 1 - x, :, c] + core_sum[:, 1 - x, :, c]).astype(narrow)
            for copy in x_sums[j * per_part : (j + 1) * per_part]:
                copy.start()
        update_trainer(0)

    @pl.when(solver)
    def _():
        all_tops.wait_recv()
        lent_out.wait_recv()
        lent_target.wait_recv()
        lent_wanted = lent_fields.reshape(groups, 2, 2, rows, cells - lent * COLUMNS)
        for j in range(lent, count):
            for side in range(2):
                residual_columns(side, chunks[j], lent_wanted[:, :, side, :, chunks[j - lent]])
        for j in range(lent, count):
            update_out(j, momentum_decay, None, None)

    def z_slope(c, slot, peer):
        return remote(
            twice(lambda: slope.at[z, x, :, c]), (slope_send, 0), (slope_recv, slot), peer
        )

    def x_slope(view):
        return remote(twice(view), (slope_send, 1), (slope_recv, len(pieces)), x_peer)

    def add_far(j, c):
        near = partial[:, x, :, c] + core_sum[:, x, :, c]
        x_sums[j].wait_recv()
        near = near + x_sum[:, :, c].astype(wide)
        partial[:, x, :, c] = near
        z_away[:, :, c] = near.astype(narrow)
        for copy in z_sums[j]:
            copy.start()

    def make_slope(j, c):
        summed(
            lambda: (z_away.at[others, :, c], z_sum.at[:, :, c]), 2, z_base + j, x_peer
        ).wait_recv()
        upstream = partial[z, x, :, c]
        for k in range(groups - 1):
            upstream = upstream + z_sum[k, :, c].astype(wide)
        slope[z, x, :, c] = (upstream * factors[last, z, x, :, c]).astype(narrow)
        slope_shares[j].start()

    def pass_slope(j, c):
        remote(
            twice(lambda: slope.at[others, x, :, c]), (slope_send, 0), (slope_recv, j), x_peer
        ).wait_recv()
        x_slope(lambda: slope.at[:, x, :, c]).start()

    for turn in range(len(pieces) + 2 * LAG):
        made, passed = turn - LAG, turn - 2 * LAG

        @pl.when(trainer)
        def _():
            if turn < len(pieces):
                add_far(turn, pieces[turn])
            if turn == len(pieces) // 2:
                update_trainer(1)
            if 0 <= made < len(pieces):
                make_slope(made, pieces[made])
            if made == len(pieces) - 1:
                for copy in residuals[1:]:
                    copy.start()
                update_trainer(2)

        if 0 <= made < len(pieces):

            @pl.when(solver)
            def _():
                slope_shares[made].wait_recv()

            for peer in z_peers:
                z_slope(pieces[made], made, peer).start()
        if passed >= 0:
            pass_slope(passed, pieces[passed])

    @pl.when(solver)
    def _():
        update_solver(0)

    @pl.when(trainer)
    def _():
        update_trainer(3)
        hidden_momentum.wait_recv()

    all_x_slopes = x_slope(lambda: slope.at[:, 1 - x])
    all_x_slopes.wait_recv()

    first_lane = pl.multiple_of((tile // 2) * LANES, LANES)

    def update_hidden(i):
        halves[i].wait_recv()
        total = gradient[i, own_units, :] + got_gradient[i]

        @pl.when(solver)
        def _():
            own_hidden[i] = momentum_decay * own_hidden[i] + total

        @pl.when(trainer)
        def _():
            fresh_momentum = momentum_decay * got_hidden[i].astype(wide) + total
            own_hidden[i] = own_hidden[i] - step_size * fresh_momentum

    slopes = [slope, slope_even, slope_odd]
    for step, i in enumerate(reversed(range(layer_count))):
        this_slope = slopes[0] if step == 0 else slopes[1 + step % 2]
        next_slope = slopes[1 + (step + 1) % 2]
        lanes = pl.ds(first_lane, LANES)
        own_inputs = features_ref[:, :, core, :, lanes] if i == 0 else inputs[i - 1, :, :, :, lanes]
        for c in parts:
            if i > 0:
                back = lax.dot_general(
                    this_slope[...].reshape(half, width),
                    weights.at[i].reshape(width, width)[c, :],
                    (((1,), (1,)), ((), ())),
                    preferred_element_type=wide,
                )
                factor = factors[i - 1, :, :, :, c].reshape(half, COLUMNS)
                next_slope[:, :, :, c] = (
                    (back * factor).astype(narrow).reshape(groups, 2, rows, COLUMNS)
                )
            gradient[i, :, c] = lax.dot_general(
                own_inputs.reshape(half, LANES),
                this_slope[:, :, :, c].reshape(half, COLUMNS),
                (((0,), (0,)), ((), ())),
                preferred_element_type=wide,
            )
        halves[i].start()
        if i < last - 1:
            update_hidden(i + 2)

    @pl.when(solver)
    def _():
        for j in range(1, lent):
            update_solver(j)

    @pl.when(trainer)
    def _():
        lent_target.wait_send()
        member = lax.broadcasted_iota(jnp.int32, (batch, batch), 0)
        chosen = jnp.where(member == assignment_ref[...], 1.0, 0.0).astype(narrow)
        for j, c in enumerate(chunks):
            fresh[j].wait_recv()
            own_fields[:, c] = lax.dot_general(
                chosen, got_fields[:, c], (((0,), (0,)), ((), ())), preferred_element_type=wide
            )

    update_hidden(1)
    update_hidden(0)

    def gone(view, semaphore, slot):
        remote(twice(view), (semaphore, slot), (x_recv, 0), x_peer).wait_send()

    gone(lambda: weights.at[:, :, :, core], core_send, 0)
    gone(lambda: weights.at[pl.ds(0, last), :, x, core], x_send, 0)
    gone(lambda: weights.at[last, z, x, core], x_send, 1)
    gone(lambda: weights.at[:, z, x, core], z_send, 0)
    gone(lambda: weights.at[last, z, x, core], z_send, 2)

    @pl.when(inner)
    def _():
        gone(lambda: weights.at[:, :, x, core], z_send, 1)
        gone(lambda: weights.at[last, :, x, core], z_send, 3)

    all_tops.wait_send()
    all_halves.wait_send()
    gone(lambda: slope.at[others, x], slope_send, 0)
    gone(lambda: slope.at[:, x], slope_send, 1)

    @pl.when(solver)
    def _():
        for copy in edges:
            copy.wait_send()
        gone(lambda: got_out, role_send, 0)
        gone(lambda: got_hidden, role_send, 1)
        gone(lambda: got_fields, role_send, 2)

    @pl.when(trainer)
    def _():
        for copy in all_sums:
            copy.wait_send()
        gone(lambda: weights.at[:, z, x, core], role_send, 0)
        gone(lambda: out_ref.at[:, lent_cells], role_send, 1)
        gone(lambda: residual.at[:, :, :, :, pl.ds(0, lent * COLUMNS)], role_send, 3)
        gone(lambda: slope.at[z, x], role_send, 4)


def store_kernel(*refs):
    semaphores = refs[-1]
    copies = [
        pltpu.make_async_copy(source, target, semaphores.at[k])
        for k, (source, target) in enumerate(zip(refs[:3], refs[3:6]))
    ]
    for copy in copies:
        copy.start()
    for copy in copies:
        copy.wait()


def fused_step(fields, velocity, growth, features, assignment, own_out, own_hidden):
    layer_count, unit_rows, width = own_hidden.shape
    batch, cells = fields.shape
    groups = lax.axis_size("tile") // 4
    rows = batch // lax.axis_size("tile")
    narrow, wide = jnp.bfloat16, jnp.float32
    dma = pltpu.SemaphoreType.DMA
    anywhere = pl.BlockSpec(memory_space=pl.ANY)
    parts, pieces = width // COLUMNS, cells // COLUMNS
    splits = width // LANES
    splits = width // LANES
    role_slots = layer_count + 3 * pieces + 1 + splits
    split = (groups, 2, 2, rows, width)
    results = pl.pallas_call(
        functools.partial(train_kernel, groups),
        out_shape=(
            jax.ShapeDtypeStruct(fields.shape, wide),
            jax.ShapeDtypeStruct(own_out.shape, wide),
            jax.ShapeDtypeStruct(own_hidden.shape, wide),
        ),
        in_specs=[anywhere] * 7,
        out_specs=[pl.BlockSpec(memory_space=pltpu.VMEM)] * 3,
        scratch_shapes=[
            pltpu.VMEM(split, narrow),
            pltpu.VMEM((1, cells), wide),
            pltpu.VMEM((1, cells), wide),
            pltpu.VMEM((1, batch), jnp.int32),
            pltpu.VMEM((1, LANES), wide),
            pltpu.VMEM((batch, LANES), wide),
            pltpu.VMEM((batch, LANES), wide),
            pltpu.VMEM((batch, cells // 2), wide),
            pltpu.VMEM((width, cells), narrow),
            pltpu.VMEM((width, cells), narrow),
            pltpu.VMEM(own_hidden.shape, narrow),
            pltpu.VMEM((batch, cells), narrow),
            pltpu.VMEM((layer_count, groups, 2, 2, unit_rows, width), narrow),
            pltpu.VMEM((layer_count - 1, groups, 2, rows, width), narrow),
            pltpu.VMEM(split, narrow),
            pltpu.VMEM((layer_count, groups, 2, rows, width), wide),
            pltpu.VMEM((groups, 2, 2, rows, cells), narrow),
            pltpu.VMEM((groups, 2, rows, width), narrow),
            pltpu.VMEM((groups, 2, rows, width), narrow),
            pltpu.VMEM((groups, 2, rows, width), wide),
            pltpu.VMEM((groups, 2, rows, width), wide),
            pltpu.VMEM((groups, 2, rows, width), narrow),
            pltpu.VMEM((layer_count, LANES, width), wide),
            pltpu.VMEM(own_hidden.shape, wide),
            pltpu.VMEM((groups, 2, rows, width), wide),
            pltpu.VMEM((groups, rows, width), narrow),
            pltpu.VMEM((groups, rows, width), narrow),
            pltpu.VMEM((groups, rows, width), narrow),
            pltpu.VMEM((groups - 1, rows, width), narrow),
            dma((4,)),
            dma((layer_count + 1, groups - 1)),
            dma((2,)),
            dma((2 * layer_count + 1,)),
            dma((1,)),
            dma((layer_count,)),
            dma((3,)),
            dma((parts + 2 * splits,)),
            dma((2,)),
            dma((splits + 1,)),
            dma((5,)),
            dma((layer_count + 2 + pieces // 2 + splits,)),
            dma((2,)),
            dma((1 + layer_count,)),
            dma((3,)),
            dma((3,)),
            dma((6 + pieces,)),
        ],
        compiler_params=pltpu.CompilerParams(
            collective_id=0, has_side_effects=True, vmem_limit_bytes=46000000
        ),
        cost_estimate=pl.CostEstimate(
            flops=60 * batch * width * width, bytes_accessed=40 * batch * width, transcendentals=0
        ),
    )(
        *(
            pltpu.with_memory_space_constraint(value, pltpu.HBM)
            for value in (
                features.reshape(split),
                fields,
                velocity[None, :],
                growth[None, :],
                assignment[None, :],
                own_out,
                own_hidden,
            )
        )
    )
    return pl.pallas_call(
        store_kernel,
        out_shape=tuple(jax.ShapeDtypeStruct(v.shape, v.dtype) for v in results),
        in_specs=[anywhere] * 3,
        out_specs=[anywhere] * 3,
        scratch_shapes=[dma((3,))],
        compiler_params=pltpu.CompilerParams(vmem_limit_bytes=1 << 20),
    )(*results)


def plain_body(fields_pair, velocity, growth, features, assignment, out_pair, hidden_pair):
    solver_side = lax.axis_index("role") == 0
    own_fields = fields_pair[0]
    own_out = out_pair[0]
    own_hidden = hidden_pair[0]
    stacked = jnp.concatenate([own_fields, velocity[None, :]], axis=0)
    advanced = advance(extended(stacked, "tile", 1, 1), growth)
    grad_out, grad_hidden, other_out, other_hidden, fresh_fields = plain_training(
        features,
        own_hidden.astype(jnp.bfloat16),
        own_out.astype(jnp.bfloat16),
        own_fields,
        own_out,
        own_hidden,
        advanced.astype(jnp.bfloat16),
    )
    grad_out, grad_hidden, other_out, other_hidden = (
        v.astype(jnp.float32) for v in (grad_out, grad_hidden, other_out, other_hidden)
    )
    out_next = jnp.where(
        solver_side,
        momentum_decay * own_out + grad_out,
        own_out - step_size * (momentum_decay * other_out + grad_out),
    )
    hidden_next = jnp.where(
        solver_side,
        momentum_decay * own_hidden + other_hidden,
        own_hidden - step_size * (momentum_decay * other_hidden + grad_hidden),
    )
    next_batch = jnp.take(fresh_fields, assignment, axis=0).astype(jnp.float32)
    fields_next = jnp.where(solver_side, advanced, next_batch)
    return (fields_next[None], out_next[None], hidden_next[None])


def body(fields_pair, velocity, growth, features, assignment, out_pair, hidden_pair):
    tiles = lax.axis_size("tile")
    batch, cells = fields_pair.shape[1:]
    layer_count, unit_rows, width = hidden_pair.shape[1:]
    fits = (
        lax.axis_size("role") == 2
        and tiles == 16
        and layer_count == 5
        and batch % tiles == 0
        and (batch // tiles) % 16 == 0
        and LANES == 2 * unit_rows
        and width % COLUMNS == 0
        and cells % COLUMNS == 0
        and cells // COLUMNS == 4
    )
    if not fits:
        return plain_body(
            fields_pair, velocity, growth, features, assignment, out_pair, hidden_pair
        )
    results = fused_step(
        fields_pair[0], velocity, growth, features, assignment, out_pair[0], hidden_pair[0]
    )
    return tuple(result[None] for result in results)


def solution(mesh):
    return jax.shard_map(
        body,
        mesh=mesh,
        in_specs=(
            P("role", None, "tile"),
            P("tile"),
            P("tile"),
            P(),
            P(),
            P("role", None, "tile"),
            P("role", None, "tile", None),
        ),
        out_specs=(P("role", None, "tile"), P("role", None, "tile"), P("role", None, "tile", None)),
        check_vma=False,
    )
```

```python
import functools

import jax
import jax.numpy as jnp
from jax import lax
from jax.experimental import pallas as pl
from jax.experimental.pallas import tpu as pltpu
from jax.sharding import PartitionSpec as P

momentum_decay = 0.9
step_size = 0.1


def extended(value, axis, dim, width):
    count, length = (lax.axis_size(axis), value.shape[dim])
    up = [(i, (i + 1) % count) for i in range(count)]
    down = [(j, i) for i, j in up]
    last = lax.slice_in_dim(value, length - width, length, axis=dim)
    leading = lax.slice_in_dim(value, 0, width, axis=dim)
    before = lax.ppermute(last, axis, up)
    after = lax.ppermute(leading, axis, down)
    return jnp.concatenate([before, value, after], axis=dim)


def silu_slope(values):
    logistic = jax.nn.sigmoid(values)
    return logistic * (1.0 + values * (1.0 - logistic))


def advance(padded, growth):
    states = padded[:-1]
    velocity_row = padded[-1]
    outflow = (
        jnp.maximum(velocity_row[:-1], 0.0) * states[:, :-1]
        + jnp.minimum(velocity_row[:-1], 0.0) * states[:, 1:]
    )
    carried = states[:, 1:-1] - outflow[:, 1:] + outflow[:, :-1]
    return carried + growth * carried * (1.0 - carried)


def to_trainer(value):
    return lax.ppermute(value.astype(jnp.bfloat16), "role", [(0, 1)])


def to_solver(value):
    return lax.ppermute(value.astype(jnp.bfloat16), "role", [(1, 0)])


def plain_training(features, hidden_narrow, out_narrow, own_fields, own_out, own_hidden, fields):
    layer_count, unit_rows = own_hidden.shape[:2]
    batch = own_fields.shape[0]
    first_unit = lax.axis_index("tile") * unit_rows
    momentum_out = to_trainer(own_out)
    momentum_hidden = to_trainer(own_hidden)
    full_hidden = [
        lax.all_gather(hidden_narrow[i], "tile", axis=0, tiled=True) for i in range(layer_count)
    ]
    inputs, summed_list = [], []
    activation = features
    for i in range(layer_count):
        inputs.append(activation)
        summed = jnp.dot(activation, full_hidden[i], preferred_element_type=jnp.float32)
        summed_list.append(summed)
        activation = jax.nn.silu(summed).astype(jnp.bfloat16)
    predicted = jnp.dot(activation, out_narrow, preferred_element_type=jnp.float32)
    residual = ((predicted - own_fields) / batch).astype(jnp.bfloat16)
    partial_grad = lax.dot_general(
        residual, out_narrow, (((1,), (1,)), ((), ())), preferred_element_type=jnp.float32
    )
    upstream = lax.psum(partial_grad, "tile")
    grad_out = jnp.dot(activation.T, residual, preferred_element_type=jnp.float32)
    sent_out = to_solver(grad_out)
    gradients, sent = [], []
    for i in reversed(range(layer_count)):
        slope = (upstream * silu_slope(summed_list[i])).astype(jnp.bfloat16)
        own_inputs = lax.dynamic_slice_in_dim(inputs[i], first_unit, unit_rows, 1)
        gradient = jnp.dot(own_inputs.T, slope, preferred_element_type=jnp.float32)
        gradients.append(gradient)
        sent.append(to_solver(gradient))
        if i > 0:
            upstream = lax.dot_general(
                slope, full_hidden[i], (((1,), (1,)), ((), ())), preferred_element_type=jnp.float32
            )
    solver_side = lax.axis_index("role") == 0
    grad_out = jnp.where(solver_side, sent_out.astype(jnp.float32), grad_out)
    other_hidden = jnp.where(solver_side, jnp.stack(sent[::-1]), momentum_hidden)
    return grad_out, jnp.stack(gradients[::-1]), momentum_out, other_hidden, to_trainer(fields)


LANES = 128
COLUMNS = 256


SUM_LAG = 7
PASS_LAG = 7


class Later:
    def __init__(self, build):
        self.build = build

    def start(self):
        self.build().start()

    def wait(self):
        self.build().wait()

    def wait_recv(self):
        self.build().wait_recv()

    def wait_send(self):
        self.build().wait_send()


def train_kernel(
    groups,
    features_hbm,
    fields_hbm,
    velocity_hbm,
    growth_hbm,
    assignment_hbm,
    out_hbm,
    hidden_hbm,
    own_fields,
    own_out,
    own_hidden,
    features_ref,
    velocity_ref,
    growth_ref,
    assignment_ref,
    left_velocity,
    left_edge,
    right_edge,
    lent_fields,
    chosen_ref,
    out_ref,
    got_out,
    got_hidden,
    got_fields,
    weights,
    inputs,
    top,
    factors,
    residual,
    slope_even,
    slope_odd,
    partial,
    core_away,
    slope,
    gradient,
    got_gradient,
    core_sum,
    x_away,
    x_sum,
    z_away,
    z_sum,
    z_send,
    z_recv,
    x_send,
    x_recv,
    core_send,
    core_recv,
    sum_send,
    sum_recv,
    slope_send,
    slope_recv,
    role_send,
    role_recv,
    pair_send,
    pair_recv,
    edge_send,
    edge_recv,
    local_sem,
):
    layer_count, unit_rows, width = hidden_hbm.shape
    batch, cells = fields_hbm.shape
    rows = partial.shape[2]
    half = batch // 2
    narrow, wide = jnp.bfloat16, jnp.float32
    tiles = groups * 4
    last = layer_count - 1
    role = lax.axis_index("role")
    tile = lax.axis_index("tile")
    core = lax.rem(tile, 2)
    x = lax.rem(tile // 2, 2)
    z = tile // 4
    solver = role == 0
    trainer = role == 1

    def device(z_at, x_at, core_at):
        return (role, z_at * 4 + x_at * 2 + core_at)

    z_places = [lax.rem(z + k, groups) for k in range(1, groups)]
    z_peers = [device(place, x, core) for place in z_places]
    x_peer = device(z, 1 - x, core)
    core_peer = device(z, x, 1 - core)
    role_peer = (1 - role, tile)
    right_peer = (role, lax.rem(tile + 1, tiles))
    left_peer = (role, lax.rem(tile + tiles - 1, tiles))
    far_peer = (role, lax.rem(tile + tiles - 1 + 2 * core, tiles))

    def remote(views, sent, arrived, peer):
        def build():
            source, target = views()
            return pltpu.make_async_remote_copy(
                src_ref=source,
                dst_ref=target,
                send_sem=sent[0].at[sent[1]],
                recv_sem=arrived[0].at[arrived[1]],
                device_id=peer,
                device_id_type=pl.DeviceIdType.MESH,
            )

        return Later(build)

    def local(views, semaphores, slot):
        def build():
            source, target = views()
            return pltpu.make_async_copy(source, target, semaphores.at[slot])

        return Later(build)

    def twice(view):
        return lambda: (view(),) * 2

    def across(view, kind, slot):
        return remote(twice(view), (role_send, kind), (role_recv, slot), role_peer)

    chunks = [pl.ds(j * COLUMNS, COLUMNS) for j in range(cells // COLUMNS)]
    parts = [pl.ds(j * COLUMNS, COLUMNS) for j in range(width // COLUMNS)]
    pieces = [pl.ds(j * LANES, LANES) for j in range(width // LANES)]
    per_part = COLUMNS // LANES
    count = len(chunks)
    lent = count // 2
    lent_cells = pl.ds(lent * COLUMNS, (count - lent) * COLUMNS)
    momenta = [across(lambda c=c: got_out.at[:, c], 0, j) for j, c in enumerate(chunks)]
    hidden_momentum = across(lambda: got_hidden, 1, count)
    fresh = [
        across(lambda c=c: got_fields.at[:, c], 2, count + 1 + j) for j, c in enumerate(chunks)
    ]
    shares = [across(lambda i=i: weights.at[i, z, x, core], 0, i) for i in range(layer_count)]
    lent_out = across(lambda: out_ref.at[:, lent_cells], 1, layer_count)
    lent_target = remote(
        lambda: (own_fields.at[:, lent_cells], lent_fields),
        (role_send, 2),
        (role_recv, layer_count + 1),
        role_peer,
    )
    residuals = [
        across(lambda c=c: residual.at[:, :, :, :, c], 3, layer_count + 2 + j)
        for j, c in enumerate(chunks[:lent])
    ]
    slope_shares = [
        across(lambda c=c: slope.at[z, x, :, c], 4, layer_count + 2 + lent + j)
        for j, c in enumerate(pieces)
    ]

    pairs = [lambda: (hidden_hbm, own_hidden)]
    pairs += [lambda c=c: (out_hbm.at[:, c], own_out.at[:, c]) for c in chunks]
    pairs += [
        lambda: (fields_hbm, own_fields),
        lambda: (velocity_hbm, velocity_ref),
        lambda: (growth_hbm, growth_ref),
        lambda: (assignment_hbm, assignment_ref),
        lambda: (features_hbm, features_ref),
    ]
    loads = [local(views, local_sem, k) for k, views in enumerate(pairs)]
    for load in loads:
        load.start()
    hidden_load, out_loads, small_loads = loads[0], loads[1 : 1 + len(chunks)], loads[1 + len(chunks) :]
    share_order = [last] + list(range(last))
    barrier = pltpu.get_barrier_semaphore()
    peers = z_peers + [x_peer, core_peer, role_peer, far_peer]
    for peer in peers:
        pl.semaphore_signal(barrier, inc=1, device_id=peer, device_id_type=pl.DeviceIdType.MESH)

    @pl.when(solver)
    def _():
        out_loads[0].wait()
        got_out[:, chunks[0]] = own_out[:, chunks[0]].astype(narrow)

    @pl.when(trainer)
    def _():
        hidden_load.wait()
        for i in share_order:
            weights[i, z, x, core] = own_hidden[i].astype(narrow)

    pl.semaphore_wait(barrier, len(peers))

    last_lanes = pl.ds(cells - LANES, LANES)
    edge_list = [
        (lambda: (fields_hbm.at[:, last_lanes], left_edge), right_peer),
        (lambda: (velocity_hbm.at[:, last_lanes], left_velocity), right_peer),
        (lambda: (fields_hbm.at[:, pl.ds(0, LANES)], right_edge), left_peer),
    ]
    edges = [
        remote(views, (edge_send, k), (edge_recv, k), peer)
        for k, (views, peer) in enumerate(edge_list)
    ]

    nearest = [
        sorted((p for p in range(groups) if p != q), key=lambda p: (abs(p - q), p))
        for q in range(groups)
    ]

    def pick(k):
        place = jnp.int32(nearest[0][k])
        for q in range(1, groups):
            place = jnp.where(z == q, nearest[q][k], place)
        return place

    z_origins = [pick(k) for k in range(groups - 1)]
    inner = jnp.logical_and(z > 0, z < groups - 1)

    def share_of(i, place, x_at):
        return twice(lambda: weights.at[i, place, x_at, core])

    def hop(i, place, item, kind, target):
        rank = jnp.where(place > target, place - 1, place)
        x_at = 1 - x if item == layer_count else x
        return remote(
            share_of(i, place, x_at),
            (z_send, kind + 2 * (item // layer_count)),
            (z_recv, (item, rank)),
            device(target, x, core),
        )

    def spread(item):
        i = min(item, last)

        @pl.when(z < groups - 1)
        def _():
            hop(i, z, item, 0, lax.rem(z + 1, groups)).start()

        @pl.when(z > 0)
        def _():
            hop(i, z, item, jnp.where(z == groups - 1, 0, 1), lax.rem(z + groups - 1, groups)).start()

    def onward(k):
        rising = z_origins[k] < z
        return jnp.logical_or(
            jnp.logical_and(rising, z < groups - 1),
            jnp.logical_and(jnp.logical_not(rising), z > 0),
        )

    def relay(item, k):
        i = min(item, last)
        place = z_origins[k]
        hop(i, place, item, 1, z).wait_recv()

        @pl.when(onward(k))
        def _():
            target = jnp.where(place < z, lax.rem(z + 1, groups), lax.rem(z + groups - 1, groups))
            hop(i, place, item, 1, target).start()

        if i < last:
            send_x(i, place, k)
        send_core(i, place, 1 - x if item == layer_count else x)

    def x_slot(i, k):
        return [0, 1, 2 + i, 2 + last + i][k + 1] if i < last else 2 + 2 * last

    def send_x(i, place, k):
        remote(share_of(i, place, x), (x_send, i // last), (x_recv, x_slot(i, k)), x_peer).start()

    def send_core(i, place, x_at):
        remote(share_of(i, place, x_at), (core_send, 0), (core_recv, i), core_peer).start()

    def arrived_x(views, slot):
        remote(twice(views), (x_send, 0), (x_recv, slot), x_peer).wait_recv()

    def cross(i, k):
        place = z if k < 0 else z_origins[k]
        arrived_x(lambda: weights.at[i, place, 1 - x, core], x_slot(i, k))
        send_core(i, place, 1 - x)

    def cross_wave(k):
        place = z if k < 0 else z_origins[k]
        arrived_x(lambda: weights.at[pl.ds(0, last), place, 1 - x, core], k + 1)
        for i in range(last):
            send_core(i, place, 1 - x)

    def send_share(i):
        @pl.when(solver)
        def _():
            shares[i].wait_recv()

        if i < last:
            spread(i)
        send_x(i, z, -1)
        send_core(i, z, x)


    def columns_of(j):
        return pl.ds(pl.multiple_of(j * COLUMNS, COLUMNS), COLUMNS)

    def advance():
        velocity = velocity_ref[...]
        forward_speed = jnp.maximum(velocity, 0.0)
        backward_speed = jnp.minimum(velocity, 0.0)
        growth = growth_ref[...]
        before = left_velocity[:, LANES - 1 :]
        step = LANES // 2

        @pl.loop(0, batch // step)
        def _(j):
            band = pl.ds(pl.multiple_of(j * step, step), step)
            current = own_fields[band, :]
            lane = lax.broadcasted_iota(jnp.int32, current.shape, 1)
            following = jnp.where(
                lane == cells - 1, right_edge[band, :1], pltpu.roll(current, cells - 1, 1)
            )
            outflow = forward_speed * current + backward_speed * following
            inflow_edge = (
                jnp.maximum(before, 0.0) * left_edge[band, :][:, LANES - 1 :]
                + jnp.minimum(before, 0.0) * current[:, :1]
            )
            inflow = jnp.where(lane == 0, inflow_edge, pltpu.roll(outflow, 1, 1))
            carried = current - outflow + inflow
            advanced = carried + growth * carried * (1.0 - carried)
            own_fields[band, :] = advanced
            got_fields[band, :] = advanced.astype(narrow)

    @pl.when(solver)
    def _():
        momenta[0].start()
        for copy in edges:
            copy.start()
        for j in range(1, count):
            out_loads[j].wait()
            got_out[:, chunks[j]] = own_out[:, chunks[j]].astype(narrow)
            if j < lent:
                momenta[j].start()
            if j == lent - 1:
                hidden_load.wait()
                got_hidden[...] = own_hidden[...].astype(narrow)
                hidden_momentum.start()

    @pl.when(trainer)
    def _():
        for i in share_order:
            shares[i].start()

    for i in share_order:
        send_share(i)

    for load in small_loads:
        load.wait()

    @pl.when(solver)
    def _():
        for copy in edges:
            copy.wait_recv()
        advance()
        for copy in fresh + momenta[lent:]:
            copy.start()

    @pl.when(trainer)
    def _():
        lent_target.start()
        for j in reversed(range(count)):
            out_loads[j].wait()
            out_ref[:, chunks[j]] = own_out[:, chunks[j]].astype(narrow)
            if j == lent:
                lent_out.start()
        member = lax.broadcasted_iota(jnp.int32, (batch, batch), 0)
        chosen = jnp.where(member == assignment_ref[...], 1.0, 0.0)
        chosen_ref[...] = chosen.T.astype(narrow)

    def beside(views, kind, slot):
        return remote(views, (pair_send, kind), (pair_recv, slot), core_peer)

    tops = [beside(twice(lambda c=c: top.at[:, :, core, :, c]), 0, 0) for c in parts]
    all_tops = beside(twice(lambda: top.at[:, :, core]), 0, 0)
    own_units = pl.ds(pl.multiple_of(core * unit_rows, unit_rows), unit_rows)
    other_units = pl.ds(pl.multiple_of((1 - core) * unit_rows, unit_rows), unit_rows)
    halves = [
        beside(lambda i=i: (gradient.at[i, other_units, :], got_gradient.at[i]), 1, 1 + i)
        for i in range(layer_count)
    ]
    all_halves = beside(lambda: (gradient.at[:, other_units, :], got_gradient), 1, 1)

    def forward_columns(i, columns):
        block = weights[i, :, :, :, :, columns].reshape(width, COLUMNS)
        activation = features_ref[:, :, core] if i == 0 else inputs[i - 1]
        summed = jnp.dot(activation.reshape(half, width), block, preferred_element_type=wide)
        logistic = jax.nn.sigmoid(summed)
        result = (summed * logistic).astype(narrow).reshape(groups, 2, rows, COLUMNS)
        factor = logistic * (1.0 + summed * (1.0 - logistic))
        factors[i, :, :, :, columns] = factor.reshape(groups, 2, rows, COLUMNS)
        return result

    def forward(i):
        for j, c in enumerate(parts):
            if i < last:
                inputs[i, :, :, :, c] = forward_columns(i, c)
                continue
            top[:, :, core, :, c] = forward_columns(i, c)
            if j % 2:
                tops[j - 1].start()
                tops[j].start()

    def finish(i):
        remote(
            twice(lambda: weights.at[i, :, :, 1 - core]), (core_send, 0), (core_recv, i), core_peer
        ).wait_recv()
        forward(i)

    outer = jnp.logical_not(inner)
    lagging = [last, layer_count]

    @pl.when(inner)
    def _():
        for item in range(last):
            relay(item, 0)
            relay(item, 1)

    @pl.when(outer)
    def _():
        for item in range(last):
            relay(item, 0)

    spread(last)
    cross(last, -1)
    cross_wave(-1)

    @pl.when(inner)
    def _():
        for item in range(last):
            relay(item, 2)

    @pl.when(outer)
    def _():
        for item in range(last):
            relay(item, 1)

    spread(layer_count)
    cross_wave(0)

    @pl.when(inner)
    def _():
        for k in range(2):
            for item in lagging:
                relay(item, k)

    for item in range(last):

        @pl.when(outer)
        def _():
            relay(item, 2)

        cross(item, 1)

    @pl.when(inner)
    def _():
        for item in lagging:
            relay(item, 2)

    held = [(item, k) for k in range(groups - 1) for item in lagging]
    for i in range(last):

        @pl.when(outer)
        def _():
            for item, k in [held[:2], held[2:3], held[3:4], held[4:5]][i]:
                relay(item, k)

        cross(i, 2)
        if i > 0:
            finish(i - 1)
    finish(last - 1)

    @pl.when(outer)
    def _():
        for item, k in held[5:]:
            relay(item, k)

    finish(last)

    def update_out(j, decay, rate, other):
        c = chunks[j]

        for units in parts:
            grad = lax.dot_general(
                top[:, :, :, :, units].reshape(batch, COLUMNS),
                residual[:, :, :, :, c].reshape(batch, COLUMNS),
                (((0,), (0,)), ((), ())),
                preferred_element_type=wide,
            )
            if rate is None:
                own_out[units, c] = decay * own_out[units, c] + grad
            elif other is None:
                own_out[units, c] = own_out[units, c] - rate * grad
            else:
                fresh_momentum = decay * other[units, c].astype(wide) + grad
                own_out[units, c] = own_out[units, c] - rate * fresh_momentum

    def update_solver(j):
        residuals[j].wait_recv()
        update_out(j, momentum_decay, None, None)

    def update_trainer(j):
        if j < lent:
            momenta[j].wait_recv()
        update_out(j, momentum_decay, step_size, got_out if j < lent else None)

    def add_momentum(j):
        momenta[j].wait_recv()
        for units in parts:
            late = momentum_decay * got_out[units, chunks[j]].astype(wide)
            own_out[units, chunks[j]] = own_out[units, chunks[j]] - step_size * late

    def gather(j):
        fresh[j].wait_recv()
        own_fields[:, chunks[j]] = jnp.dot(
            chosen_ref[...], got_fields[:, chunks[j]], preferred_element_type=wide
        )

    def summed(views, kind, slot, peer):
        return remote(views, (sum_send, kind), (sum_recv, slot), peer)

    core_sums = [
        summed(lambda c=c: (core_away.at[:, :, :, c], core_sum.at[:, :, :, c]), 0, j, core_peer)
        for j, c in enumerate(parts)
    ]
    x_sums = [
        summed(lambda c=c: (x_away.at[:, :, c], x_sum.at[:, :, c]), 1, len(parts) + j, x_peer)
        for j, c in enumerate(pieces)
    ]
    z_base = len(parts) + len(pieces)
    z_sums = [
        [
            summed(
                lambda c=c, k=k: (z_away.at[z_places[k], :, c], z_sum.at[k, :, c]),
                2,
                z_base + j,
                z_peers[k],
            )
            for k in range(groups - 1)
        ]
        for j, c in enumerate(pieces)
    ]
    others = pl.ds(0, groups - 1)
    all_sums = [
        summed(lambda: (core_away, core_sum), 0, 0, core_peer),
        summed(lambda: (x_away, x_sum), 1, 0, x_peer),
        summed(lambda: (z_away.at[others], z_sum), 2, 0, x_peer),
    ]
    targets = own_fields.reshape(groups, 2, 2, rows, cells)

    def residual_columns(side, c, wanted):
        rows_of = top[:, :, side].reshape(half, width)
        predicted = jnp.dot(rows_of, out_ref[:, c], preferred_element_type=wide)
        kept = ((predicted - wanted.reshape(half, COLUMNS)) / batch).astype(narrow)
        residual[:, :, side, :, c] = kept.reshape(groups, 2, rows, COLUMNS)

    def upstream_columns(side, c):
        return lax.dot_general(
            residual[:, :, side].reshape(half, cells),
            out_ref[c, :],
            (((1,), (1,)), ((), ())),
            preferred_element_type=wide,
        ).reshape(groups, 2, rows, COLUMNS)

    @pl.when(trainer)
    def _():
        for c in chunks:
            residual_columns(core, c, targets[:, :, core, :, c])
        early = len(parts) // 2
        for c in parts[:early]:
            partial[:, :, :, c] = upstream_columns(core, c)
        all_tops.wait_recv()
        for c in chunks:
            residual_columns(1 - core, c, targets[:, :, 1 - core, :, c])
        residuals[0].start()
        for c in parts:
            core_away[:, :, :, c] = upstream_columns(1 - core, c)
        for copy in core_sums:
            copy.start()
        for c in parts[early:]:
            partial[:, :, :, c] = upstream_columns(core, c)
        for j, c in enumerate(parts):
            core_sums[j].wait_recv()
            x_away[:, :, c] = (partial[:, 1 - x, :, c] + core_sum[:, 1 - x, :, c]).astype(narrow)
            for copy in x_sums[j * per_part : (j + 1) * per_part]:
                copy.start()
        update_trainer(0)
        lent_target.wait_send()
        for j in range(lent):
            gather(j)

    @pl.when(solver)
    def _():
        all_tops.wait_recv()
        lent_out.wait_recv()
        lent_target.wait_recv()
        lent_wanted = lent_fields.reshape(groups, 2, 2, rows, cells - lent * COLUMNS)
        for j in range(lent, count):
            for side in range(2):
                residual_columns(side, chunks[j], lent_wanted[:, :, side, :, chunks[j - lent]])
        for j in range(lent, count):
            update_out(j, momentum_decay, None, None)
        update_solver(0)

    def z_slope(c, slot, peer):
        return remote(
            twice(lambda: slope.at[z, x, :, c]), (slope_send, 0), (slope_recv, slot), peer
        )

    def x_slope(view):
        return remote(twice(view), (slope_send, 1), (slope_recv, len(pieces)), x_peer)

    def add_far(j, c):
        near = partial[:, x, :, c] + core_sum[:, x, :, c]
        x_sums[j].wait_recv()
        near = near + x_sum[:, :, c].astype(wide)
        partial[:, x, :, c] = near
        z_away[:, :, c] = near.astype(narrow)
        for copy in z_sums[j]:
            copy.start()

    def make_slope(j, c):
        summed(
            lambda: (z_away.at[others, :, c], z_sum.at[:, :, c]), 2, z_base + j, x_peer
        ).wait_recv()
        upstream = partial[z, x, :, c]
        for k in range(groups - 1):
            upstream = upstream + z_sum[k, :, c].astype(wide)
        slope[z, x, :, c] = (upstream * factors[last, z, x, :, c]).astype(narrow)
        slope_shares[j].start()

    def pass_slope(j, c):
        remote(
            twice(lambda: slope.at[others, x, :, c]), (slope_send, 0), (slope_recv, j), x_peer
        ).wait_recv()
        x_slope(lambda: slope.at[:, x, :, c]).start()

    for turn in range(len(pieces) + SUM_LAG + PASS_LAG):
        made, passed = turn - SUM_LAG, turn - SUM_LAG - PASS_LAG

        @pl.when(trainer)
        def _():
            if turn < len(pieces):
                add_far(turn, pieces[turn])
            if turn == len(pieces) // 2:
                update_trainer(1)
            if 0 <= made < len(pieces):
                make_slope(made, pieces[made])
            if made == len(pieces) - 1:
                for copy in residuals[1:]:
                    copy.start()
                for j in range(lent, count):
                    gather(j)

        if 0 <= made < len(pieces):

            @pl.when(solver)
            def _():
                slope_shares[made].wait_recv()

            for peer in z_peers:
                z_slope(pieces[made], made, peer).start()
        if passed >= 0:
            pass_slope(passed, pieces[passed])

    @pl.when(trainer)
    def _():
        for j in range(lent, count):
            update_trainer(j)
        hidden_momentum.wait_recv()

    @pl.when(solver)
    def _():
        for j in range(1, lent):
            update_solver(j)

    all_x_slopes = x_slope(lambda: slope.at[:, 1 - x])
    all_x_slopes.wait_recv()

    first_lane = pl.multiple_of((tile // 2) * LANES, LANES)

    def update_hidden(i):
        halves[i].wait_recv()
        total = gradient[i, own_units, :] + got_gradient[i]

        @pl.when(solver)
        def _():
            own_hidden[i] = momentum_decay * own_hidden[i] + total

        @pl.when(trainer)
        def _():
            fresh_momentum = momentum_decay * got_hidden[i].astype(wide) + total
            own_hidden[i] = own_hidden[i] - step_size * fresh_momentum

    slopes = [slope, slope_even, slope_odd]
    for step, i in enumerate(reversed(range(layer_count))):
        this_slope = slopes[0] if step == 0 else slopes[1 + step % 2]
        next_slope = slopes[1 + (step + 1) % 2]
        lanes = pl.ds(first_lane, LANES)
        own_inputs = features_ref[:, :, core, :, lanes] if i == 0 else inputs[i - 1, :, :, :, lanes]
        for c in parts:
            if i > 0:
                back = lax.dot_general(
                    this_slope[...].reshape(half, width),
                    weights.at[i].reshape(width, width)[c, :],
                    (((1,), (1,)), ((), ())),
                    preferred_element_type=wide,
                )
                factor = factors[i - 1, :, :, :, c].reshape(half, COLUMNS)
                next_slope[:, :, :, c] = (
                    (back * factor).astype(narrow).reshape(groups, 2, rows, COLUMNS)
                )
            gradient[i, :, c] = lax.dot_general(
                own_inputs.reshape(half, LANES),
                this_slope[:, :, :, c].reshape(half, COLUMNS),
                (((0,), (0,)), ((), ())),
                preferred_element_type=wide,
            )
        halves[i].start()
        if i < last - 1:
            update_hidden(i + 2)

    @pl.when(trainer)
    def _():
        for j in range(lent, count):
            add_momentum(j)

    update_hidden(1)
    update_hidden(0)

    def gone(view, semaphore, slot):
        remote(twice(view), (semaphore, slot), (x_recv, 0), x_peer).wait_send()

    gone(lambda: weights.at[:, :, :, core], core_send, 0)
    gone(lambda: weights.at[pl.ds(0, last), :, x, core], x_send, 0)
    gone(lambda: weights.at[last, z, x, core], x_send, 1)
    gone(lambda: weights.at[:, z, x, core], z_send, 0)
    gone(lambda: weights.at[last, z, x, core], z_send, 2)

    @pl.when(inner)
    def _():
        gone(lambda: weights.at[:, :, x, core], z_send, 1)
        gone(lambda: weights.at[last, :, x, core], z_send, 3)

    all_tops.wait_send()
    all_halves.wait_send()
    gone(lambda: slope.at[others, x], slope_send, 0)
    gone(lambda: slope.at[:, x], slope_send, 1)

    @pl.when(solver)
    def _():
        for copy in edges:
            copy.wait_send()
        gone(lambda: got_out, role_send, 0)
        gone(lambda: got_hidden, role_send, 1)
        gone(lambda: got_fields, role_send, 2)

    @pl.when(trainer)
    def _():
        for copy in all_sums:
            copy.wait_send()
        gone(lambda: weights.at[:, z, x, core], role_send, 0)
        gone(lambda: out_ref.at[:, lent_cells], role_send, 1)
        gone(lambda: residual.at[:, :, :, :, pl.ds(0, lent * COLUMNS)], role_send, 3)
        gone(lambda: slope.at[z, x], role_send, 4)


def store_kernel(*refs):
    semaphores = refs[-1]
    copies = []
    for source, target in zip(refs[:3], refs[3:6]):
        length = source.shape[0]
        step = length if length % 4 else length // 4
        for at in range(0, length, step):
            band = pl.ds(at, step)
            copies.append(
                pltpu.make_async_copy(
                    source.at[band], target.at[band], semaphores.at[len(copies)]
                )
            )
    for copy in copies:
        copy.start()
    for copy in copies:
        copy.wait()


def fused_step(fields, velocity, growth, features, assignment, own_out, own_hidden):
    layer_count, unit_rows, width = own_hidden.shape
    batch, cells = fields.shape
    groups = lax.axis_size("tile") // 4
    rows = batch // lax.axis_size("tile")
    narrow, wide = jnp.bfloat16, jnp.float32
    dma = pltpu.SemaphoreType.DMA
    anywhere = pl.BlockSpec(memory_space=pl.ANY)
    parts, pieces = width // COLUMNS, cells // COLUMNS
    splits = width // LANES
    splits = width // LANES
    role_slots = layer_count + 3 * pieces + 1 + splits
    split = (groups, 2, 2, rows, width)
    results = pl.pallas_call(
        functools.partial(train_kernel, groups),
        out_shape=(
            jax.ShapeDtypeStruct(fields.shape, wide),
            jax.ShapeDtypeStruct(own_out.shape, wide),
            jax.ShapeDtypeStruct(own_hidden.shape, wide),
        ),
        in_specs=[anywhere] * 7,
        out_specs=[pl.BlockSpec(memory_space=pltpu.VMEM)] * 3,
        scratch_shapes=[
            pltpu.VMEM(split, narrow),
            pltpu.VMEM((1, cells), wide),
            pltpu.VMEM((1, cells), wide),
            pltpu.VMEM((1, batch), jnp.int32),
            pltpu.VMEM((1, LANES), wide),
            pltpu.VMEM((batch, LANES), wide),
            pltpu.VMEM((batch, LANES), wide),
            pltpu.VMEM((batch, cells // 2), wide),
            pltpu.VMEM((batch, batch), narrow),
            pltpu.VMEM((width, cells), narrow),
            pltpu.VMEM((width, cells), narrow),
            pltpu.VMEM(own_hidden.shape, narrow),
            pltpu.VMEM((batch, cells), narrow),
            pltpu.VMEM((layer_count, groups, 2, 2, unit_rows, width), narrow),
            pltpu.VMEM((layer_count - 1, groups, 2, rows, width), narrow),
            pltpu.VMEM(split, narrow),
            pltpu.VMEM((layer_count, groups, 2, rows, width), wide),
            pltpu.VMEM((groups, 2, 2, rows, cells), narrow),
            pltpu.VMEM((groups, 2, rows, width), narrow),
            pltpu.VMEM((groups, 2, rows, width), narrow),
            pltpu.VMEM((groups, 2, rows, width), wide),
            pltpu.VMEM((groups, 2, rows, width), wide),
            pltpu.VMEM((groups, 2, rows, width), narrow),
            pltpu.VMEM((layer_count, LANES, width), wide),
            pltpu.VMEM(own_hidden.shape, wide),
            pltpu.VMEM((groups, 2, rows, width), wide),
            pltpu.VMEM((groups, rows, width), narrow),
            pltpu.VMEM((groups, rows, width), narrow),
            pltpu.VMEM((groups, rows, width), narrow),
            pltpu.VMEM((groups - 1, rows, width), narrow),
            dma((4,)),
            dma((layer_count + 1, groups - 1)),
            dma((2,)),
            dma((2 * layer_count + 1,)),
            dma((1,)),
            dma((layer_count,)),
            dma((3,)),
            dma((parts + 2 * splits,)),
            dma((2,)),
            dma((splits + 1,)),
            dma((5,)),
            dma((layer_count + 2 + pieces // 2 + splits,)),
            dma((2,)),
            dma((1 + layer_count,)),
            dma((3,)),
            dma((3,)),
            dma((6 + pieces,)),
        ],
        compiler_params=pltpu.CompilerParams(
            collective_id=0, has_side_effects=True, vmem_limit_bytes=46000000
        ),
        cost_estimate=pl.CostEstimate(
            flops=60 * batch * width * width, bytes_accessed=40 * batch * width, transcendentals=0
        ),
    )(
        *(
            pltpu.with_memory_space_constraint(value, pltpu.HBM)
            for value in (
                features.reshape(split),
                fields,
                velocity[None, :],
                growth[None, :],
                assignment[None, :],
                own_out,
                own_hidden,
            )
        )
    )
    return pl.pallas_call(
        store_kernel,
        out_shape=tuple(jax.ShapeDtypeStruct(v.shape, v.dtype) for v in results),
        in_specs=[anywhere] * 3,
        out_specs=[anywhere] * 3,
        scratch_shapes=[dma((12,))],
        compiler_params=pltpu.CompilerParams(vmem_limit_bytes=1 << 20),
    )(*results)


def plain_body(fields_pair, velocity, growth, features, assignment, out_pair, hidden_pair):
    solver_side = lax.axis_index("role") == 0
    own_fields = fields_pair[0]
    own_out = out_pair[0]
    own_hidden = hidden_pair[0]
    stacked = jnp.concatenate([own_fields, velocity[None, :]], axis=0)
    advanced = advance(extended(stacked, "tile", 1, 1), growth)
    grad_out, grad_hidden, other_out, other_hidden, fresh_fields = plain_training(
        features,
        own_hidden.astype(jnp.bfloat16),
        own_out.astype(jnp.bfloat16),
        own_fields,
        own_out,
        own_hidden,
        advanced.astype(jnp.bfloat16),
    )
    grad_out, grad_hidden, other_out, other_hidden = (
        v.astype(jnp.float32) for v in (grad_out, grad_hidden, other_out, other_hidden)
    )
    out_next = jnp.where(
        solver_side,
        momentum_decay * own_out + grad_out,
        own_out - step_size * (momentum_decay * other_out + grad_out),
    )
    hidden_next = jnp.where(
        solver_side,
        momentum_decay * own_hidden + other_hidden,
        own_hidden - step_size * (momentum_decay * other_hidden + grad_hidden),
    )
    next_batch = jnp.take(fresh_fields, assignment, axis=0).astype(jnp.float32)
    fields_next = jnp.where(solver_side, advanced, next_batch)
    return (fields_next[None], out_next[None], hidden_next[None])


def body(fields_pair, velocity, growth, features, assignment, out_pair, hidden_pair):
    tiles = lax.axis_size("tile")
    batch, cells = fields_pair.shape[1:]
    layer_count, unit_rows, width = hidden_pair.shape[1:]
    fits = (
        lax.axis_size("role") == 2
        and tiles == 16
        and layer_count == 5
        and batch % tiles == 0
        and (batch // tiles) % 16 == 0
        and LANES == 2 * unit_rows
        and width % COLUMNS == 0
        and cells % COLUMNS == 0
        and cells // COLUMNS == 4
    )
    if not fits:
        return plain_body(
            fields_pair, velocity, growth, features, assignment, out_pair, hidden_pair
        )
    results = fused_step(
        fields_pair[0], velocity, growth, features, assignment, out_pair[0], hidden_pair[0]
    )
    return tuple(result[None] for result in results)


def solution(mesh):
    return jax.shard_map(
        body,
        mesh=mesh,
        in_specs=(
            P("role", None, "tile"),
            P("tile"),
            P("tile"),
            P(),
            P(),
            P("role", None, "tile"),
            P("role", None, "tile", None),
        ),
        out_specs=(P("role", None, "tile"), P("role", None, "tile"), P("role", None, "tile", None)),
        check_vma=False,
    )
```

```python
import functools

import jax
import jax.numpy as jnp
from jax import lax
from jax.experimental import pallas as pl
from jax.experimental.pallas import tpu as pltpu
from jax.sharding import PartitionSpec as P

momentum_decay = 0.9
step_size = 0.1


def extended(value, axis, dim, width):
    count, length = (lax.axis_size(axis), value.shape[dim])
    up = [(i, (i + 1) % count) for i in range(count)]
    down = [(j, i) for i, j in up]
    last = lax.slice_in_dim(value, length - width, length, axis=dim)
    leading = lax.slice_in_dim(value, 0, width, axis=dim)
    before = lax.ppermute(last, axis, up)
    after = lax.ppermute(leading, axis, down)
    return jnp.concatenate([before, value, after], axis=dim)


def silu_slope(values):
    logistic = jax.nn.sigmoid(values)
    return logistic * (1.0 + values * (1.0 - logistic))


def advance(padded, growth):
    states = padded[:-1]
    velocity_row = padded[-1]
    outflow = (
        jnp.maximum(velocity_row[:-1], 0.0) * states[:, :-1]
        + jnp.minimum(velocity_row[:-1], 0.0) * states[:, 1:]
    )
    carried = states[:, 1:-1] - outflow[:, 1:] + outflow[:, :-1]
    return carried + growth * carried * (1.0 - carried)


def to_trainer(value):
    return lax.ppermute(value.astype(jnp.bfloat16), "role", [(0, 1)])


def to_solver(value):
    return lax.ppermute(value.astype(jnp.bfloat16), "role", [(1, 0)])


def plain_training(features, hidden_narrow, out_narrow, own_fields, own_out, own_hidden, fields):
    layer_count, unit_rows = own_hidden.shape[:2]
    batch = own_fields.shape[0]
    first_unit = lax.axis_index("tile") * unit_rows
    momentum_out = to_trainer(own_out)
    momentum_hidden = to_trainer(own_hidden)
    full_hidden = [
        lax.all_gather(hidden_narrow[i], "tile", axis=0, tiled=True) for i in range(layer_count)
    ]
    inputs, summed_list = [], []
    activation = features
    for i in range(layer_count):
        inputs.append(activation)
        summed = jnp.dot(activation, full_hidden[i], preferred_element_type=jnp.float32)
        summed_list.append(summed)
        activation = jax.nn.silu(summed).astype(jnp.bfloat16)
    predicted = jnp.dot(activation, out_narrow, preferred_element_type=jnp.float32)
    residual = ((predicted - own_fields) / batch).astype(jnp.bfloat16)
    partial_grad = lax.dot_general(
        residual, out_narrow, (((1,), (1,)), ((), ())), preferred_element_type=jnp.float32
    )
    upstream = lax.psum(partial_grad, "tile")
    grad_out = jnp.dot(activation.T, residual, preferred_element_type=jnp.float32)
    sent_out = to_solver(grad_out)
    gradients, sent = [], []
    for i in reversed(range(layer_count)):
        slope = (upstream * silu_slope(summed_list[i])).astype(jnp.bfloat16)
        own_inputs = lax.dynamic_slice_in_dim(inputs[i], first_unit, unit_rows, 1)
        gradient = jnp.dot(own_inputs.T, slope, preferred_element_type=jnp.float32)
        gradients.append(gradient)
        sent.append(to_solver(gradient))
        if i > 0:
            upstream = lax.dot_general(
                slope, full_hidden[i], (((1,), (1,)), ((), ())), preferred_element_type=jnp.float32
            )
    solver_side = lax.axis_index("role") == 0
    grad_out = jnp.where(solver_side, sent_out.astype(jnp.float32), grad_out)
    other_hidden = jnp.where(solver_side, jnp.stack(sent[::-1]), momentum_hidden)
    return grad_out, jnp.stack(gradients[::-1]), momentum_out, other_hidden, to_trainer(fields)


LANES = 128
COLUMNS = 256


SUM_LAG = 7
PASS_LAG = 7


class Later:
    def __init__(self, build):
        self.build = build

    def start(self):
        self.build().start()

    def wait(self):
        self.build().wait()

    def wait_recv(self):
        self.build().wait_recv()

    def wait_send(self):
        self.build().wait_send()


def train_kernel(
    groups,
    features_hbm,
    fields_hbm,
    velocity_hbm,
    growth_hbm,
    assignment_hbm,
    out_hbm,
    hidden_hbm,
    own_fields,
    own_out,
    own_hidden,
    features_ref,
    velocity_ref,
    growth_ref,
    assignment_ref,
    left_velocity,
    left_edge,
    right_edge,
    lent_fields,
    chosen_ref,
    out_ref,
    got_out,
    got_hidden,
    got_fields,
    weights,
    inputs,
    top,
    factors,
    residual,
    slope_even,
    slope_odd,
    partial,
    core_away,
    slope,
    gradient,
    got_gradient,
    core_sum,
    x_away,
    x_sum,
    z_away,
    z_sum,
    z_send,
    z_recv,
    x_send,
    x_recv,
    core_send,
    core_recv,
    sum_send,
    sum_recv,
    slope_send,
    slope_recv,
    role_send,
    role_recv,
    pair_send,
    pair_recv,
    edge_send,
    edge_recv,
    local_sem,
):
    layer_count, unit_rows, width = hidden_hbm.shape
    batch, cells = fields_hbm.shape
    rows = partial.shape[2]
    half = batch // 2
    narrow, wide = jnp.bfloat16, jnp.float32
    tiles = groups * 4
    last = layer_count - 1
    role = lax.axis_index("role")
    tile = lax.axis_index("tile")
    core = lax.rem(tile, 2)
    x = lax.rem(tile // 2, 2)
    z = tile // 4
    solver = role == 0
    trainer = role == 1

    def device(z_at, x_at, core_at):
        return (role, z_at * 4 + x_at * 2 + core_at)

    z_places = [lax.rem(z + k, groups) for k in range(1, groups)]
    z_peers = [device(place, x, core) for place in z_places]
    x_peer = device(z, 1 - x, core)
    core_peer = device(z, x, 1 - core)
    role_peer = (1 - role, tile)
    right_peer = (role, lax.rem(tile + 1, tiles))
    left_peer = (role, lax.rem(tile + tiles - 1, tiles))
    far_peer = (role, lax.rem(tile + tiles - 1 + 2 * core, tiles))

    def remote(views, sent, arrived, peer):
        def build():
            source, target = views()
            return pltpu.make_async_remote_copy(
                src_ref=source,
                dst_ref=target,
                send_sem=sent[0].at[sent[1]],
                recv_sem=arrived[0].at[arrived[1]],
                device_id=peer,
                device_id_type=pl.DeviceIdType.MESH,
            )

        return Later(build)

    def local(views, semaphores, slot):
        def build():
            source, target = views()
            return pltpu.make_async_copy(source, target, semaphores.at[slot])

        return Later(build)

    def twice(view):
        return lambda: (view(),) * 2

    def across(view, kind, slot):
        return remote(twice(view), (role_send, kind), (role_recv, slot), role_peer)

    chunks = [pl.ds(j * COLUMNS, COLUMNS) for j in range(cells // COLUMNS)]
    parts = [pl.ds(j * COLUMNS, COLUMNS) for j in range(width // COLUMNS)]
    pieces = [pl.ds(j * LANES, LANES) for j in range(width // LANES)]
    per_part = COLUMNS // LANES
    count = len(chunks)
    lent = count // 2
    lent_cells = pl.ds(lent * COLUMNS, (count - lent) * COLUMNS)
    momenta = [across(lambda c=c: got_out.at[:, c], 0, j) for j, c in enumerate(chunks)]
    hidden_momentum = across(lambda: got_hidden, 1, count)
    fresh = [
        across(lambda c=c: got_fields.at[:, c], 2, count + 1 + j) for j, c in enumerate(chunks)
    ]
    shares = [across(lambda i=i: weights.at[i, z, x, core], 0, i) for i in range(layer_count)]
    lent_out = across(lambda: out_ref.at[:, lent_cells], 1, layer_count)
    lent_target = remote(
        lambda: (own_fields.at[:, lent_cells], lent_fields),
        (role_send, 2),
        (role_recv, layer_count + 1),
        role_peer,
    )
    residuals = [
        across(lambda c=c: residual.at[:, :, :, :, c], 3, layer_count + 2 + j)
        for j, c in enumerate(chunks[:lent])
    ]
    slope_shares = [
        across(lambda c=c: slope.at[z, x, :, c], 4, layer_count + 2 + lent + j)
        for j, c in enumerate(pieces)
    ]

    pairs = [lambda: (hidden_hbm, own_hidden)]
    pairs += [lambda c=c: (out_hbm.at[:, c], own_out.at[:, c]) for c in chunks]
    pairs += [
        lambda: (fields_hbm, own_fields),
        lambda: (velocity_hbm, velocity_ref),
        lambda: (growth_hbm, growth_ref),
        lambda: (assignment_hbm, assignment_ref),
        lambda: (features_hbm, features_ref),
    ]
    loads = [local(views, local_sem, k) for k, views in enumerate(pairs)]
    for load in loads:
        load.start()
    hidden_load, out_loads, small_loads = loads[0], loads[1 : 1 + len(chunks)], loads[1 + len(chunks) :]
    share_order = [last] + list(range(last))
    barrier = pltpu.get_barrier_semaphore()
    peers = z_peers + [x_peer, core_peer, role_peer, far_peer]
    for peer in peers:
        pl.semaphore_signal(barrier, inc=1, device_id=peer, device_id_type=pl.DeviceIdType.MESH)

    @pl.when(solver)
    def _():
        out_loads[0].wait()
        got_out[:, chunks[0]] = own_out[:, chunks[0]].astype(narrow)

    @pl.when(trainer)
    def _():
        hidden_load.wait()
        for i in share_order:
            weights[i, z, x, core] = own_hidden[i].astype(narrow)

    pl.semaphore_wait(barrier, len(peers))

    last_lanes = pl.ds(cells - LANES, LANES)
    edge_list = [
        (lambda: (fields_hbm.at[:, last_lanes], left_edge), right_peer),
        (lambda: (velocity_hbm.at[:, last_lanes], left_velocity), right_peer),
        (lambda: (fields_hbm.at[:, pl.ds(0, LANES)], right_edge), left_peer),
    ]
    edges = [
        remote(views, (edge_send, k), (edge_recv, k), peer)
        for k, (views, peer) in enumerate(edge_list)
    ]

    nearest = [
        sorted((p for p in range(groups) if p != q), key=lambda p: (abs(p - q), p))
        for q in range(groups)
    ]

    def pick(k):
        place = jnp.int32(nearest[0][k])
        for q in range(1, groups):
            place = jnp.where(z == q, nearest[q][k], place)
        return place

    z_origins = [pick(k) for k in range(groups - 1)]
    inner = jnp.logical_and(z > 0, z < groups - 1)

    def share_of(i, place, x_at):
        return twice(lambda: weights.at[i, place, x_at, core])

    def hop(i, place, item, kind, target):
        rank = jnp.where(place > target, place - 1, place)
        x_at = 1 - x if item == layer_count else x
        return remote(
            share_of(i, place, x_at),
            (z_send, kind + 2 * (item // layer_count)),
            (z_recv, (item, rank)),
            device(target, x, core),
        )

    def spread(item):
        i = min(item, last)

        @pl.when(z < groups - 1)
        def _():
            hop(i, z, item, 0, lax.rem(z + 1, groups)).start()

        @pl.when(z > 0)
        def _():
            hop(i, z, item, jnp.where(z == groups - 1, 0, 1), lax.rem(z + groups - 1, groups)).start()

    def onward(k):
        rising = z_origins[k] < z
        return jnp.logical_or(
            jnp.logical_and(rising, z < groups - 1),
            jnp.logical_and(jnp.logical_not(rising), z > 0),
        )

    def relay(item, k):
        i = min(item, last)
        place = z_origins[k]
        hop(i, place, item, 1, z).wait_recv()

        @pl.when(onward(k))
        def _():
            target = jnp.where(place < z, lax.rem(z + 1, groups), lax.rem(z + groups - 1, groups))
            hop(i, place, item, 1, target).start()

        if i < last:
            send_x(i, place, k)
        send_core(i, place, 1 - x if item == layer_count else x)

    def x_slot(i, k):
        return [0, 1, 2 + i, 2 + last + i][k + 1] if i < last else 2 + 2 * last

    def send_x(i, place, k):
        remote(share_of(i, place, x), (x_send, i // last), (x_recv, x_slot(i, k)), x_peer).start()

    def send_core(i, place, x_at):
        remote(share_of(i, place, x_at), (core_send, 0), (core_recv, i), core_peer).start()

    def arrived_x(views, slot):
        remote(twice(views), (x_send, 0), (x_recv, slot), x_peer).wait_recv()

    def cross(i, k):
        place = z if k < 0 else z_origins[k]
        arrived_x(lambda: weights.at[i, place, 1 - x, core], x_slot(i, k))
        send_core(i, place, 1 - x)

    def cross_wave(k):
        place = z if k < 0 else z_origins[k]
        arrived_x(lambda: weights.at[pl.ds(0, last), place, 1 - x, core], k + 1)
        for i in range(last):
            send_core(i, place, 1 - x)

    def send_share(i):
        @pl.when(solver)
        def _():
            shares[i].wait_recv()

        if i < last:
            spread(i)
        send_x(i, z, -1)
        send_core(i, z, x)


    def columns_of(j):
        return pl.ds(pl.multiple_of(j * COLUMNS, COLUMNS), COLUMNS)

    def advance():
        velocity = velocity_ref[...]
        forward_speed = jnp.maximum(velocity, 0.0)
        backward_speed = jnp.minimum(velocity, 0.0)
        growth = growth_ref[...]
        before = left_velocity[:, LANES - 1 :]
        step = LANES // 2

        @pl.loop(0, batch // step)
        def _(j):
            band = pl.ds(pl.multiple_of(j * step, step), step)
            current = own_fields[band, :]
            lane = lax.broadcasted_iota(jnp.int32, current.shape, 1)
            following = jnp.where(
                lane == cells - 1, right_edge[band, :1], pltpu.roll(current, cells - 1, 1)
            )
            outflow = forward_speed * current + backward_speed * following
            inflow_edge = (
                jnp.maximum(before, 0.0) * left_edge[band, :][:, LANES - 1 :]
                + jnp.minimum(before, 0.0) * current[:, :1]
            )
            inflow = jnp.where(lane == 0, inflow_edge, pltpu.roll(outflow, 1, 1))
            carried = current - outflow + inflow
            advanced = carried + growth * carried * (1.0 - carried)
            own_fields[band, :] = advanced
            got_fields[band, :] = advanced.astype(narrow)

    @pl.when(solver)
    def _():
        momenta[0].start()
        for copy in edges:
            copy.start()
        for j in range(1, count):
            out_loads[j].wait()
            got_out[:, chunks[j]] = own_out[:, chunks[j]].astype(narrow)
            if j < lent:
                momenta[j].start()
            if j == lent - 1:
                hidden_load.wait()
                got_hidden[...] = own_hidden[...].astype(narrow)
                hidden_momentum.start()

    @pl.when(trainer)
    def _():
        for i in share_order:
            shares[i].start()

    for i in share_order:
        send_share(i)

    for load in small_loads:
        load.wait()

    @pl.when(solver)
    def _():
        for copy in edges:
            copy.wait_recv()
        advance()
        for copy in fresh + momenta[lent:]:
            copy.start()

    @pl.when(trainer)
    def _():
        lent_target.start()
        for j in reversed(range(count)):
            out_loads[j].wait()
            out_ref[:, chunks[j]] = own_out[:, chunks[j]].astype(narrow)
            if j == lent:
                lent_out.start()
        member = lax.broadcasted_iota(jnp.int32, (batch, batch), 0)
        chosen = jnp.where(member == assignment_ref[...], 1.0, 0.0)
        chosen_ref[...] = chosen.T.astype(narrow)

    def beside(views, kind, slot):
        return remote(views, (pair_send, kind), (pair_recv, slot), core_peer)

    tops = [beside(twice(lambda c=c: top.at[:, :, core, :, c]), 0, 0) for c in parts]
    all_tops = beside(twice(lambda: top.at[:, :, core]), 0, 0)
    own_units = pl.ds(pl.multiple_of(core * unit_rows, unit_rows), unit_rows)
    other_units = pl.ds(pl.multiple_of((1 - core) * unit_rows, unit_rows), unit_rows)
    halves = [
        beside(lambda i=i: (gradient.at[i, other_units, :], got_gradient.at[i]), 1, 1 + i)
        for i in range(layer_count)
    ]
    all_halves = beside(lambda: (gradient.at[:, other_units, :], got_gradient), 1, 1)

    def forward_columns(i, columns):
        block = weights[i, :, :, :, :, columns].reshape(width, COLUMNS)
        activation = features_ref[:, :, core] if i == 0 else inputs[i - 1]
        summed = jnp.dot(activation.reshape(half, width), block, preferred_element_type=wide)
        logistic = jax.nn.sigmoid(summed)
        result = (summed * logistic).astype(narrow).reshape(groups, 2, rows, COLUMNS)
        factor = logistic * (1.0 + summed * (1.0 - logistic))
        factors[i, :, :, :, columns] = factor.reshape(groups, 2, rows, COLUMNS)
        return result

    def forward(i, between=None):
        for j, c in enumerate(parts):
            if between is not None and j == len(parts) // 2:
                between()
            if i < last:
                inputs[i, :, :, :, c] = forward_columns(i, c)
                continue
            top[:, :, core, :, c] = forward_columns(i, c)
            if j % 2:
                tops[j - 1].start()
                tops[j].start()

    def finish(i, between=None):
        remote(
            twice(lambda: weights.at[i, :, :, 1 - core]), (core_send, 0), (core_recv, i), core_peer
        ).wait_recv()
        forward(i, between)

    outer = jnp.logical_not(inner)
    lagging = [last, layer_count]

    @pl.when(inner)
    def _():
        for item in range(last):
            relay(item, 0)
            relay(item, 1)

    @pl.when(outer)
    def _():
        for item in range(last):
            relay(item, 0)

    spread(last)
    cross(last, -1)
    cross_wave(-1)

    @pl.when(inner)
    def _():
        for item in range(last):
            relay(item, 2)

    @pl.when(outer)
    def _():
        for item in range(last):
            relay(item, 1)

    spread(layer_count)
    cross_wave(0)

    @pl.when(inner)
    def _():
        for k in range(2):
            for item in lagging:
                relay(item, k)

    for item in range(last):

        @pl.when(outer)
        def _():
            relay(item, 2)

        cross(item, 1)

    @pl.when(inner)
    def _():
        for item in lagging:
            relay(item, 2)

    held = [(item, k) for k in range(groups - 1) for item in lagging]
    for i in range(last):

        @pl.when(outer)
        def _():
            for item, k in [held[:2], held[2:3], held[3:4], held[4:5]][i]:
                relay(item, k)

        cross(i, 2)
        if i > 0:
            finish(i - 1)
    def relay_held():
        @pl.when(outer)
        def _():
            for item, k in held[5:]:
                relay(item, k)

    finish(last - 1, relay_held)
    finish(last)

    def update_out(j, decay, rate, other):
        c = chunks[j]

        for units in parts:
            grad = lax.dot_general(
                top[:, :, :, :, units].reshape(batch, COLUMNS),
                residual[:, :, :, :, c].reshape(batch, COLUMNS),
                (((0,), (0,)), ((), ())),
                preferred_element_type=wide,
            )
            if rate is None:
                own_out[units, c] = decay * own_out[units, c] + grad
            elif other is None:
                own_out[units, c] = own_out[units, c] - rate * grad
            else:
                fresh_momentum = decay * other[units, c].astype(wide) + grad
                own_out[units, c] = own_out[units, c] - rate * fresh_momentum

    def update_solver(j):
        residuals[j].wait_recv()
        update_out(j, momentum_decay, None, None)

    def update_trainer(j):
        if j < lent:
            momenta[j].wait_recv()
        update_out(j, momentum_decay, step_size, got_out if j < lent else None)

    def add_momentum(j):
        momenta[j].wait_recv()
        for units in parts:
            late = momentum_decay * got_out[units, chunks[j]].astype(wide)
            own_out[units, chunks[j]] = own_out[units, chunks[j]] - step_size * late

    def gather(j):
        fresh[j].wait_recv()
        own_fields[:, chunks[j]] = jnp.dot(
            chosen_ref[...], got_fields[:, chunks[j]], preferred_element_type=wide
        )

    def summed(views, kind, slot, peer):
        return remote(views, (sum_send, kind), (sum_recv, slot), peer)

    core_sums = [
        summed(lambda c=c: (core_away.at[:, :, :, c], core_sum.at[:, :, :, c]), 0, j, core_peer)
        for j, c in enumerate(parts)
    ]
    x_sums = [
        summed(lambda c=c: (x_away.at[:, :, c], x_sum.at[:, :, c]), 1, len(parts) + j, x_peer)
        for j, c in enumerate(pieces)
    ]
    z_base = len(parts) + len(pieces)
    z_sums = [
        [
            summed(
                lambda c=c, k=k: (z_away.at[z_places[k], :, c], z_sum.at[k, :, c]),
                2,
                z_base + j,
                z_peers[k],
            )
            for k in range(groups - 1)
        ]
        for j, c in enumerate(pieces)
    ]
    others = pl.ds(0, groups - 1)
    all_sums = [
        summed(lambda: (core_away, core_sum), 0, 0, core_peer),
        summed(lambda: (x_away, x_sum), 1, 0, x_peer),
        summed(lambda: (z_away.at[others], z_sum), 2, 0, x_peer),
    ]
    targets = own_fields.reshape(groups, 2, 2, rows, cells)

    def residual_columns(side, c, wanted):
        rows_of = top[:, :, side].reshape(half, width)
        predicted = jnp.dot(rows_of, out_ref[:, c], preferred_element_type=wide)
        kept = ((predicted - wanted.reshape(half, COLUMNS)) / batch).astype(narrow)
        residual[:, :, side, :, c] = kept.reshape(groups, 2, rows, COLUMNS)

    def upstream_columns(side, c):
        return lax.dot_general(
            residual[:, :, side].reshape(half, cells),
            out_ref[c, :],
            (((1,), (1,)), ((), ())),
            preferred_element_type=wide,
        ).reshape(groups, 2, rows, COLUMNS)

    @pl.when(trainer)
    def _():
        for c in chunks:
            residual_columns(core, c, targets[:, :, core, :, c])
        early = len(parts) // 2
        for c in parts[:early]:
            partial[:, :, :, c] = upstream_columns(core, c)
        all_tops.wait_recv()
        for c in chunks:
            residual_columns(1 - core, c, targets[:, :, 1 - core, :, c])
        residuals[0].start()
        for c in parts:
            core_away[:, :, :, c] = upstream_columns(1 - core, c)
        for copy in core_sums:
            copy.start()
        for c in parts[early:]:
            partial[:, :, :, c] = upstream_columns(core, c)
        for j, c in enumerate(parts):
            core_sums[j].wait_recv()
            x_away[:, :, c] = (partial[:, 1 - x, :, c] + core_sum[:, 1 - x, :, c]).astype(narrow)
            for copy in x_sums[j * per_part : (j + 1) * per_part]:
                copy.start()
        update_trainer(0)
        lent_target.wait_send()
        for j in range(lent):
            gather(j)

    @pl.when(solver)
    def _():
        all_tops.wait_recv()
        lent_out.wait_recv()
        lent_target.wait_recv()
        lent_wanted = lent_fields.reshape(groups, 2, 2, rows, cells - lent * COLUMNS)
        for j in range(lent, count):
            for side in range(2):
                residual_columns(side, chunks[j], lent_wanted[:, :, side, :, chunks[j - lent]])
        for j in range(lent, count):
            update_out(j, momentum_decay, None, None)
        update_solver(0)

    def z_slope(c, slot, peer):
        return remote(
            twice(lambda: slope.at[z, x, :, c]), (slope_send, 0), (slope_recv, slot), peer
        )

    def x_slope(view):
        return remote(twice(view), (slope_send, 1), (slope_recv, len(pieces)), x_peer)

    def add_far(j, c):
        near = partial[:, x, :, c] + core_sum[:, x, :, c]
        x_sums[j].wait_recv()
        near = near + x_sum[:, :, c].astype(wide)
        partial[:, x, :, c] = near
        z_away[:, :, c] = near.astype(narrow)
        for copy in z_sums[j]:
            copy.start()

    def make_slope(j, c):
        summed(
            lambda: (z_away.at[others, :, c], z_sum.at[:, :, c]), 2, z_base + j, x_peer
        ).wait_recv()
        upstream = partial[z, x, :, c]
        for k in range(groups - 1):
            upstream = upstream + z_sum[k, :, c].astype(wide)
        slope[z, x, :, c] = (upstream * factors[last, z, x, :, c]).astype(narrow)
        slope_shares[j].start()

    def pass_slope(j, c):
        remote(
            twice(lambda: slope.at[others, x, :, c]), (slope_send, 0), (slope_recv, j), x_peer
        ).wait_recv()
        x_slope(lambda: slope.at[:, x, :, c]).start()

    for turn in range(len(pieces) + SUM_LAG + PASS_LAG):
        made, passed = turn - SUM_LAG, turn - SUM_LAG - PASS_LAG

        @pl.when(trainer)
        def _():
            if turn < len(pieces):
                add_far(turn, pieces[turn])
            if turn == len(pieces) // 2:
                update_trainer(1)
            if 0 <= made < len(pieces):
                make_slope(made, pieces[made])
            if made == len(pieces) - 1:
                for copy in residuals[1:]:
                    copy.start()
                for j in range(lent, count):
                    gather(j)

        if 0 <= made < len(pieces):

            @pl.when(solver)
            def _():
                slope_shares[made].wait_recv()

            for peer in z_peers:
                z_slope(pieces[made], made, peer).start()
        if passed >= 0:
            pass_slope(passed, pieces[passed])

    @pl.when(trainer)
    def _():
        for j in range(lent, count):
            update_trainer(j)
        hidden_momentum.wait_recv()

    @pl.when(solver)
    def _():
        for j in range(1, lent):
            update_solver(j)

    all_x_slopes = x_slope(lambda: slope.at[:, 1 - x])
    all_x_slopes.wait_recv()

    first_lane = pl.multiple_of((tile // 2) * LANES, LANES)

    def update_hidden(i):
        halves[i].wait_recv()
        total = gradient[i, own_units, :] + got_gradient[i]

        @pl.when(solver)
        def _():
            own_hidden[i] = momentum_decay * own_hidden[i] + total

        @pl.when(trainer)
        def _():
            fresh_momentum = momentum_decay * got_hidden[i].astype(wide) + total
            own_hidden[i] = own_hidden[i] - step_size * fresh_momentum

    slopes = [slope, slope_even, slope_odd]
    for step, i in enumerate(reversed(range(layer_count))):
        this_slope = slopes[0] if step == 0 else slopes[1 + step % 2]
        next_slope = slopes[1 + (step + 1) % 2]
        lanes = pl.ds(first_lane, LANES)
        own_inputs = features_ref[:, :, core, :, lanes] if i == 0 else inputs[i - 1, :, :, :, lanes]
        for c in parts:
            if i > 0:
                back = lax.dot_general(
                    this_slope[...].reshape(half, width),
                    weights.at[i].reshape(width, width)[c, :],
                    (((1,), (1,)), ((), ())),
                    preferred_element_type=wide,
                )
                factor = factors[i - 1, :, :, :, c].reshape(half, COLUMNS)
                next_slope[:, :, :, c] = (
                    (back * factor).astype(narrow).reshape(groups, 2, rows, COLUMNS)
                )
            gradient[i, :, c] = lax.dot_general(
                own_inputs.reshape(half, LANES),
                this_slope[:, :, :, c].reshape(half, COLUMNS),
                (((0,), (0,)), ((), ())),
                preferred_element_type=wide,
            )
        halves[i].start()

    @pl.when(trainer)
    def _():
        for j in range(lent, count):
            add_momentum(j)

    for i in reversed(range(layer_count)):
        update_hidden(i)

    def gone(view, semaphore, slot):
        remote(twice(view), (semaphore, slot), (x_recv, 0), x_peer).wait_send()

    gone(lambda: weights.at[:, :, :, core], core_send, 0)
    gone(lambda: weights.at[pl.ds(0, last), :, x, core], x_send, 0)
    gone(lambda: weights.at[last, z, x, core], x_send, 1)
    gone(lambda: weights.at[:, z, x, core], z_send, 0)
    gone(lambda: weights.at[last, z, x, core], z_send, 2)

    @pl.when(inner)
    def _():
        gone(lambda: weights.at[:, :, x, core], z_send, 1)
        gone(lambda: weights.at[last, :, x, core], z_send, 3)

    all_tops.wait_send()
    all_halves.wait_send()
    gone(lambda: slope.at[others, x], slope_send, 0)
    gone(lambda: slope.at[:, x], slope_send, 1)

    @pl.when(solver)
    def _():
        for copy in edges:
            copy.wait_send()
        gone(lambda: got_out, role_send, 0)
        gone(lambda: got_hidden, role_send, 1)
        gone(lambda: got_fields, role_send, 2)

    @pl.when(trainer)
    def _():
        for copy in all_sums:
            copy.wait_send()
        gone(lambda: weights.at[:, z, x, core], role_send, 0)
        gone(lambda: out_ref.at[:, lent_cells], role_send, 1)
        gone(lambda: residual.at[:, :, :, :, pl.ds(0, lent * COLUMNS)], role_send, 3)
        gone(lambda: slope.at[z, x], role_send, 4)


def store_kernel(*refs):
    semaphores = refs[-1]
    copies = []
    for source, target in zip(refs[:3], refs[3:6]):
        length = source.shape[0]
        step = length if length % 4 else length // 4
        for at in range(0, length, step):
            band = pl.ds(at, step)
            copies.append(
                pltpu.make_async_copy(
                    source.at[band], target.at[band], semaphores.at[len(copies)]
                )
            )
    for copy in copies:
        copy.start()
    for copy in copies:
        copy.wait()


def fused_step(fields, velocity, growth, features, assignment, own_out, own_hidden):
    layer_count, unit_rows, width = own_hidden.shape
    batch, cells = fields.shape
    groups = lax.axis_size("tile") // 4
    rows = batch // lax.axis_size("tile")
    narrow, wide = jnp.bfloat16, jnp.float32
    dma = pltpu.SemaphoreType.DMA
    anywhere = pl.BlockSpec(memory_space=pl.ANY)
    parts, pieces = width // COLUMNS, cells // COLUMNS
    splits = width // LANES
    splits = width // LANES
    role_slots = layer_count + 3 * pieces + 1 + splits
    split = (groups, 2, 2, rows, width)
    results = pl.pallas_call(
        functools.partial(train_kernel, groups),
        out_shape=(
            jax.ShapeDtypeStruct(fields.shape, wide),
            jax.ShapeDtypeStruct(own_out.shape, wide),
            jax.ShapeDtypeStruct(own_hidden.shape, wide),
        ),
        in_specs=[anywhere] * 7,
        out_specs=[pl.BlockSpec(memory_space=pltpu.VMEM)] * 3,
        scratch_shapes=[
            pltpu.VMEM(split, narrow),
            pltpu.VMEM((1, cells), wide),
            pltpu.VMEM((1, cells), wide),
            pltpu.VMEM((1, batch), jnp.int32),
            pltpu.VMEM((1, LANES), wide),
            pltpu.VMEM((batch, LANES), wide),
            pltpu.VMEM((batch, LANES), wide),
            pltpu.VMEM((batch, cells // 2), wide),
            pltpu.VMEM((batch, batch), narrow),
            pltpu.VMEM((width, cells), narrow),
            pltpu.VMEM((width, cells), narrow),
            pltpu.VMEM(own_hidden.shape, narrow),
            pltpu.VMEM((batch, cells), narrow),
            pltpu.VMEM((layer_count, groups, 2, 2, unit_rows, width), narrow),
            pltpu.VMEM((layer_count - 1, groups, 2, rows, width), narrow),
            pltpu.VMEM(split, narrow),
            pltpu.VMEM((layer_count, groups, 2, rows, width), wide),
            pltpu.VMEM((groups, 2, 2, rows, cells), narrow),
            pltpu.VMEM((groups, 2, rows, width), narrow),
            pltpu.VMEM((groups, 2, rows, width), narrow),
            pltpu.VMEM((groups, 2, rows, width), wide),
            pltpu.VMEM((groups, 2, rows, width), wide),
            pltpu.VMEM((groups, 2, rows, width), narrow),
            pltpu.VMEM((layer_count, LANES, width), wide),
            pltpu.VMEM(own_hidden.shape, wide),
            pltpu.VMEM((groups, 2, rows, width), wide),
            pltpu.VMEM((groups, rows, width), narrow),
            pltpu.VMEM((groups, rows, width), narrow),
            pltpu.VMEM((groups, rows, width), narrow),
            pltpu.VMEM((groups - 1, rows, width), narrow),
            dma((4,)),
            dma((layer_count + 1, groups - 1)),
            dma((2,)),
            dma((2 * layer_count + 1,)),
            dma((1,)),
            dma((layer_count,)),
            dma((3,)),
            dma((parts + 2 * splits,)),
            dma((2,)),
            dma((splits + 1,)),
            dma((5,)),
            dma((layer_count + 2 + pieces // 2 + splits,)),
            dma((2,)),
            dma((1 + layer_count,)),
            dma((3,)),
            dma((3,)),
            dma((6 + pieces,)),
        ],
        compiler_params=pltpu.CompilerParams(
            collective_id=0, has_side_effects=True, vmem_limit_bytes=46000000
        ),
        cost_estimate=pl.CostEstimate(
            flops=60 * batch * width * width, bytes_accessed=40 * batch * width, transcendentals=0
        ),
    )(
        *(
            pltpu.with_memory_space_constraint(value, pltpu.HBM)
            for value in (
                features.reshape(split),
                fields,
                velocity[None, :],
                growth[None, :],
                assignment[None, :],
                own_out,
                own_hidden,
            )
        )
    )
    return pl.pallas_call(
        store_kernel,
        out_shape=tuple(jax.ShapeDtypeStruct(v.shape, v.dtype) for v in results),
        in_specs=[anywhere] * 3,
        out_specs=[anywhere] * 3,
        scratch_shapes=[dma((12,))],
        compiler_params=pltpu.CompilerParams(vmem_limit_bytes=1 << 20),
    )(*results)


def plain_body(fields_pair, velocity, growth, features, assignment, out_pair, hidden_pair):
    solver_side = lax.axis_index("role") == 0
    own_fields = fields_pair[0]
    own_out = out_pair[0]
    own_hidden = hidden_pair[0]
    stacked = jnp.concatenate([own_fields, velocity[None, :]], axis=0)
    advanced = advance(extended(stacked, "tile", 1, 1), growth)
    grad_out, grad_hidden, other_out, other_hidden, fresh_fields = plain_training(
        features,
        own_hidden.astype(jnp.bfloat16),
        own_out.astype(jnp.bfloat16),
        own_fields,
        own_out,
        own_hidden,
        advanced.astype(jnp.bfloat16),
    )
    grad_out, grad_hidden, other_out, other_hidden = (
        v.astype(jnp.float32) for v in (grad_out, grad_hidden, other_out, other_hidden)
    )
    out_next = jnp.where(
        solver_side,
        momentum_decay * own_out + grad_out,
        own_out - step_size * (momentum_decay * other_out + grad_out),
    )
    hidden_next = jnp.where(
        solver_side,
        momentum_decay * own_hidden + other_hidden,
        own_hidden - step_size * (momentum_decay * other_hidden + grad_hidden),
    )
    next_batch = jnp.take(fresh_fields, assignment, axis=0).astype(jnp.float32)
    fields_next = jnp.where(solver_side, advanced, next_batch)
    return (fields_next[None], out_next[None], hidden_next[None])


def body(fields_pair, velocity, growth, features, assignment, out_pair, hidden_pair):
    tiles = lax.axis_size("tile")
    batch, cells = fields_pair.shape[1:]
    layer_count, unit_rows, width = hidden_pair.shape[1:]
    fits = (
        lax.axis_size("role") == 2
        and tiles == 16
        and layer_count == 5
        and batch % tiles == 0
        and (batch // tiles) % 16 == 0
        and LANES == 2 * unit_rows
        and width % COLUMNS == 0
        and cells % COLUMNS == 0
        and cells // COLUMNS == 4
    )
    if not fits:
        return plain_body(
            fields_pair, velocity, growth, features, assignment, out_pair, hidden_pair
        )
    results = fused_step(
        fields_pair[0], velocity, growth, features, assignment, out_pair[0], hidden_pair[0]
    )
    return tuple(result[None] for result in results)


def solution(mesh):
    return jax.shard_map(
        body,
        mesh=mesh,
        in_specs=(
            P("role", None, "tile"),
            P("tile"),
            P("tile"),
            P(),
            P(),
            P("role", None, "tile"),
            P("role", None, "tile", None),
        ),
        out_specs=(P("role", None, "tile"), P("role", None, "tile"), P("role", None, "tile", None)),
        check_vma=False,
    )
```

```python
import functools

import jax
import jax.numpy as jnp
from jax import lax
from jax.experimental import pallas as pl
from jax.experimental.pallas import tpu as pltpu
from jax.sharding import PartitionSpec as P

momentum_decay = 0.9
step_size = 0.1


def extended(value, axis, dim, width):
    count, length = (lax.axis_size(axis), value.shape[dim])
    up = [(i, (i + 1) % count) for i in range(count)]
    down = [(j, i) for i, j in up]
    last = lax.slice_in_dim(value, length - width, length, axis=dim)
    leading = lax.slice_in_dim(value, 0, width, axis=dim)
    before = lax.ppermute(last, axis, up)
    after = lax.ppermute(leading, axis, down)
    return jnp.concatenate([before, value, after], axis=dim)


def silu_slope(values):
    logistic = jax.nn.sigmoid(values)
    return logistic * (1.0 + values * (1.0 - logistic))


def advance(padded, growth):
    states = padded[:-1]
    velocity_row = padded[-1]
    outflow = (
        jnp.maximum(velocity_row[:-1], 0.0) * states[:, :-1]
        + jnp.minimum(velocity_row[:-1], 0.0) * states[:, 1:]
    )
    carried = states[:, 1:-1] - outflow[:, 1:] + outflow[:, :-1]
    return carried + growth * carried * (1.0 - carried)


def to_trainer(value):
    return lax.ppermute(value.astype(jnp.bfloat16), "role", [(0, 1)])


def to_solver(value):
    return lax.ppermute(value.astype(jnp.bfloat16), "role", [(1, 0)])


def plain_training(features, hidden_narrow, out_narrow, own_fields, own_out, own_hidden, fields):
    layer_count, unit_rows = own_hidden.shape[:2]
    batch = own_fields.shape[0]
    first_unit = lax.axis_index("tile") * unit_rows
    momentum_out = to_trainer(own_out)
    momentum_hidden = to_trainer(own_hidden)
    full_hidden = [
        lax.all_gather(hidden_narrow[i], "tile", axis=0, tiled=True) for i in range(layer_count)
    ]
    inputs, summed_list = [], []
    activation = features
    for i in range(layer_count):
        inputs.append(activation)
        summed = jnp.dot(activation, full_hidden[i], preferred_element_type=jnp.float32)
        summed_list.append(summed)
        activation = jax.nn.silu(summed).astype(jnp.bfloat16)
    predicted = jnp.dot(activation, out_narrow, preferred_element_type=jnp.float32)
    residual = ((predicted - own_fields) / batch).astype(jnp.bfloat16)
    partial_grad = lax.dot_general(
        residual, out_narrow, (((1,), (1,)), ((), ())), preferred_element_type=jnp.float32
    )
    upstream = lax.psum(partial_grad, "tile")
    grad_out = jnp.dot(activation.T, residual, preferred_element_type=jnp.float32)
    sent_out = to_solver(grad_out)
    gradients, sent = [], []
    for i in reversed(range(layer_count)):
        slope = (upstream * silu_slope(summed_list[i])).astype(jnp.bfloat16)
        own_inputs = lax.dynamic_slice_in_dim(inputs[i], first_unit, unit_rows, 1)
        gradient = jnp.dot(own_inputs.T, slope, preferred_element_type=jnp.float32)
        gradients.append(gradient)
        sent.append(to_solver(gradient))
        if i > 0:
            upstream = lax.dot_general(
                slope, full_hidden[i], (((1,), (1,)), ((), ())), preferred_element_type=jnp.float32
            )
    solver_side = lax.axis_index("role") == 0
    grad_out = jnp.where(solver_side, sent_out.astype(jnp.float32), grad_out)
    other_hidden = jnp.where(solver_side, jnp.stack(sent[::-1]), momentum_hidden)
    return grad_out, jnp.stack(gradients[::-1]), momentum_out, other_hidden, to_trainer(fields)


LANES = 128
COLUMNS = 256


SUM_LAG = 7
PASS_LAG = 7


class Later:
    def __init__(self, build):
        self.build = build

    def start(self):
        self.build().start()

    def wait(self):
        self.build().wait()

    def wait_recv(self):
        self.build().wait_recv()

    def wait_send(self):
        self.build().wait_send()


def train_kernel(
    groups,
    features_hbm,
    fields_hbm,
    velocity_hbm,
    growth_hbm,
    assignment_hbm,
    out_hbm,
    hidden_hbm,
    own_fields,
    own_out,
    own_hidden,
    features_ref,
    velocity_ref,
    growth_ref,
    assignment_ref,
    left_velocity,
    left_edge,
    right_edge,
    lent_fields,
    chosen_ref,
    out_ref,
    got_out,
    got_hidden,
    got_fields,
    weights,
    inputs,
    top,
    factors,
    residual,
    slope_even,
    slope_odd,
    partial,
    core_away,
    slope,
    gradient,
    got_gradient,
    core_sum,
    x_away,
    x_sum,
    z_away,
    z_sum,
    z_send,
    z_recv,
    x_send,
    x_recv,
    core_send,
    core_recv,
    sum_send,
    sum_recv,
    slope_send,
    slope_recv,
    role_send,
    role_recv,
    pair_send,
    pair_recv,
    edge_send,
    edge_recv,
    local_sem,
):
    layer_count, unit_rows, width = hidden_hbm.shape
    batch, cells = fields_hbm.shape
    rows = partial.shape[2]
    half = batch // 2
    narrow, wide = jnp.bfloat16, jnp.float32
    tiles = groups * 4
    last = layer_count - 1
    role = lax.axis_index("role")
    tile = lax.axis_index("tile")
    core = lax.rem(tile, 2)
    x = lax.rem(tile // 2, 2)
    z = tile // 4
    solver = role == 0
    trainer = role == 1

    def device(z_at, x_at, core_at):
        return (role, z_at * 4 + x_at * 2 + core_at)

    z_places = [lax.rem(z + k, groups) for k in range(1, groups)]
    z_peers = [device(place, x, core) for place in z_places]
    x_peer = device(z, 1 - x, core)
    core_peer = device(z, x, 1 - core)
    role_peer = (1 - role, tile)
    right_peer = (role, lax.rem(tile + 1, tiles))
    left_peer = (role, lax.rem(tile + tiles - 1, tiles))
    far_peer = (role, lax.rem(tile + tiles - 1 + 2 * core, tiles))

    def remote(views, sent, arrived, peer):
        def build():
            source, target = views()
            return pltpu.make_async_remote_copy(
                src_ref=source,
                dst_ref=target,
                send_sem=sent[0].at[sent[1]],
                recv_sem=arrived[0].at[arrived[1]],
                device_id=peer,
                device_id_type=pl.DeviceIdType.MESH,
            )

        return Later(build)

    def local(views, semaphores, slot):
        def build():
            source, target = views()
            return pltpu.make_async_copy(source, target, semaphores.at[slot])

        return Later(build)

    def twice(view):
        return lambda: (view(),) * 2

    def across(view, kind, slot):
        return remote(twice(view), (role_send, kind), (role_recv, slot), role_peer)

    chunks = [pl.ds(j * COLUMNS, COLUMNS) for j in range(cells // COLUMNS)]
    parts = [pl.ds(j * COLUMNS, COLUMNS) for j in range(width // COLUMNS)]
    pieces = [pl.ds(j * LANES, LANES) for j in range(width // LANES)]
    per_part = COLUMNS // LANES
    count = len(chunks)
    lent = count // 2
    lent_cells = pl.ds(lent * COLUMNS, (count - lent) * COLUMNS)
    momenta = [across(lambda c=c: got_out.at[:, c], 0, j) for j, c in enumerate(chunks)]
    hidden_momentum = across(lambda: got_hidden, 1, count)
    fresh = [
        across(lambda c=c: got_fields.at[:, c], 2, count + 1 + j) for j, c in enumerate(chunks)
    ]
    shares = [across(lambda i=i: weights.at[i, z, x, core], 0, i) for i in range(layer_count)]
    lent_out = across(lambda: out_ref.at[:, lent_cells], 1, layer_count)
    lent_target = remote(
        lambda: (own_fields.at[:, lent_cells], lent_fields),
        (role_send, 2),
        (role_recv, layer_count + 1),
        role_peer,
    )
    residuals = [
        across(lambda c=c: residual.at[:, :, :, :, c], 3, layer_count + 2 + j)
        for j, c in enumerate(chunks[:lent])
    ]
    slope_shares = [
        across(lambda c=c: slope.at[z, x, :, c], 4, layer_count + 2 + lent + j)
        for j, c in enumerate(pieces)
    ]

    pairs = [lambda: (hidden_hbm, own_hidden)]
    pairs += [lambda c=c: (out_hbm.at[:, c], own_out.at[:, c]) for c in chunks]
    pairs += [
        lambda: (fields_hbm, own_fields),
        lambda: (velocity_hbm, velocity_ref),
        lambda: (growth_hbm, growth_ref),
        lambda: (assignment_hbm, assignment_ref),
        lambda: (features_hbm, features_ref),
    ]
    loads = [local(views, local_sem, k) for k, views in enumerate(pairs)]
    for load in loads:
        load.start()
    hidden_load, out_loads, small_loads = loads[0], loads[1 : 1 + len(chunks)], loads[1 + len(chunks) :]
    share_order = [last] + list(range(last))
    barrier = pltpu.get_barrier_semaphore()
    peers = z_peers + [x_peer, core_peer, role_peer, far_peer]
    for peer in peers:
        pl.semaphore_signal(barrier, inc=1, device_id=peer, device_id_type=pl.DeviceIdType.MESH)

    @pl.when(solver)
    def _():
        out_loads[0].wait()
        got_out[:, chunks[0]] = own_out[:, chunks[0]].astype(narrow)

    @pl.when(trainer)
    def _():
        hidden_load.wait()
        for i in share_order:
            weights[i, z, x, core] = own_hidden[i].astype(narrow)

    pl.semaphore_wait(barrier, len(peers))

    last_lanes = pl.ds(cells - LANES, LANES)
    edge_list = [
        (lambda: (fields_hbm.at[:, last_lanes], left_edge), right_peer),
        (lambda: (velocity_hbm.at[:, last_lanes], left_velocity), right_peer),
        (lambda: (fields_hbm.at[:, pl.ds(0, LANES)], right_edge), left_peer),
    ]
    edges = [
        remote(views, (edge_send, k), (edge_recv, k), peer)
        for k, (views, peer) in enumerate(edge_list)
    ]

    nearest = [
        sorted((p for p in range(groups) if p != q), key=lambda p: (abs(p - q), p))
        for q in range(groups)
    ]

    def pick(k):
        place = jnp.int32(nearest[0][k])
        for q in range(1, groups):
            place = jnp.where(z == q, nearest[q][k], place)
        return place

    z_origins = [pick(k) for k in range(groups - 1)]
    inner = jnp.logical_and(z > 0, z < groups - 1)

    def share_of(i, place, x_at):
        return twice(lambda: weights.at[i, place, x_at, core])

    def hop(i, place, item, kind, target):
        rank = jnp.where(place > target, place - 1, place)
        x_at = 1 - x if item == layer_count else x
        return remote(
            share_of(i, place, x_at),
            (z_send, kind + 2 * (item // layer_count)),
            (z_recv, (item, rank)),
            device(target, x, core),
        )

    def spread(item):
        i = min(item, last)

        @pl.when(z < groups - 1)
        def _():
            hop(i, z, item, 0, lax.rem(z + 1, groups)).start()

        @pl.when(z > 0)
        def _():
            hop(i, z, item, jnp.where(z == groups - 1, 0, 1), lax.rem(z + groups - 1, groups)).start()

    def onward(k):
        rising = z_origins[k] < z
        return jnp.logical_or(
            jnp.logical_and(rising, z < groups - 1),
            jnp.logical_and(jnp.logical_not(rising), z > 0),
        )

    def relay(item, k):
        i = min(item, last)
        place = z_origins[k]
        hop(i, place, item, 1, z).wait_recv()

        @pl.when(onward(k))
        def _():
            target = jnp.where(place < z, lax.rem(z + 1, groups), lax.rem(z + groups - 1, groups))
            hop(i, place, item, 1, target).start()

        if i < last:
            send_x(i, place, k)
        send_core(i, place, 1 - x if item == layer_count else x)

    def x_slot(i, k):
        return [0, 1, 2 + i, 2 + last + i][k + 1] if i < last else 2 + 2 * last

    def send_x(i, place, k):
        remote(share_of(i, place, x), (x_send, i // last), (x_recv, x_slot(i, k)), x_peer).start()

    def send_core(i, place, x_at):
        remote(share_of(i, place, x_at), (core_send, 0), (core_recv, i), core_peer).start()

    def arrived_x(views, slot):
        remote(twice(views), (x_send, 0), (x_recv, slot), x_peer).wait_recv()

    def cross(i, k):
        place = z if k < 0 else z_origins[k]
        arrived_x(lambda: weights.at[i, place, 1 - x, core], x_slot(i, k))
        send_core(i, place, 1 - x)

    def cross_wave(k):
        place = z if k < 0 else z_origins[k]
        arrived_x(lambda: weights.at[pl.ds(0, last), place, 1 - x, core], k + 1)
        for i in range(last):
            send_core(i, place, 1 - x)

    def send_share(i):
        @pl.when(solver)
        def _():
            shares[i].wait_recv()

        if i < last:
            spread(i)
        send_x(i, z, -1)
        send_core(i, z, x)


    def columns_of(j):
        return pl.ds(pl.multiple_of(j * COLUMNS, COLUMNS), COLUMNS)

    def advance():
        velocity = velocity_ref[...]
        forward_speed = jnp.maximum(velocity, 0.0)
        backward_speed = jnp.minimum(velocity, 0.0)
        growth = growth_ref[...]
        before = left_velocity[:, LANES - 1 :]
        step = LANES // 2

        @pl.loop(0, batch // step)
        def _(j):
            band = pl.ds(pl.multiple_of(j * step, step), step)
            current = own_fields[band, :]
            lane = lax.broadcasted_iota(jnp.int32, current.shape, 1)
            following = jnp.where(
                lane == cells - 1, right_edge[band, :1], pltpu.roll(current, cells - 1, 1)
            )
            outflow = forward_speed * current + backward_speed * following
            inflow_edge = (
                jnp.maximum(before, 0.0) * left_edge[band, :][:, LANES - 1 :]
                + jnp.minimum(before, 0.0) * current[:, :1]
            )
            inflow = jnp.where(lane == 0, inflow_edge, pltpu.roll(outflow, 1, 1))
            carried = current - outflow + inflow
            advanced = carried + growth * carried * (1.0 - carried)
            own_fields[band, :] = advanced
            got_fields[band, :] = advanced.astype(narrow)

    @pl.when(solver)
    def _():
        momenta[0].start()
        for copy in edges:
            copy.start()
        for j in range(1, count):
            out_loads[j].wait()
            got_out[:, chunks[j]] = own_out[:, chunks[j]].astype(narrow)
            if j < lent:
                momenta[j].start()
            if j == lent - 1:
                hidden_load.wait()
                got_hidden[...] = own_hidden[...].astype(narrow)
                hidden_momentum.start()

    @pl.when(trainer)
    def _():
        for i in share_order:
            shares[i].start()

    for i in share_order:
        send_share(i)

    for load in small_loads:
        load.wait()

    @pl.when(solver)
    def _():
        for copy in edges:
            copy.wait_recv()
        advance()
        for copy in fresh + momenta[lent:]:
            copy.start()

    @pl.when(trainer)
    def _():
        lent_target.start()
        for j in reversed(range(count)):
            out_loads[j].wait()
            out_ref[:, chunks[j]] = own_out[:, chunks[j]].astype(narrow)
            if j == lent:
                lent_out.start()
        member = lax.broadcasted_iota(jnp.int32, (batch, batch), 0)
        chosen = jnp.where(member == assignment_ref[...], 1.0, 0.0)
        chosen_ref[...] = chosen.T.astype(narrow)

    def beside(views, kind, slot):
        return remote(views, (pair_send, kind), (pair_recv, slot), core_peer)

    tops = [beside(twice(lambda c=c: top.at[:, :, core, :, c]), 0, 0) for c in parts]
    all_tops = beside(twice(lambda: top.at[:, :, core]), 0, 0)
    own_units = pl.ds(pl.multiple_of(core * unit_rows, unit_rows), unit_rows)
    other_units = pl.ds(pl.multiple_of((1 - core) * unit_rows, unit_rows), unit_rows)
    halves = [
        beside(lambda i=i: (gradient.at[i, other_units, :], got_gradient.at[i]), 1, 1 + i)
        for i in range(layer_count)
    ]
    all_halves = beside(lambda: (gradient.at[:, other_units, :], got_gradient), 1, 1)

    def forward_columns(i, columns):
        block = weights[i, :, :, :, :, columns].reshape(width, COLUMNS)
        activation = features_ref[:, :, core] if i == 0 else inputs[i - 1]
        summed = jnp.dot(activation.reshape(half, width), block, preferred_element_type=wide)
        logistic = jax.nn.sigmoid(summed)
        result = (summed * logistic).astype(narrow).reshape(groups, 2, rows, COLUMNS)
        factor = logistic * (1.0 + summed * (1.0 - logistic))
        factors[i, :, :, :, columns] = factor.reshape(groups, 2, rows, COLUMNS)
        return result

    def forward(i, between=None):
        for j, c in enumerate(parts):
            if between is not None and j == len(parts) // 2:
                between()
            if i < last:
                inputs[i, :, :, :, c] = forward_columns(i, c)
                continue
            top[:, :, core, :, c] = forward_columns(i, c)
            if j % 2:
                tops[j - 1].start()
                tops[j].start()

    def finish(i, between=None):
        remote(
            twice(lambda: weights.at[i, :, :, 1 - core]), (core_send, 0), (core_recv, i), core_peer
        ).wait_recv()
        forward(i, between)

    outer = jnp.logical_not(inner)
    lagging = [last, layer_count]

    @pl.when(inner)
    def _():
        for item in range(last):
            relay(item, 0)
            relay(item, 1)

    @pl.when(outer)
    def _():
        for item in range(last):
            relay(item, 0)

    spread(last)
    cross(last, -1)
    cross_wave(-1)

    @pl.when(inner)
    def _():
        for item in range(last):
            relay(item, 2)

    @pl.when(outer)
    def _():
        for item in range(last):
            relay(item, 1)

    spread(layer_count)
    cross_wave(0)

    @pl.when(inner)
    def _():
        for k in range(2):
            for item in lagging:
                relay(item, k)

    for item in range(last):

        @pl.when(outer)
        def _():
            relay(item, 2)

        cross(item, 1)

    @pl.when(inner)
    def _():
        for item in lagging:
            relay(item, 2)

    held = [(item, k) for k in range(groups - 1) for item in lagging]
    for i in range(last):

        @pl.when(outer)
        def _():
            for item, k in [held[:2], held[2:3], held[3:4], held[4:5]][i]:
                relay(item, k)

        cross(i, 2)
        if i > 0:
            finish(i - 1)
    def relay_held():
        @pl.when(outer)
        def _():
            for item, k in held[5:]:
                relay(item, k)

    finish(last - 1, relay_held)
    finish(last)

    def update_out(j, decay, rate, other):
        c = chunks[j]

        for units in parts:
            grad = lax.dot_general(
                top[:, :, :, :, units].reshape(batch, COLUMNS),
                residual[:, :, :, :, c].reshape(batch, COLUMNS),
                (((0,), (0,)), ((), ())),
                preferred_element_type=wide,
            )
            if rate is None:
                own_out[units, c] = decay * own_out[units, c] + grad
            elif other is None:
                own_out[units, c] = own_out[units, c] - rate * grad
            else:
                fresh_momentum = decay * other[units, c].astype(wide) + grad
                own_out[units, c] = own_out[units, c] - rate * fresh_momentum

    def update_solver(j):
        residuals[j].wait_recv()
        update_out(j, momentum_decay, None, None)

    def update_trainer(j):
        if j < lent:
            momenta[j].wait_recv()
        update_out(j, momentum_decay, step_size, got_out if j < lent else None)

    def add_momentum(j):
        momenta[j].wait_recv()
        for units in parts:
            late = momentum_decay * got_out[units, chunks[j]].astype(wide)
            own_out[units, chunks[j]] = own_out[units, chunks[j]] - step_size * late

    def gather(j):
        fresh[j].wait_recv()
        own_fields[:, chunks[j]] = jnp.dot(
            chosen_ref[...], got_fields[:, chunks[j]], preferred_element_type=wide
        )

    def summed(views, kind, slot, peer):
        return remote(views, (sum_send, kind), (sum_recv, slot), peer)

    core_sums = [
        summed(lambda c=c: (core_away.at[:, :, :, c], core_sum.at[:, :, :, c]), 0, j, core_peer)
        for j, c in enumerate(parts)
    ]
    x_sums = [
        summed(lambda c=c: (x_away.at[:, :, c], x_sum.at[:, :, c]), 1, len(parts) + j, x_peer)
        for j, c in enumerate(pieces)
    ]
    z_base = len(parts) + len(pieces)
    z_sums = [
        [
            summed(
                lambda c=c, k=k: (z_away.at[z_places[k], :, c], z_sum.at[k, :, c]),
                2,
                z_base + j,
                z_peers[k],
            )
            for k in range(groups - 1)
        ]
        for j, c in enumerate(pieces)
    ]
    others = pl.ds(0, groups - 1)
    all_sums = [
        summed(lambda: (core_away, core_sum), 0, 0, core_peer),
        summed(lambda: (x_away, x_sum), 1, 0, x_peer),
        summed(lambda: (z_away.at[others], z_sum), 2, 0, x_peer),
    ]
    targets = own_fields.reshape(groups, 2, 2, rows, cells)

    def residual_columns(side, c, wanted):
        rows_of = top[:, :, side].reshape(half, width)
        predicted = jnp.dot(rows_of, out_ref[:, c], preferred_element_type=wide)
        kept = ((predicted - wanted.reshape(half, COLUMNS)) / batch).astype(narrow)
        residual[:, :, side, :, c] = kept.reshape(groups, 2, rows, COLUMNS)

    def upstream_columns(side, c):
        return lax.dot_general(
            residual[:, :, side].reshape(half, cells),
            out_ref[c, :],
            (((1,), (1,)), ((), ())),
            preferred_element_type=wide,
        ).reshape(groups, 2, rows, COLUMNS)

    @pl.when(trainer)
    def _():
        for c in chunks:
            residual_columns(core, c, targets[:, :, core, :, c])
        early = len(parts) // 2
        for c in parts[:early]:
            partial[:, :, :, c] = upstream_columns(core, c)
        all_tops.wait_recv()
        for c in chunks:
            residual_columns(1 - core, c, targets[:, :, 1 - core, :, c])
        residuals[0].start()
        for c in parts:
            core_away[:, :, :, c] = upstream_columns(1 - core, c)
        for copy in core_sums:
            copy.start()
        for c in parts[early:]:
            partial[:, :, :, c] = upstream_columns(core, c)
        for j, c in enumerate(parts):
            core_sums[j].wait_recv()
            x_away[:, :, c] = (partial[:, 1 - x, :, c] + core_sum[:, 1 - x, :, c]).astype(narrow)
            for copy in x_sums[j * per_part : (j + 1) * per_part]:
                copy.start()
        update_trainer(0)
        lent_target.wait_send()

    @pl.when(solver)
    def _():
        all_tops.wait_recv()
        lent_out.wait_recv()
        lent_target.wait_recv()
        lent_wanted = lent_fields.reshape(groups, 2, 2, rows, cells - lent * COLUMNS)
        for j in range(lent, count):
            for side in range(2):
                residual_columns(side, chunks[j], lent_wanted[:, :, side, :, chunks[j - lent]])
        for j in range(lent, count):
            update_out(j, momentum_decay, None, None)
        update_solver(0)

    def z_slope(c, slot, peer):
        return remote(
            twice(lambda: slope.at[z, x, :, c]), (slope_send, 0), (slope_recv, slot), peer
        )

    def x_slope(view):
        return remote(twice(view), (slope_send, 1), (slope_recv, len(pieces)), x_peer)

    def add_far(j, c):
        near = partial[:, x, :, c] + core_sum[:, x, :, c]
        x_sums[j].wait_recv()
        near = near + x_sum[:, :, c].astype(wide)
        partial[:, x, :, c] = near
        z_away[:, :, c] = near.astype(narrow)
        for copy in z_sums[j]:
            copy.start()

    def make_slope(j, c):
        summed(
            lambda: (z_away.at[others, :, c], z_sum.at[:, :, c]), 2, z_base + j, x_peer
        ).wait_recv()
        upstream = partial[z, x, :, c]
        for k in range(groups - 1):
            upstream = upstream + z_sum[k, :, c].astype(wide)
        slope[z, x, :, c] = (upstream * factors[last, z, x, :, c]).astype(narrow)
        slope_shares[j].start()

    def pass_slope(j, c):
        remote(
            twice(lambda: slope.at[others, x, :, c]), (slope_send, 0), (slope_recv, j), x_peer
        ).wait_recv()
        x_slope(lambda: slope.at[:, x, :, c]).start()

    for turn in range(len(pieces) + SUM_LAG + PASS_LAG):
        made, passed = turn - SUM_LAG, turn - SUM_LAG - PASS_LAG

        @pl.when(trainer)
        def _():
            if turn < len(pieces):
                add_far(turn, pieces[turn])
            if turn == len(pieces) // 2:
                update_trainer(1)
            if 0 <= made < len(pieces):
                make_slope(made, pieces[made])
            if made == len(pieces) - 1:
                for copy in residuals[1:]:
                    copy.start()
                for j in range(count):
                    gather(j)

        if 0 <= made < len(pieces):

            @pl.when(solver)
            def _():
                slope_shares[made].wait_recv()

            for peer in z_peers:
                z_slope(pieces[made], made, peer).start()
        if passed >= 0:
            pass_slope(passed, pieces[passed])

    @pl.when(trainer)
    def _():
        for j in range(lent, count):
            update_trainer(j)
        hidden_momentum.wait_recv()

    @pl.when(solver)
    def _():
        for j in range(1, lent):
            update_solver(j)

    all_x_slopes = x_slope(lambda: slope.at[:, 1 - x])
    all_x_slopes.wait_recv()

    first_lane = pl.multiple_of((tile // 2) * LANES, LANES)

    def update_hidden(i):
        halves[i].wait_recv()
        total = gradient[i, own_units, :] + got_gradient[i]

        @pl.when(solver)
        def _():
            own_hidden[i] = momentum_decay * own_hidden[i] + total

        @pl.when(trainer)
        def _():
            fresh_momentum = momentum_decay * got_hidden[i].astype(wide) + total
            own_hidden[i] = own_hidden[i] - step_size * fresh_momentum

    slopes = [slope, slope_even, slope_odd]
    for step, i in enumerate(reversed(range(layer_count))):
        this_slope = slopes[0] if step == 0 else slopes[1 + step % 2]
        next_slope = slopes[1 + (step + 1) % 2]
        lanes = pl.ds(first_lane, LANES)
        own_inputs = features_ref[:, :, core, :, lanes] if i == 0 else inputs[i - 1, :, :, :, lanes]
        for c in parts:
            if i > 0:
                back = lax.dot_general(
                    this_slope[...].reshape(half, width),
                    weights.at[i].reshape(width, width)[c, :],
                    (((1,), (1,)), ((), ())),
                    preferred_element_type=wide,
                )
                factor = factors[i - 1, :, :, :, c].reshape(half, COLUMNS)
                next_slope[:, :, :, c] = (
                    (back * factor).astype(narrow).reshape(groups, 2, rows, COLUMNS)
                )
            gradient[i, :, c] = lax.dot_general(
                own_inputs.reshape(half, LANES),
                this_slope[:, :, :, c].reshape(half, COLUMNS),
                (((0,), (0,)), ((), ())),
                preferred_element_type=wide,
            )
        halves[i].start()

    @pl.when(trainer)
    def _():
        for j in range(lent, count):
            add_momentum(j)

    for i in reversed(range(layer_count)):
        update_hidden(i)

    def gone(view, semaphore, slot):
        remote(twice(view), (semaphore, slot), (x_recv, 0), x_peer).wait_send()

    gone(lambda: weights.at[:, :, :, core], core_send, 0)
    gone(lambda: weights.at[pl.ds(0, last), :, x, core], x_send, 0)
    gone(lambda: weights.at[last, z, x, core], x_send, 1)
    gone(lambda: weights.at[:, z, x, core], z_send, 0)
    gone(lambda: weights.at[last, z, x, core], z_send, 2)

    @pl.when(inner)
    def _():
        gone(lambda: weights.at[:, :, x, core], z_send, 1)
        gone(lambda: weights.at[last, :, x, core], z_send, 3)

    all_tops.wait_send()
    all_halves.wait_send()
    gone(lambda: slope.at[others, x], slope_send, 0)
    gone(lambda: slope.at[:, x], slope_send, 1)

    @pl.when(solver)
    def _():
        for copy in edges:
            copy.wait_send()
        gone(lambda: got_out, role_send, 0)
        gone(lambda: got_hidden, role_send, 1)
        gone(lambda: got_fields, role_send, 2)

    @pl.when(trainer)
    def _():
        for copy in all_sums:
            copy.wait_send()
        gone(lambda: weights.at[:, z, x, core], role_send, 0)
        gone(lambda: out_ref.at[:, lent_cells], role_send, 1)
        gone(lambda: residual.at[:, :, :, :, pl.ds(0, lent * COLUMNS)], role_send, 3)
        gone(lambda: slope.at[z, x], role_send, 4)


def store_kernel(*refs):
    semaphores = refs[-1]
    pairs = list(zip(refs[:3], refs[3:6]))
    for k, (source, target) in enumerate(pairs):
        length = source.shape[0]
        step = length if length % 4 else length // 4
        for at in range(0, length, step):
            band = pl.ds(at, step)
            pltpu.make_async_copy(source.at[band], target.at[band], semaphores.at[k]).start()
    for k, (source, target) in enumerate(pairs):
        pltpu.make_async_copy(source, target, semaphores.at[k]).wait()


def fused_step(fields, velocity, growth, features, assignment, own_out, own_hidden):
    layer_count, unit_rows, width = own_hidden.shape
    batch, cells = fields.shape
    groups = lax.axis_size("tile") // 4
    rows = batch // lax.axis_size("tile")
    narrow, wide = jnp.bfloat16, jnp.float32
    dma = pltpu.SemaphoreType.DMA
    anywhere = pl.BlockSpec(memory_space=pl.ANY)
    parts, pieces = width // COLUMNS, cells // COLUMNS
    splits = width // LANES
    splits = width // LANES
    role_slots = layer_count + 3 * pieces + 1 + splits
    split = (groups, 2, 2, rows, width)
    results = pl.pallas_call(
        functools.partial(train_kernel, groups),
        out_shape=(
            jax.ShapeDtypeStruct(fields.shape, wide),
            jax.ShapeDtypeStruct(own_out.shape, wide),
            jax.ShapeDtypeStruct(own_hidden.shape, wide),
        ),
        in_specs=[anywhere] * 7,
        out_specs=[pl.BlockSpec(memory_space=pltpu.VMEM)] * 3,
        scratch_shapes=[
            pltpu.VMEM(split, narrow),
            pltpu.VMEM((1, cells), wide),
            pltpu.VMEM((1, cells), wide),
            pltpu.VMEM((1, batch), jnp.int32),
            pltpu.VMEM((1, LANES), wide),
            pltpu.VMEM((batch, LANES), wide),
            pltpu.VMEM((batch, LANES), wide),
            pltpu.VMEM((batch, cells // 2), wide),
            pltpu.VMEM((batch, batch), narrow),
            pltpu.VMEM((width, cells), narrow),
            pltpu.VMEM((width, cells), narrow),
            pltpu.VMEM(own_hidden.shape, narrow),
            pltpu.VMEM((batch, cells), narrow),
            pltpu.VMEM((layer_count, groups, 2, 2, unit_rows, width), narrow),
            pltpu.VMEM((layer_count - 1, groups, 2, rows, width), narrow),
            pltpu.VMEM(split, narrow),
            pltpu.VMEM((layer_count, groups, 2, rows, width), wide),
            pltpu.VMEM((groups, 2, 2, rows, cells), narrow),
            pltpu.VMEM((groups, 2, rows, width), narrow),
            pltpu.VMEM((groups, 2, rows, width), narrow),
            pltpu.VMEM((groups, 2, rows, width), wide),
            pltpu.VMEM((groups, 2, rows, width), wide),
            pltpu.VMEM((groups, 2, rows, width), narrow),
            pltpu.VMEM((layer_count, LANES, width), wide),
            pltpu.VMEM(own_hidden.shape, wide),
            pltpu.VMEM((groups, 2, rows, width), wide),
            pltpu.VMEM((groups, rows, width), narrow),
            pltpu.VMEM((groups, rows, width), narrow),
            pltpu.VMEM((groups, rows, width), narrow),
            pltpu.VMEM((groups - 1, rows, width), narrow),
            dma((4,)),
            dma((layer_count + 1, groups - 1)),
            dma((2,)),
            dma((2 * layer_count + 1,)),
            dma((1,)),
            dma((layer_count,)),
            dma((3,)),
            dma((parts + 2 * splits,)),
            dma((2,)),
            dma((splits + 1,)),
            dma((5,)),
            dma((layer_count + 2 + pieces // 2 + splits,)),
            dma((2,)),
            dma((1 + layer_count,)),
            dma((3,)),
            dma((3,)),
            dma((6 + pieces,)),
        ],
        compiler_params=pltpu.CompilerParams(
            collective_id=0, has_side_effects=True, vmem_limit_bytes=46000000
        ),
        cost_estimate=pl.CostEstimate(
            flops=60 * batch * width * width, bytes_accessed=40 * batch * width, transcendentals=0
        ),
    )(
        *(
            pltpu.with_memory_space_constraint(value, pltpu.HBM)
            for value in (
                features.reshape(split),
                fields,
                velocity[None, :],
                growth[None, :],
                assignment[None, :],
                own_out,
                own_hidden,
            )
        )
    )
    return pl.pallas_call(
        store_kernel,
        out_shape=tuple(jax.ShapeDtypeStruct(v.shape, v.dtype) for v in results),
        in_specs=[anywhere] * 3,
        out_specs=[anywhere] * 3,
        scratch_shapes=[dma((3,))],
        compiler_params=pltpu.CompilerParams(vmem_limit_bytes=1 << 20),
    )(*results)


def plain_body(fields_pair, velocity, growth, features, assignment, out_pair, hidden_pair):
    solver_side = lax.axis_index("role") == 0
    own_fields = fields_pair[0]
    own_out = out_pair[0]
    own_hidden = hidden_pair[0]
    stacked = jnp.concatenate([own_fields, velocity[None, :]], axis=0)
    advanced = advance(extended(stacked, "tile", 1, 1), growth)
    grad_out, grad_hidden, other_out, other_hidden, fresh_fields = plain_training(
        features,
        own_hidden.astype(jnp.bfloat16),
        own_out.astype(jnp.bfloat16),
        own_fields,
        own_out,
        own_hidden,
        advanced.astype(jnp.bfloat16),
    )
    grad_out, grad_hidden, other_out, other_hidden = (
        v.astype(jnp.float32) for v in (grad_out, grad_hidden, other_out, other_hidden)
    )
    out_next = jnp.where(
        solver_side,
        momentum_decay * own_out + grad_out,
        own_out - step_size * (momentum_decay * other_out + grad_out),
    )
    hidden_next = jnp.where(
        solver_side,
        momentum_decay * own_hidden + other_hidden,
        own_hidden - step_size * (momentum_decay * other_hidden + grad_hidden),
    )
    next_batch = jnp.take(fresh_fields, assignment, axis=0).astype(jnp.float32)
    fields_next = jnp.where(solver_side, advanced, next_batch)
    return (fields_next[None], out_next[None], hidden_next[None])


def body(fields_pair, velocity, growth, features, assignment, out_pair, hidden_pair):
    tiles = lax.axis_size("tile")
    batch, cells = fields_pair.shape[1:]
    layer_count, unit_rows, width = hidden_pair.shape[1:]
    fits = (
        lax.axis_size("role") == 2
        and tiles == 16
        and layer_count == 5
        and batch % tiles == 0
        and (batch // tiles) % 16 == 0
        and LANES == 2 * unit_rows
        and width % COLUMNS == 0
        and cells % COLUMNS == 0
        and cells // COLUMNS == 4
    )
    if not fits:
        return plain_body(
            fields_pair, velocity, growth, features, assignment, out_pair, hidden_pair
        )
    results = fused_step(
        fields_pair[0], velocity, growth, features, assignment, out_pair[0], hidden_pair[0]
    )
    return tuple(result[None] for result in results)


def solution(mesh):
    return jax.shard_map(
        body,
        mesh=mesh,
        in_specs=(
            P("role", None, "tile"),
            P("tile"),
            P("tile"),
            P(),
            P(),
            P("role", None, "tile"),
            P("role", None, "tile", None),
        ),
        out_specs=(P("role", None, "tile"), P("role", None, "tile"), P("role", None, "tile", None)),
        check_vma=False,
    )
```

```python
import functools

import jax
import jax.numpy as jnp
from jax import lax
from jax.experimental import pallas as pl
from jax.experimental.pallas import tpu as pltpu
from jax.sharding import PartitionSpec as P

momentum_decay = 0.9
step_size = 0.1


def extended(value, axis, dim, width):
    count, length = (lax.axis_size(axis), value.shape[dim])
    up = [(i, (i + 1) % count) for i in range(count)]
    down = [(j, i) for i, j in up]
    last = lax.slice_in_dim(value, length - width, length, axis=dim)
    leading = lax.slice_in_dim(value, 0, width, axis=dim)
    before = lax.ppermute(last, axis, up)
    after = lax.ppermute(leading, axis, down)
    return jnp.concatenate([before, value, after], axis=dim)


def silu_slope(values):
    logistic = jax.nn.sigmoid(values)
    return logistic * (1.0 + values * (1.0 - logistic))


def advance(padded, growth):
    states = padded[:-1]
    velocity_row = padded[-1]
    outflow = (
        jnp.maximum(velocity_row[:-1], 0.0) * states[:, :-1]
        + jnp.minimum(velocity_row[:-1], 0.0) * states[:, 1:]
    )
    carried = states[:, 1:-1] - outflow[:, 1:] + outflow[:, :-1]
    return carried + growth * carried * (1.0 - carried)


def to_trainer(value):
    return lax.ppermute(value.astype(jnp.bfloat16), "role", [(0, 1)])


def to_solver(value):
    return lax.ppermute(value.astype(jnp.bfloat16), "role", [(1, 0)])


def plain_training(features, hidden_narrow, out_narrow, own_fields, own_out, own_hidden, fields):
    layer_count, unit_rows = own_hidden.shape[:2]
    batch = own_fields.shape[0]
    first_unit = lax.axis_index("tile") * unit_rows
    momentum_out = to_trainer(own_out)
    momentum_hidden = to_trainer(own_hidden)
    full_hidden = [
        lax.all_gather(hidden_narrow[i], "tile", axis=0, tiled=True) for i in range(layer_count)
    ]
    inputs, summed_list = [], []
    activation = features
    for i in range(layer_count):
        inputs.append(activation)
        summed = jnp.dot(activation, full_hidden[i], preferred_element_type=jnp.float32)
        summed_list.append(summed)
        activation = jax.nn.silu(summed).astype(jnp.bfloat16)
    predicted = jnp.dot(activation, out_narrow, preferred_element_type=jnp.float32)
    residual = ((predicted - own_fields) / batch).astype(jnp.bfloat16)
    partial_grad = lax.dot_general(
        residual, out_narrow, (((1,), (1,)), ((), ())), preferred_element_type=jnp.float32
    )
    upstream = lax.psum(partial_grad, "tile")
    grad_out = jnp.dot(activation.T, residual, preferred_element_type=jnp.float32)
    sent_out = to_solver(grad_out)
    gradients, sent = [], []
    for i in reversed(range(layer_count)):
        slope = (upstream * silu_slope(summed_list[i])).astype(jnp.bfloat16)
        own_inputs = lax.dynamic_slice_in_dim(inputs[i], first_unit, unit_rows, 1)
        gradient = jnp.dot(own_inputs.T, slope, preferred_element_type=jnp.float32)
        gradients.append(gradient)
        sent.append(to_solver(gradient))
        if i > 0:
            upstream = lax.dot_general(
                slope, full_hidden[i], (((1,), (1,)), ((), ())), preferred_element_type=jnp.float32
            )
    solver_side = lax.axis_index("role") == 0
    grad_out = jnp.where(solver_side, sent_out.astype(jnp.float32), grad_out)
    other_hidden = jnp.where(solver_side, jnp.stack(sent[::-1]), momentum_hidden)
    return grad_out, jnp.stack(gradients[::-1]), momentum_out, other_hidden, to_trainer(fields)


LANES = 128
COLUMNS = 256


SUM_LAG = 7
PASS_LAG = 7


class Later:
    def __init__(self, build):
        self.build = build

    def start(self):
        self.build().start()

    def wait(self):
        self.build().wait()

    def wait_recv(self):
        self.build().wait_recv()

    def wait_send(self):
        self.build().wait_send()


def train_kernel(
    groups,
    features_hbm,
    fields_hbm,
    velocity_hbm,
    growth_hbm,
    assignment_hbm,
    out_hbm,
    hidden_hbm,
    own_fields,
    own_out,
    own_hidden,
    features_ref,
    velocity_ref,
    growth_ref,
    assignment_ref,
    left_velocity,
    left_edge,
    right_edge,
    lent_fields,
    chosen_ref,
    out_ref,
    got_out,
    got_hidden,
    got_fields,
    weights,
    inputs,
    top,
    factors,
    residual,
    slope_even,
    slope_odd,
    partial,
    core_away,
    slope,
    gradient,
    got_gradient,
    core_sum,
    x_away,
    x_sum,
    z_away,
    z_sum,
    z_send,
    z_recv,
    x_send,
    x_recv,
    core_send,
    core_recv,
    sum_send,
    sum_recv,
    slope_send,
    slope_recv,
    role_send,
    role_recv,
    pair_send,
    pair_recv,
    edge_send,
    edge_recv,
    local_sem,
):
    layer_count, unit_rows, width = hidden_hbm.shape
    batch, cells = fields_hbm.shape
    rows = partial.shape[2]
    half = batch // 2
    narrow, wide = jnp.bfloat16, jnp.float32
    tiles = groups * 4
    last = layer_count - 1
    role = lax.axis_index("role")
    tile = lax.axis_index("tile")
    core = lax.rem(tile, 2)
    x = lax.rem(tile // 2, 2)
    z = tile // 4
    solver = role == 0
    trainer = role == 1

    def device(z_at, x_at, core_at):
        return (role, z_at * 4 + x_at * 2 + core_at)

    z_places = [lax.rem(z + k, groups) for k in range(1, groups)]
    z_peers = [device(place, x, core) for place in z_places]
    x_peer = device(z, 1 - x, core)
    core_peer = device(z, x, 1 - core)
    role_peer = (1 - role, tile)
    right_peer = (role, lax.rem(tile + 1, tiles))
    left_peer = (role, lax.rem(tile + tiles - 1, tiles))
    far_peer = (role, lax.rem(tile + tiles - 1 + 2 * core, tiles))

    def remote(views, sent, arrived, peer):
        def build():
            source, target = views()
            return pltpu.make_async_remote_copy(
                src_ref=source,
                dst_ref=target,
                send_sem=sent[0].at[sent[1]],
                recv_sem=arrived[0].at[arrived[1]],
                device_id=peer,
                device_id_type=pl.DeviceIdType.MESH,
            )

        return Later(build)

    def local(views, semaphores, slot):
        def build():
            source, target = views()
            return pltpu.make_async_copy(source, target, semaphores.at[slot])

        return Later(build)

    def twice(view):
        return lambda: (view(),) * 2

    def across(view, kind, slot):
        return remote(twice(view), (role_send, kind), (role_recv, slot), role_peer)

    chunks = [pl.ds(j * COLUMNS, COLUMNS) for j in range(cells // COLUMNS)]
    parts = [pl.ds(j * COLUMNS, COLUMNS) for j in range(width // COLUMNS)]
    pieces = [pl.ds(j * LANES, LANES) for j in range(width // LANES)]
    per_part = COLUMNS // LANES
    count = len(chunks)
    lent = count // 2
    lent_cells = pl.ds(lent * COLUMNS, (count - lent) * COLUMNS)
    momenta = [across(lambda c=c: got_out.at[:, c], 0, j) for j, c in enumerate(chunks)]
    hidden_momentum = across(lambda: got_hidden, 1, count)
    fresh = [
        across(lambda c=c: got_fields.at[:, c], 2, count + 1 + j) for j, c in enumerate(chunks)
    ]
    shares = [across(lambda i=i: weights.at[i, z, x, core], 0, i) for i in range(layer_count)]
    lent_out = across(lambda: out_ref.at[:, lent_cells], 1, layer_count)
    lent_target = remote(
        lambda: (own_fields.at[:, lent_cells], lent_fields),
        (role_send, 2),
        (role_recv, layer_count + 1),
        role_peer,
    )
    residuals = [
        across(lambda c=c: residual.at[:, :, :, :, c], 3, layer_count + 2 + j)
        for j, c in enumerate(chunks[:lent])
    ]
    slope_shares = [
        across(lambda c=c: slope.at[z, x, :, c], 4, layer_count + 2 + lent + j)
        for j, c in enumerate(pieces)
    ]

    pairs = [lambda: (hidden_hbm, own_hidden)]
    pairs += [lambda c=c: (out_hbm.at[:, c], own_out.at[:, c]) for c in chunks]
    pairs += [
        lambda: (fields_hbm, own_fields),
        lambda: (velocity_hbm, velocity_ref),
        lambda: (growth_hbm, growth_ref),
        lambda: (assignment_hbm, assignment_ref),
        lambda: (features_hbm, features_ref),
    ]
    loads = [local(views, local_sem, k) for k, views in enumerate(pairs)]
    for load in [loads[1], loads[0]] + loads[2:]:
        load.start()
    hidden_load, out_loads, small_loads = loads[0], loads[1 : 1 + len(chunks)], loads[1 + len(chunks) :]
    share_order = [last] + list(range(last))
    barrier = pltpu.get_barrier_semaphore()
    peers = z_peers + [x_peer, core_peer, role_peer, far_peer]
    for peer in peers:
        pl.semaphore_signal(barrier, inc=1, device_id=peer, device_id_type=pl.DeviceIdType.MESH)

    @pl.when(solver)
    def _():
        out_loads[0].wait()
        got_out[:, chunks[0]] = own_out[:, chunks[0]].astype(narrow)

    @pl.when(trainer)
    def _():
        hidden_load.wait()
        for i in share_order:
            weights[i, z, x, core] = own_hidden[i].astype(narrow)

    pl.semaphore_wait(barrier, len(peers))

    last_lanes = pl.ds(cells - LANES, LANES)
    edge_list = [
        (lambda: (fields_hbm.at[:, last_lanes], left_edge), right_peer),
        (lambda: (velocity_hbm.at[:, last_lanes], left_velocity), right_peer),
        (lambda: (fields_hbm.at[:, pl.ds(0, LANES)], right_edge), left_peer),
    ]
    edges = [
        remote(views, (edge_send, k), (edge_recv, k), peer)
        for k, (views, peer) in enumerate(edge_list)
    ]

    nearest = [
        sorted((p for p in range(groups) if p != q), key=lambda p: (abs(p - q), p))
        for q in range(groups)
    ]

    def pick(k):
        place = jnp.int32(nearest[0][k])
        for q in range(1, groups):
            place = jnp.where(z == q, nearest[q][k], place)
        return place

    z_origins = [pick(k) for k in range(groups - 1)]
    inner = jnp.logical_and(z > 0, z < groups - 1)

    def share_of(i, place, x_at):
        return twice(lambda: weights.at[i, place, x_at, core])

    def hop(i, place, item, kind, target):
        rank = jnp.where(place > target, place - 1, place)
        x_at = 1 - x if item == layer_count else x
        return remote(
            share_of(i, place, x_at),
            (z_send, kind + 2 * (item // layer_count)),
            (z_recv, (item, rank)),
            device(target, x, core),
        )

    def spread(item):
        i = min(item, last)

        @pl.when(z < groups - 1)
        def _():
            hop(i, z, item, 0, lax.rem(z + 1, groups)).start()

        @pl.when(z > 0)
        def _():
            hop(i, z, item, jnp.where(z == groups - 1, 0, 1), lax.rem(z + groups - 1, groups)).start()

    def onward(k):
        rising = z_origins[k] < z
        return jnp.logical_or(
            jnp.logical_and(rising, z < groups - 1),
            jnp.logical_and(jnp.logical_not(rising), z > 0),
        )

    def relay(item, k):
        i = min(item, last)
        place = z_origins[k]
        hop(i, place, item, 1, z).wait_recv()

        @pl.when(onward(k))
        def _():
            target = jnp.where(place < z, lax.rem(z + 1, groups), lax.rem(z + groups - 1, groups))
            hop(i, place, item, 1, target).start()

        if i < last:
            send_x(i, place, k)
        send_core(i, place, 1 - x if item == layer_count else x)

    def x_slot(i, k):
        return [0, 1, 2 + i, 2 + last + i][k + 1] if i < last else 2 + 2 * last

    def send_x(i, place, k):
        remote(share_of(i, place, x), (x_send, i // last), (x_recv, x_slot(i, k)), x_peer).start()

    def send_core(i, place, x_at):
        remote(share_of(i, place, x_at), (core_send, 0), (core_recv, i), core_peer).start()

    def arrived_x(views, slot):
        remote(twice(views), (x_send, 0), (x_recv, slot), x_peer).wait_recv()

    def cross(i, k):
        place = z if k < 0 else z_origins[k]
        arrived_x(lambda: weights.at[i, place, 1 - x, core], x_slot(i, k))
        send_core(i, place, 1 - x)

    def cross_wave(k):
        place = z if k < 0 else z_origins[k]
        arrived_x(lambda: weights.at[pl.ds(0, last), place, 1 - x, core], k + 1)
        for i in range(last):
            send_core(i, place, 1 - x)

    def send_share(i):
        @pl.when(solver)
        def _():
            shares[i].wait_recv()

        if i < last:
            spread(i)
        send_x(i, z, -1)
        send_core(i, z, x)


    def columns_of(j):
        return pl.ds(pl.multiple_of(j * COLUMNS, COLUMNS), COLUMNS)

    def advance():
        velocity = velocity_ref[...]
        forward_speed = jnp.maximum(velocity, 0.0)
        backward_speed = jnp.minimum(velocity, 0.0)
        growth = growth_ref[...]
        before = left_velocity[:, LANES - 1 :]
        step = LANES // 2

        @pl.loop(0, batch // step)
        def _(j):
            band = pl.ds(pl.multiple_of(j * step, step), step)
            current = own_fields[band, :]
            lane = lax.broadcasted_iota(jnp.int32, current.shape, 1)
            following = jnp.where(
                lane == cells - 1, right_edge[band, :1], pltpu.roll(current, cells - 1, 1)
            )
            outflow = forward_speed * current + backward_speed * following
            inflow_edge = (
                jnp.maximum(before, 0.0) * left_edge[band, :][:, LANES - 1 :]
                + jnp.minimum(before, 0.0) * current[:, :1]
            )
            inflow = jnp.where(lane == 0, inflow_edge, pltpu.roll(outflow, 1, 1))
            carried = current - outflow + inflow
            advanced = carried + growth * carried * (1.0 - carried)
            own_fields[band, :] = advanced
            got_fields[band, :] = advanced.astype(narrow)

    @pl.when(solver)
    def _():
        momenta[0].start()
        for copy in edges:
            copy.start()
        for j in range(1, count):
            out_loads[j].wait()
            got_out[:, chunks[j]] = own_out[:, chunks[j]].astype(narrow)
            if j < lent:
                momenta[j].start()
            if j == lent - 1:
                hidden_load.wait()
                got_hidden[...] = own_hidden[...].astype(narrow)
                hidden_momentum.start()

    @pl.when(trainer)
    def _():
        for i in share_order:
            shares[i].start()

    for i in share_order:
        send_share(i)

    for load in small_loads:
        load.wait()

    @pl.when(solver)
    def _():
        for copy in edges:
            copy.wait_recv()
        advance()
        for copy in fresh + momenta[lent:]:
            copy.start()

    @pl.when(trainer)
    def _():
        lent_target.start()
        for j in reversed(range(count)):
            out_loads[j].wait()
            out_ref[:, chunks[j]] = own_out[:, chunks[j]].astype(narrow)
            if j == lent:
                lent_out.start()
        member = lax.broadcasted_iota(jnp.int32, (batch, batch), 0)
        chosen = jnp.where(member == assignment_ref[...], 1.0, 0.0)
        chosen_ref[...] = chosen.T.astype(narrow)

    def beside(views, kind, slot):
        return remote(views, (pair_send, kind), (pair_recv, slot), core_peer)

    tops = [beside(twice(lambda c=c: top.at[:, :, core, :, c]), 0, 0) for c in parts]
    all_tops = beside(twice(lambda: top.at[:, :, core]), 0, 0)
    own_units = pl.ds(pl.multiple_of(core * unit_rows, unit_rows), unit_rows)
    other_units = pl.ds(pl.multiple_of((1 - core) * unit_rows, unit_rows), unit_rows)
    halves = [
        beside(lambda i=i: (gradient.at[i, other_units, :], got_gradient.at[i]), 1, 1 + i)
        for i in range(layer_count)
    ]
    all_halves = beside(lambda: (gradient.at[:, other_units, :], got_gradient), 1, 1)

    def forward_columns(i, columns):
        block = weights[i, :, :, :, :, columns].reshape(width, COLUMNS)
        activation = features_ref[:, :, core] if i == 0 else inputs[i - 1]
        summed = jnp.dot(activation.reshape(half, width), block, preferred_element_type=wide)
        logistic = jax.nn.sigmoid(summed)
        result = (summed * logistic).astype(narrow).reshape(groups, 2, rows, COLUMNS)
        factor = logistic * (1.0 + summed * (1.0 - logistic))
        factors[i, :, :, :, columns] = factor.reshape(groups, 2, rows, COLUMNS)
        return result

    def forward(i, between=None):
        for j, c in enumerate(parts):
            if between is not None and j == len(parts) // 2:
                between()
            if i < last:
                inputs[i, :, :, :, c] = forward_columns(i, c)
                continue
            top[:, :, core, :, c] = forward_columns(i, c)
            if j % 2:
                tops[j - 1].start()
                tops[j].start()

    def finish(i, between=None):
        remote(
            twice(lambda: weights.at[i, :, :, 1 - core]), (core_send, 0), (core_recv, i), core_peer
        ).wait_recv()
        forward(i, between)

    outer = jnp.logical_not(inner)
    lagging = [last, layer_count]

    @pl.when(inner)
    def _():
        for item in range(last):
            relay(item, 0)
            relay(item, 1)

    @pl.when(outer)
    def _():
        for item in range(last):
            relay(item, 0)

    spread(last)
    cross(last, -1)
    cross_wave(-1)

    @pl.when(inner)
    def _():
        for item in range(last):
            relay(item, 2)

    @pl.when(outer)
    def _():
        for item in range(last):
            relay(item, 1)

    spread(layer_count)
    cross_wave(0)

    @pl.when(inner)
    def _():
        for k in range(2):
            for item in lagging:
                relay(item, k)

    for item in range(last):

        @pl.when(outer)
        def _():
            relay(item, 2)

        cross(item, 1)

    @pl.when(inner)
    def _():
        for item in lagging:
            relay(item, 2)

    held = [(item, k) for k in range(groups - 1) for item in lagging]
    for i in range(last):

        @pl.when(outer)
        def _():
            for item, k in [held[:2], held[2:3], held[3:4], held[4:5]][i]:
                relay(item, k)

        cross(i, 2)
        if i > 0:
            finish(i - 1)
    def relay_held():
        @pl.when(outer)
        def _():
            for item, k in held[5:]:
                relay(item, k)

    finish(last - 1, relay_held)
    finish(last)

    def update_out(j, decay, rate, other):
        c = chunks[j]

        for units in parts:
            grad = lax.dot_general(
                top[:, :, :, :, units].reshape(batch, COLUMNS),
                residual[:, :, :, :, c].reshape(batch, COLUMNS),
                (((0,), (0,)), ((), ())),
                preferred_element_type=wide,
            )
            if rate is None:
                own_out[units, c] = decay * own_out[units, c] + grad
            elif other is None:
                own_out[units, c] = own_out[units, c] - rate * grad
            else:
                fresh_momentum = decay * other[units, c].astype(wide) + grad
                own_out[units, c] = own_out[units, c] - rate * fresh_momentum

    def update_solver(j):
        residuals[j].wait_recv()
        update_out(j, momentum_decay, None, None)

    def update_trainer(j):
        if j < lent:
            momenta[j].wait_recv()
        update_out(j, momentum_decay, step_size, got_out if j < lent else None)

    def add_momentum(j):
        momenta[j].wait_recv()
        for units in parts:
            late = momentum_decay * got_out[units, chunks[j]].astype(wide)
            own_out[units, chunks[j]] = own_out[units, chunks[j]] - step_size * late

    def gather(j):
        fresh[j].wait_recv()
        own_fields[:, chunks[j]] = jnp.dot(
            chosen_ref[...], got_fields[:, chunks[j]], preferred_element_type=wide
        )

    def summed(views, kind, slot, peer):
        return remote(views, (sum_send, kind), (sum_recv, slot), peer)

    core_sums = [
        summed(lambda c=c: (core_away.at[:, :, :, c], core_sum.at[:, :, :, c]), 0, j, core_peer)
        for j, c in enumerate(parts)
    ]
    x_sums = [
        summed(lambda c=c: (x_away.at[:, :, c], x_sum.at[:, :, c]), 1, len(parts) + j, x_peer)
        for j, c in enumerate(pieces)
    ]
    z_base = len(parts) + len(pieces)
    z_sums = [
        [
            summed(
                lambda c=c, k=k: (z_away.at[z_places[k], :, c], z_sum.at[k, :, c]),
                2,
                z_base + j,
                z_peers[k],
            )
            for k in range(groups - 1)
        ]
        for j, c in enumerate(pieces)
    ]
    others = pl.ds(0, groups - 1)
    all_sums = [
        summed(lambda: (core_away, core_sum), 0, 0, core_peer),
        summed(lambda: (x_away, x_sum), 1, 0, x_peer),
        summed(lambda: (z_away.at[others], z_sum), 2, 0, x_peer),
    ]
    targets = own_fields.reshape(groups, 2, 2, rows, cells)

    def residual_columns(side, c, wanted):
        rows_of = top[:, :, side].reshape(half, width)
        predicted = jnp.dot(rows_of, out_ref[:, c], preferred_element_type=wide)
        kept = ((predicted - wanted.reshape(half, COLUMNS)) / batch).astype(narrow)
        residual[:, :, side, :, c] = kept.reshape(groups, 2, rows, COLUMNS)

    def upstream_columns(side, c):
        return lax.dot_general(
            residual[:, :, side].reshape(half, cells),
            out_ref[c, :],
            (((1,), (1,)), ((), ())),
            preferred_element_type=wide,
        ).reshape(groups, 2, rows, COLUMNS)

    @pl.when(trainer)
    def _():
        for c in chunks:
            residual_columns(core, c, targets[:, :, core, :, c])
        early = len(parts) // 2
        for c in parts[:early]:
            partial[:, :, :, c] = upstream_columns(core, c)
        all_tops.wait_recv()
        for c in chunks:
            residual_columns(1 - core, c, targets[:, :, 1 - core, :, c])
        residuals[0].start()
        for c in parts:
            core_away[:, :, :, c] = upstream_columns(1 - core, c)
        for copy in core_sums:
            copy.start()
        for c in parts[early:]:
            partial[:, :, :, c] = upstream_columns(core, c)
        for j, c in enumerate(parts):
            core_sums[j].wait_recv()
            x_away[:, :, c] = (partial[:, 1 - x, :, c] + core_sum[:, 1 - x, :, c]).astype(narrow)
            for copy in x_sums[j * per_part : (j + 1) * per_part]:
                copy.start()
        update_trainer(0)
        lent_target.wait_send()

    @pl.when(solver)
    def _():
        all_tops.wait_recv()
        lent_out.wait_recv()
        lent_target.wait_recv()
        lent_wanted = lent_fields.reshape(groups, 2, 2, rows, cells - lent * COLUMNS)
        for j in range(lent, count):
            for side in range(2):
                residual_columns(side, chunks[j], lent_wanted[:, :, side, :, chunks[j - lent]])
        for j in range(lent, count):
            update_out(j, momentum_decay, None, None)
        update_solver(0)

    def z_slope(c, slot, peer):
        return remote(
            twice(lambda: slope.at[z, x, :, c]), (slope_send, 0), (slope_recv, slot), peer
        )

    def x_slope(view):
        return remote(twice(view), (slope_send, 1), (slope_recv, len(pieces)), x_peer)

    def add_far(j, c):
        near = partial[:, x, :, c] + core_sum[:, x, :, c]
        x_sums[j].wait_recv()
        near = near + x_sum[:, :, c].astype(wide)
        partial[:, x, :, c] = near
        z_away[:, :, c] = near.astype(narrow)
        for copy in z_sums[j]:
            copy.start()

    def make_slope(j, c):
        summed(
            lambda: (z_away.at[others, :, c], z_sum.at[:, :, c]), 2, z_base + j, x_peer
        ).wait_recv()
        upstream = partial[z, x, :, c]
        for k in range(groups - 1):
            upstream = upstream + z_sum[k, :, c].astype(wide)
        slope[z, x, :, c] = (upstream * factors[last, z, x, :, c]).astype(narrow)
        slope_shares[j].start()

    def pass_slope(j, c):
        remote(
            twice(lambda: slope.at[others, x, :, c]), (slope_send, 0), (slope_recv, j), x_peer
        ).wait_recv()
        x_slope(lambda: slope.at[:, x, :, c]).start()

    for turn in range(len(pieces) + SUM_LAG + PASS_LAG):
        made, passed = turn - SUM_LAG, turn - SUM_LAG - PASS_LAG

        @pl.when(trainer)
        def _():
            if turn < len(pieces):
                add_far(turn, pieces[turn])
            if turn == len(pieces) // 2:
                update_trainer(1)
            if 0 <= made < len(pieces):
                make_slope(made, pieces[made])
            if made == len(pieces) - 1:
                for copy in residuals[1:]:
                    copy.start()
                for j in range(count):
                    gather(j)

        if 0 <= made < len(pieces):

            @pl.when(solver)
            def _():
                slope_shares[made].wait_recv()

            for peer in z_peers:
                z_slope(pieces[made], made, peer).start()
        if passed >= 0:
            pass_slope(passed, pieces[passed])

    @pl.when(trainer)
    def _():
        for j in range(lent, count):
            update_trainer(j)
        hidden_momentum.wait_recv()

    @pl.when(solver)
    def _():
        for j in range(1, lent):
            update_solver(j)

    all_x_slopes = x_slope(lambda: slope.at[:, 1 - x])
    all_x_slopes.wait_recv()

    first_lane = pl.multiple_of((tile // 2) * LANES, LANES)

    def update_hidden(i):
        halves[i].wait_recv()
        total = gradient[i, own_units, :] + got_gradient[i]

        @pl.when(solver)
        def _():
            own_hidden[i] = momentum_decay * own_hidden[i] + total

        @pl.when(trainer)
        def _():
            fresh_momentum = momentum_decay * got_hidden[i].astype(wide) + total
            own_hidden[i] = own_hidden[i] - step_size * fresh_momentum

    slopes = [slope, slope_even, slope_odd]
    for step, i in enumerate(reversed(range(layer_count))):
        this_slope = slopes[0] if step == 0 else slopes[1 + step % 2]
        next_slope = slopes[1 + (step + 1) % 2]
        lanes = pl.ds(first_lane, LANES)
        own_inputs = features_ref[:, :, core, :, lanes] if i == 0 else inputs[i - 1, :, :, :, lanes]
        for c in parts:
            if i > 0:
                back = lax.dot_general(
                    this_slope[...].reshape(half, width),
                    weights.at[i].reshape(width, width)[c, :],
                    (((1,), (1,)), ((), ())),
                    preferred_element_type=wide,
                )
                factor = factors[i - 1, :, :, :, c].reshape(half, COLUMNS)
                next_slope[:, :, :, c] = (
                    (back * factor).astype(narrow).reshape(groups, 2, rows, COLUMNS)
                )
            gradient[i, :, c] = lax.dot_general(
                own_inputs.reshape(half, LANES),
                this_slope[:, :, :, c].reshape(half, COLUMNS),
                (((0,), (0,)), ((), ())),
                preferred_element_type=wide,
            )
        halves[i].start()

    @pl.when(trainer)
    def _():
        for j in range(lent, count):
            add_momentum(j)

    for i in reversed(range(layer_count)):
        update_hidden(i)

    def gone(view, semaphore, slot):
        remote(twice(view), (semaphore, slot), (x_recv, 0), x_peer).wait_send()

    gone(lambda: weights.at[:, :, :, core], core_send, 0)
    gone(lambda: weights.at[pl.ds(0, last), :, x, core], x_send, 0)
    gone(lambda: weights.at[last, z, x, core], x_send, 1)
    gone(lambda: weights.at[:, z, x, core], z_send, 0)
    gone(lambda: weights.at[last, z, x, core], z_send, 2)

    @pl.when(inner)
    def _():
        gone(lambda: weights.at[:, :, x, core], z_send, 1)
        gone(lambda: weights.at[last, :, x, core], z_send, 3)

    all_tops.wait_send()
    all_halves.wait_send()
    gone(lambda: slope.at[others, x], slope_send, 0)
    gone(lambda: slope.at[:, x], slope_send, 1)

    @pl.when(solver)
    def _():
        for copy in edges:
            copy.wait_send()
        gone(lambda: got_out, role_send, 0)
        gone(lambda: got_hidden, role_send, 1)
        gone(lambda: got_fields, role_send, 2)

    @pl.when(trainer)
    def _():
        for copy in all_sums:
            copy.wait_send()
        gone(lambda: weights.at[:, z, x, core], role_send, 0)
        gone(lambda: out_ref.at[:, lent_cells], role_send, 1)
        gone(lambda: residual.at[:, :, :, :, pl.ds(0, lent * COLUMNS)], role_send, 3)
        gone(lambda: slope.at[z, x], role_send, 4)


def store_kernel(*refs):
    semaphores = refs[-1]
    pairs = list(zip(refs[:3], refs[3:6]))
    for k, (source, target) in enumerate(pairs):
        length = source.shape[0]
        step = length if length % 4 else length // 4
        for at in range(0, length, step):
            band = pl.ds(at, step)
            pltpu.make_async_copy(source.at[band], target.at[band], semaphores.at[k]).start()
    for k, (source, target) in enumerate(pairs):
        pltpu.make_async_copy(source, target, semaphores.at[k]).wait()


def fused_step(fields, velocity, growth, features, assignment, own_out, own_hidden):
    layer_count, unit_rows, width = own_hidden.shape
    batch, cells = fields.shape
    groups = lax.axis_size("tile") // 4
    rows = batch // lax.axis_size("tile")
    narrow, wide = jnp.bfloat16, jnp.float32
    dma = pltpu.SemaphoreType.DMA
    anywhere = pl.BlockSpec(memory_space=pl.ANY)
    parts, pieces = width // COLUMNS, cells // COLUMNS
    splits = width // LANES
    splits = width // LANES
    role_slots = layer_count + 3 * pieces + 1 + splits
    split = (groups, 2, 2, rows, width)
    results = pl.pallas_call(
        functools.partial(train_kernel, groups),
        out_shape=(
            jax.ShapeDtypeStruct(fields.shape, wide),
            jax.ShapeDtypeStruct(own_out.shape, wide),
            jax.ShapeDtypeStruct(own_hidden.shape, wide),
        ),
        in_specs=[anywhere] * 7,
        out_specs=[pl.BlockSpec(memory_space=pltpu.VMEM)] * 3,
        scratch_shapes=[
            pltpu.VMEM(split, narrow),
            pltpu.VMEM((1, cells), wide),
            pltpu.VMEM((1, cells), wide),
            pltpu.VMEM((1, batch), jnp.int32),
            pltpu.VMEM((1, LANES), wide),
            pltpu.VMEM((batch, LANES), wide),
            pltpu.VMEM((batch, LANES), wide),
            pltpu.VMEM((batch, cells // 2), wide),
            pltpu.VMEM((batch, batch), narrow),
            pltpu.VMEM((width, cells), narrow),
            pltpu.VMEM((width, cells), narrow),
            pltpu.VMEM(own_hidden.shape, narrow),
            pltpu.VMEM((batch, cells), narrow),
            pltpu.VMEM((layer_count, groups, 2, 2, unit_rows, width), narrow),
            pltpu.VMEM((layer_count - 1, groups, 2, rows, width), narrow),
            pltpu.VMEM(split, narrow),
            pltpu.VMEM((layer_count, groups, 2, rows, width), wide),
            pltpu.VMEM((groups, 2, 2, rows, cells), narrow),
            pltpu.VMEM((groups, 2, rows, width), narrow),
            pltpu.VMEM((groups, 2, rows, width), narrow),
            pltpu.VMEM((groups, 2, rows, width), wide),
            pltpu.VMEM((groups, 2, rows, width), wide),
            pltpu.VMEM((groups, 2, rows, width), narrow),
            pltpu.VMEM((layer_count, LANES, width), wide),
            pltpu.VMEM(own_hidden.shape, wide),
            pltpu.VMEM((groups, 2, rows, width), wide),
            pltpu.VMEM((groups, rows, width), narrow),
            pltpu.VMEM((groups, rows, width), narrow),
            pltpu.VMEM((groups, rows, width), narrow),
            pltpu.VMEM((groups - 1, rows, width), narrow),
            dma((4,)),
            dma((layer_count + 1, groups - 1)),
            dma((2,)),
            dma((2 * layer_count + 1,)),
            dma((1,)),
            dma((layer_count,)),
            dma((3,)),
            dma((parts + 2 * splits,)),
            dma((2,)),
            dma((splits + 1,)),
            dma((5,)),
            dma((layer_count + 2 + pieces // 2 + splits,)),
            dma((2,)),
            dma((1 + layer_count,)),
            dma((3,)),
            dma((3,)),
            dma((6 + pieces,)),
        ],
        compiler_params=pltpu.CompilerParams(
            collective_id=0, has_side_effects=True, vmem_limit_bytes=46000000
        ),
        cost_estimate=pl.CostEstimate(
            flops=60 * batch * width * width, bytes_accessed=40 * batch * width, transcendentals=0
        ),
    )(
        *(
            pltpu.with_memory_space_constraint(value, pltpu.HBM)
            for value in (
                features.reshape(split),
                fields,
                velocity[None, :],
                growth[None, :],
                assignment[None, :],
                own_out,
                own_hidden,
            )
        )
    )
    return pl.pallas_call(
        store_kernel,
        out_shape=tuple(jax.ShapeDtypeStruct(v.shape, v.dtype) for v in results),
        in_specs=[anywhere] * 3,
        out_specs=[anywhere] * 3,
        scratch_shapes=[dma((3,))],
        compiler_params=pltpu.CompilerParams(vmem_limit_bytes=1 << 20),
    )(*results)


def plain_body(fields_pair, velocity, growth, features, assignment, out_pair, hidden_pair):
    solver_side = lax.axis_index("role") == 0
    own_fields = fields_pair[0]
    own_out = out_pair[0]
    own_hidden = hidden_pair[0]
    stacked = jnp.concatenate([own_fields, velocity[None, :]], axis=0)
    advanced = advance(extended(stacked, "tile", 1, 1), growth)
    grad_out, grad_hidden, other_out, other_hidden, fresh_fields = plain_training(
        features,
        own_hidden.astype(jnp.bfloat16),
        own_out.astype(jnp.bfloat16),
        own_fields,
        own_out,
        own_hidden,
        advanced.astype(jnp.bfloat16),
    )
    grad_out, grad_hidden, other_out, other_hidden = (
        v.astype(jnp.float32) for v in (grad_out, grad_hidden, other_out, other_hidden)
    )
    out_next = jnp.where(
        solver_side,
        momentum_decay * own_out + grad_out,
        own_out - step_size * (momentum_decay * other_out + grad_out),
    )
    hidden_next = jnp.where(
        solver_side,
        momentum_decay * own_hidden + other_hidden,
        own_hidden - step_size * (momentum_decay * other_hidden + grad_hidden),
    )
    next_batch = jnp.take(fresh_fields, assignment, axis=0).astype(jnp.float32)
    fields_next = jnp.where(solver_side, advanced, next_batch)
    return (fields_next[None], out_next[None], hidden_next[None])


def body(fields_pair, velocity, growth, features, assignment, out_pair, hidden_pair):
    tiles = lax.axis_size("tile")
    batch, cells = fields_pair.shape[1:]
    layer_count, unit_rows, width = hidden_pair.shape[1:]
    fits = (
        lax.axis_size("role") == 2
        and tiles == 16
        and layer_count == 5
        and batch % tiles == 0
        and (batch // tiles) % 16 == 0
        and LANES == 2 * unit_rows
        and width % COLUMNS == 0
        and cells % COLUMNS == 0
        and cells // COLUMNS == 4
    )
    if not fits:
        return plain_body(
            fields_pair, velocity, growth, features, assignment, out_pair, hidden_pair
        )
    results = fused_step(
        fields_pair[0], velocity, growth, features, assignment, out_pair[0], hidden_pair[0]
    )
    return tuple(result[None] for result in results)


def solution(mesh):
    return jax.shard_map(
        body,
        mesh=mesh,
        in_specs=(
            P("role", None, "tile"),
            P("tile"),
            P("tile"),
            P(),
            P(),
            P("role", None, "tile"),
            P("role", None, "tile", None),
        ),
        out_specs=(P("role", None, "tile"), P("role", None, "tile"), P("role", None, "tile", None)),
        check_vma=False,
    )
```
